32 devices in a mesh: group: 4 (over x, core), replica: 8 (over z, y).
Axes of the slice: x: 2, y: 2, z: 4, core: 2. Of those that a mesh axis runs over, the one named last changes fastest.
Arguments:
- tokens: bfloat16 [8, 8, 196, 768], P('replica', 'group'), may hold values from -6 to 6
- out_grad: bfloat16 [8, 8, 196, 768], P('replica', 'group'), may hold values from -6 to 6
- slot_mask: int32 [8], P('replica'), may hold values 0 or 1
- time_norm_gain: bfloat16 [768], P('group'), may hold values from 0.5 to 1.5
- time_norm_shift: bfloat16 [768], P('group'), may hold values from -2.5 to 2.5
- time_qkv: bfloat16 [768, 2304], P('group'), may hold values from -0.21875 to 0.21875
- time_qv_bias: bfloat16 [1536], P('group'), may hold values from -2.5 to 2.5
- time_proj: bfloat16 [768, 768], P('group'), may hold values from -0.4375 to 0.4375
- time_proj_bias: bfloat16 [768], P('group'), may hold values from -2.5 to 2.5
- time_fc: bfloat16 [768, 768], P('group'), may hold values from -0.21875 to 0.21875
- time_fc_bias: bfloat16 [768], P('group'), may hold values from -2.5 to 2.5
- space_norm_gain: bfloat16 [768], P('group'), may hold values from 0.5 to 1.5
- space_norm_shift: bfloat16 [768], P('group'), may hold values from -2.5 to 2.5
- space_qkv: bfloat16 [768, 2304], P('group'), may hold values from -0.21875 to 0.21875
- space_qv_bias: bfloat16 [1536], P('group'), may hold values from -2.5 to 2.5
- space_proj: bfloat16 [768, 768], P('group'), may hold values from -1.75 to 1.75
- space_proj_bias: bfloat16 [768], P('group'), may hold values from -2.5 to 2.5
- mlp_norm_gain: bfloat16 [768], P('group'), may hold values from 0.5 to 1.5
- mlp_norm_shift: bfloat16 [768], P('group'), may hold values from -2.5 to 2.5
- mlp_in: bfloat16 [768, 3072], P('group'), may hold values from -0.21875 to 0.21875
- mlp_in_bias: bfloat16 [3072], P('group'), may hold values from -2.5 to 2.5
- mlp_out: bfloat16 [3072, 768], P('group'), may hold values from -0.15625 to 0.15625
- mlp_out_bias: bfloat16 [768], P('group'), may hold values from -2.5 to 2.5
Outputs:
- layer_out: bfloat16 [8, 8, 196, 768], P('replica', 'group')
- tokens_grad: float32 [8, 8, 196, 768], P('replica', 'group')
- time_norm_gain_grad: float32 [768], P('group')
- time_norm_shift_grad: float32 [768], P('group')
- time_qkv_grad: float32 [768, 2304], P('group')
- time_qv_bias_grad: float32 [1536], P('group')
- time_proj_grad: float32 [768, 768], P('group')
- time_proj_bias_grad: float32 [768], P('group')
- time_fc_grad: float32 [768, 768], P('group')
- time_fc_bias_grad: float32 [768], P('group')
- space_norm_gain_grad: float32 [768], P('group')
- space_norm_shift_grad: float32 [768], P('group')
- space_qkv_grad: float32 [768, 2304], P('group')
- space_qv_bias_grad: float32 [1536], P('group')
- space_proj_grad: float32 [768, 768], P('group')
- space_proj_bias_grad: float32 [768], P('group')
- mlp_norm_gain_grad: float32 [768], P('group')
- mlp_norm_shift_grad: float32 [768], P('group')
- mlp_in_grad: float32 [768, 3072], P('group')
- mlp_in_bias_grad: float32 [3072], P('group')
- mlp_out_grad: float32 [3072, 768], P('group')
- mlp_out_bias_grad: float32 [768], P('group')
The draws below stay inside these ranges and needn't reach their ends.
All inputs are finite; a program needn't handle non-finite values. No bound on the sum of `slot_mask` on one device may be relied on, other than what follows from the above.
Results may differ from the reference program's by a relative error of at most 0.02.
Values may be sent and summed in bfloat16 or wider, within the bound.
No kernel may reach another device: no remote copies, remote signals or barrier semaphores. Data moves between devices by JAX's collectives and lax.ppermute only.
A program may use at most 192 MiB of HBM per device.

```python
import jax
import jax.numpy as jnp
from jax import lax

D = 768
FF = 3072
HEADS = 12
HEAD_DIM = 64
FRAMES = 8
PLACES = 196
SLOTS = 8


def touch_ends(array, rng, low, top_value):
    dims = array.shape
    spot = [jax.random.randint(jax.random.fold_in(rng, axis), (), 0, dims[axis]) for axis in range(len(dims))]
    array = array.at[tuple(spot)].set(low)
    longest = dims.index(max(dims))
    spot[longest] = (spot[longest] + 1) % dims[longest]
    return array.at[tuple(spot)].set(top_value)


def shard_levels(stream_key, shape, shards, least, high):
    level = 1.0
    for axis_at, shards_of in shards:
        steps = jax.random.uniform(jax.random.fold_in(jax.random.fold_in(stream_key, 6), axis_at), (shards_of,), jnp.float32, least / len(shards), high / len(shards))
        level = level * jnp.repeat(jnp.exp(steps), shape[axis_at] // shards_of).reshape((-1,) + (1,) * (len(shape) - 1 - axis_at))
    return level


def noise(stream_key, shape, scale, reach, pieces=(), dtype=jnp.bfloat16):
    array = scale * jax.random.normal(stream_key, shape, jnp.float32)
    if pieces:
        array = array * shard_levels(stream_key, shape, pieces, -0.22, 0.18)
    return jnp.clip(array, -reach, reach).astype(dtype)


def setup_inputs(seed: int = 0) -> dict:
    splits = jax.random.split(jax.random.key(seed), 24)
    return {
        "tokens": noise(splits[0], (SLOTS, FRAMES, PLACES, D), 1.0, 6.0, ((0, 8), (1, 4))),
        "out_grad": noise(splits[1], (SLOTS, FRAMES, PLACES, D), 1.0, 6.0, ((0, 8), (1, 4))),
        "slot_mask": touch_ends((jax.random.randint(splits[2], (SLOTS,), 0, 4) < 3).astype(jnp.int32), jax.random.fold_in(splits[2], 1), 0, 1),
        "time_norm_gain": jnp.clip(1.0 + 0.1 * jax.random.normal(splits[3], (D,), jnp.float32), 0.5, 1.5).astype(jnp.bfloat16),
        "time_norm_shift": noise(splits[4], (D,), 0.2, 2.5, ((0, 4),)),
        "time_qkv": noise(splits[5], (D, 3 * D), D ** -0.5, 0.21875, ((0, 4),)),
        "time_qv_bias": noise(splits[6], (2 * D,), 0.2, 2.5, ((0, 4),)),
        "time_proj": noise(splits[7], (D, D), (D // 4) ** -0.5, 0.4375, ((0, 4),)),
        "time_proj_bias": noise(splits[8], (D,), 0.2, 2.5, ((0, 4),)),
        "time_fc": noise(splits[9], (D, D), D ** -0.5, 0.21875, ((0, 4),)),
        "time_fc_bias": noise(splits[10], (D,), 0.2, 2.5, ((0, 4),)),
        "space_norm_gain": jnp.clip(1.0 + 0.1 * jax.random.normal(splits[11], (D,), jnp.float32), 0.5, 1.5).astype(jnp.bfloat16),
        "space_norm_shift": noise(splits[12], (D,), 0.2, 2.5, ((0, 4),)),
        "space_qkv": noise(splits[13], (D, 3 * D), D ** -0.5, 0.21875, ((0, 4),)),
        "space_qv_bias": noise(splits[14], (2 * D,), 0.2, 2.5, ((0, 4),)),
        "space_proj": noise(splits[15], (D, D), (max(D // 64, 3 * D // PLACES)) ** -0.5, 1.75, ((0, 4),)),
        "space_proj_bias": noise(splits[16], (D,), 0.2, 2.5, ((0, 4),)),
        "mlp_norm_gain": jnp.clip(1.0 + 0.1 * jax.random.normal(splits[17], (D,), jnp.float32), 0.5, 1.5).astype(jnp.bfloat16),
        "mlp_norm_shift": noise(splits[18], (D,), 0.2, 2.5, ((0, 4),)),
        "mlp_in": noise(splits[19], (D, FF), D ** -0.5, 0.21875, ((0, 4),)),
        "mlp_in_bias": noise(splits[20], (FF,), 0.2, 2.5, ((0, 4),)),
        "mlp_out": noise(splits[21], (FF, D), (FF // 2) ** -0.5, 0.15625, ((0, 4),)),
        "mlp_out_bias": noise(splits[22], (D,), 0.2, 2.5, ((0, 4),)),
    }


@jax.custom_vjp
def low(v):
    return lax.optimization_barrier(v.astype(jnp.bfloat16)).astype(jnp.float32)

@jax.custom_vjp
def low_back(v):
    return v

def low_keep(v):
    return (low(v), None)

def low_pass(kept, grad):
    return (grad,)

def back_keep(v):
    return (v, None)

def back_low(kept, grad):
    return (low(grad),)
low.defvjp(low_keep, low_pass)
low_back.defvjp(back_keep, back_low)
epsilon = 1e-06

def product(left, right):
    return jnp.dot(left, right, precision=lax.Precision.HIGHEST, preferred_element_type=jnp.float32)

def layer_norm(values, gain, shift):
    average = lax.optimization_barrier(jnp.mean(values, axis=-1, keepdims=True))
    centred = values - average
    variance = lax.optimization_barrier(jnp.mean(centred * centred, axis=-1, keepdims=True))
    return centred * lax.rsqrt(variance + epsilon) * gain + shift

def projected(normed, weight, qv_bias):
    bias_full = jnp.concatenate([qv_bias[:D], jnp.zeros_like(qv_bias[:D]), qv_bias[D:]])
    return low_back(low(product(normed, weight) + bias_full))

def clip_layer(clip, weights, slot_live):
    time_norm_gain, time_norm_shift, time_qkv, time_qv_bias, time_proj, time_proj_bias, time_fc, time_fc_bias, space_norm_gain, space_norm_shift, space_qkv, space_qv_bias, space_proj, space_proj_bias, mlp_norm_gain, mlp_norm_shift, mlp_in, mlp_in_bias, mlp_out, mlp_out_bias = weights
    score_scale = HEAD_DIM ** (-0.5)
    highest = lax.Precision.HIGHEST
    tokens_flat = clip.reshape(FRAMES * PLACES, D)
    normed = low(layer_norm(tokens_flat, time_norm_gain, time_norm_shift))
    packed = projected(normed, time_qkv, time_qv_bias).reshape(FRAMES, PLACES, 3, HEADS, HEAD_DIM)
    scores = low_back(jnp.einsum('fphd,gphd->phfg', packed[:, :, 0], packed[:, :, 1], precision=highest) * score_scale)
    probs = low(jax.nn.softmax(scores, axis=-1))
    mixed = jnp.einsum('phfg,gphd->fphd', probs, packed[:, :, 2], precision=highest)
    mixed = low_back(low(mixed.reshape(FRAMES * PLACES, D)))
    proj_out = low_back(low(product(mixed, time_proj) + time_proj_bias))
    branch = low_back(product(proj_out, time_fc) + time_fc_bias)
    after_time = tokens_flat + branch
    normed = low(layer_norm(after_time, space_norm_gain, space_norm_shift))
    packed = projected(normed, space_qkv, space_qv_bias).reshape(FRAMES, PLACES, 3, HEADS, HEAD_DIM)
    scores = low_back(jnp.einsum('fphd,fqhd->fhpq', packed[:, :, 0], packed[:, :, 1], precision=highest) * score_scale)
    probs = low(jax.nn.softmax(scores, axis=-1))
    mixed = jnp.einsum('fhpq,fqhd->fphd', probs, packed[:, :, 2], precision=highest)
    mixed = low_back(low(mixed.reshape(FRAMES * PLACES, D)))
    branch = low_back(product(mixed, space_proj) + space_proj_bias)
    after_space = after_time + branch
    normed = low(layer_norm(after_space, mlp_norm_gain, mlp_norm_shift))
    pre_act = low_back(product(normed, mlp_in) + mlp_in_bias)
    hidden = low(jax.nn.gelu(pre_act, approximate=False))
    branch = low_back(product(hidden, mlp_out) + mlp_out_bias)
    return (slot_live * (after_space + branch)).reshape(FRAMES, PLACES, D)

def reference(tokens, out_grad, slot_mask, time_norm_gain, time_norm_shift, time_qkv, time_qv_bias, time_proj, time_proj_bias, time_fc, time_fc_bias, space_norm_gain, space_norm_shift, space_qkv, space_qv_bias, space_proj, space_proj_bias, mlp_norm_gain, mlp_norm_shift, mlp_in, mlp_in_bias, mlp_out, mlp_out_bias):
    weights = tuple((weight.astype(jnp.float32) for weight in (time_norm_gain, time_norm_shift, time_qkv, time_qv_bias, time_proj, time_proj_bias, time_fc, time_fc_bias, space_norm_gain, space_norm_shift, space_qkv, space_qv_bias, space_proj, space_proj_bias, mlp_norm_gain, mlp_norm_shift, mlp_in, mlp_in_bias, mlp_out, mlp_out_bias)))

    def one_slot(totals, inputs):
        clip, clip_grad, marker = inputs
        slot_live = marker.astype(jnp.float32)
        layer_value, pullback = jax.vjp(lambda values, params: clip_layer(values, params, slot_live), clip.astype(jnp.float32), weights)
        input_grad, weight_grads = pullback(clip_grad.astype(jnp.float32))
        totals = tuple((left + right for left, right in zip(totals, weight_grads)))
        return (totals, (layer_value.astype(jnp.bfloat16), input_grad))
    zeros_start = tuple((jnp.zeros_like(weight) for weight in weights))
    totals, (layer_out, tokens_grad) = lax.scan(one_slot, zeros_start, (tokens, out_grad, slot_mask))
    return (layer_out, tokens_grad, totals[0], totals[1], totals[2], totals[3], totals[4], totals[5], totals[6], totals[7], totals[8], totals[9], totals[10], totals[11], totals[12], totals[13], totals[14], totals[15], totals[16], totals[17], totals[18], totals[19])
```

```python
import jax
import jax.numpy as jnp
from jax import lax
from jax.sharding import PartitionSpec as P

D = 768
HEADS = 12
HEAD_DIM = 64
PLACES = 196
BLOCK = 192
CHUNK = 104
PLACE_ROWS = 392
FRAME_PAD = 208
FRAME_ROWS = 416
epsilon = 1e-06
bf16 = jnp.bfloat16
f32 = jnp.float32


def matmul(left, right):
    return jnp.dot(left, right, preferred_element_type=f32)


def times_trans(left, right):
    return lax.dot_general(left, right, (((1,), (1,)), ((), ())), preferred_element_type=f32)


def outer_sum(left, right):
    return lax.dot_general(left, right, (((0,), (0,)), ((), ())), preferred_element_type=f32)


def column_sums(values):
    return jnp.sum(values.astype(f32), axis=0)


def norm_parts(values):
    centred = values - jnp.mean(values, axis=-1, keepdims=True)
    inverse = lax.rsqrt(jnp.mean(centred * centred, axis=-1, keepdims=True) + epsilon)
    return centred * inverse, inverse


def norm_back(values, gain, grad_normed):
    normal, inverse = norm_parts(values)
    scaled = grad_normed * gain
    grad = inverse * (
        scaled
        - jnp.mean(scaled, axis=-1, keepdims=True)
        - normal * jnp.mean(scaled * normal, axis=-1, keepdims=True)
    )
    return grad, jnp.sum(grad_normed * normal, axis=0), jnp.sum(grad_normed, axis=0)


def flip(array, axis, bit, size):
    return lax.ppermute(array, axis, [(at, at ^ bit) for at in range(size)])


def pick(array, at):
    return lax.dynamic_index_in_dim(array, at, 0, keepdims=False)


def add_rounded(left, right):
    return (left.astype(f32) + right.astype(f32)).astype(bf16)


def gather_shard(own, place):
    group_at, ring_bit, ring_size = place
    rows = own.shape[0]
    partner = flip(own, "group", 1, 4)
    if ring_size > 1:
        half = rows // 2
        sent = lax.dynamic_slice_in_dim(own, ring_bit * half, half, 0)
        direct = flip(sent, "group", 2, 4)
        relayed = flip(direct, "replica", 1, ring_size)
        remote = jnp.where(
            ring_bit == 0,
            jnp.concatenate([direct, relayed], 0),
            jnp.concatenate([relayed, direct], 0),
        )
    else:
        remote = flip(own, "group", 2, 4)
    across = flip(remote, "group", 1, 4)
    held = jnp.stack([own, partner, remote, across])
    return jnp.stack([pick(held, group_at ^ shard) for shard in range(4)])


def reduce_chunk(packed, place, replica_at, ring_size):
    group_at = place[0]
    chip_at = group_at // 2
    core_at = group_at % 2
    rows = packed.shape[1]
    halves = packed.reshape(2, 2, rows, D).transpose(1, 0, 2, 3)
    current = add_rounded(pick(halves, core_at), flip(pick(halves, 1 - core_at), "group", 1, 4))
    current = add_rounded(
        pick(current, chip_at), flip(pick(current, 1 - chip_at), "group", 2, 4)
    )
    bits = [1 << at for at in range(ring_size.bit_length() - 1)]
    for bit in bits:
        mine = (replica_at // bit) % 2
        split = current.reshape(2, current.shape[0] // 2, D)
        current = add_rounded(
            pick(split, mine), flip(pick(split, 1 - mine), "replica", bit, ring_size)
        )
    for bit in reversed(bits):
        mine = (replica_at // bit) % 2
        other = flip(current, "replica", bit, ring_size)
        current = jnp.where(
            mine == 0,
            jnp.concatenate([current, other], 0),
            jnp.concatenate([other, current], 0),
        )
    return current.astype(f32)


def pack_weight(shard):
    rows, width = shard.shape
    return shard.reshape(rows, width // D, D).transpose(1, 0, 2).reshape(-1, D)


def unpack_weight(full, start, blocks):
    part = full[:, start * BLOCK : (start + blocks) * BLOCK]
    return part.reshape(4, blocks, BLOCK, D).transpose(0, 2, 1, 3).reshape(4 * BLOCK, blocks * D)


def pack_grad(grad):
    rounded = grad.astype(bf16)
    blocks = grad.shape[1] // D
    return (
        rounded.reshape(4, BLOCK, blocks, D).transpose(0, 2, 1, 3).reshape(4, blocks * BLOCK, D)
    )


def unpack_grad(summed, start, blocks):
    part = summed[start * BLOCK : (start + blocks) * BLOCK]
    return part.reshape(blocks, BLOCK, D).transpose(1, 0, 2).reshape(BLOCK, blocks * D)


def bias_row(qv_bias):
    qv_float = qv_bias.astype(f32)
    return jnp.concatenate([qv_float[:D], jnp.zeros((D,), f32), qv_float[D:]])


def split_heads(packed, member):
    leading = packed.shape[:-1]
    return packed[..., member * D : (member + 1) * D].reshape(leading + (HEADS, HEAD_DIM))


def attend(packed, live_keys):
    query, key_part, value_part = (split_heads(packed, member) for member in range(3))
    scores = jnp.einsum("bqhd,bkhd->bhqk", query, key_part, preferred_element_type=f32)
    scores = scores * HEAD_DIM ** (-0.5)
    if live_keys is not None:
        scores = jnp.where(live_keys, scores, -1e30)
    maximum = jnp.max(scores, axis=-1, keepdims=True)
    weights = jnp.exp(scores - maximum)
    probs = weights / jnp.sum(weights, axis=-1, keepdims=True)
    mixed = jnp.einsum(
        "bhqk,bkhd->bqhd", probs.astype(bf16), value_part, preferred_element_type=f32
    )
    return mixed.reshape(packed.shape[:-1] + (D,)).astype(bf16), probs


def attend_back(packed, probs, grad_mixed):
    query, key_part, value_part = (split_heads(packed, member) for member in range(3))
    score_scale = HEAD_DIM ** (-0.5)
    grad_heads = grad_mixed.reshape(grad_mixed.shape[:-1] + (HEADS, HEAD_DIM))
    grad_value = jnp.einsum(
        "bhqk,bqhd->bkhd", probs.astype(bf16), grad_heads, preferred_element_type=f32
    )
    grad_probs = jnp.einsum("bqhd,bkhd->bhqk", grad_heads, value_part, preferred_element_type=f32)
    centre = jnp.sum(grad_probs * probs, axis=-1, keepdims=True)
    grad_scores = (probs * (grad_probs - centre)).astype(bf16)
    grad_query = (
        jnp.einsum("bhqk,bkhd->bqhd", grad_scores, key_part, preferred_element_type=f32)
        * score_scale
    )
    grad_key = (
        jnp.einsum("bhqk,bqhd->bkhd", grad_scores, query, preferred_element_type=f32) * score_scale
    )
    flat = packed.shape[:-1] + (D,)
    return jnp.concatenate(
        [grad_query.reshape(flat), grad_key.reshape(flat), grad_value.reshape(flat)], axis=-1
    ).astype(bf16)


def place_to_send():
    row = lax.broadcasted_iota(jnp.int32, (FRAME_ROWS, PLACE_ROWS), 0)
    col = lax.broadcasted_iota(jnp.int32, (FRAME_ROWS, PLACE_ROWS), 1)
    dest = row // CHUNK
    local = row % CHUNK
    source = (local // 2) * 8 + dest * 2 + local % 2
    return ((col == source) & (local < 98)).astype(bf16)


def recv_to_frame(group_at):
    row = lax.broadcasted_iota(jnp.int32, (FRAME_ROWS, FRAME_ROWS), 0)
    col = lax.broadcasted_iota(jnp.int32, (FRAME_ROWS, FRAME_ROWS), 1)
    frame = row // FRAME_PAD
    spot = row % FRAME_PAD
    source = ((spot // 49) ^ group_at) * CHUNK + (spot % 49) * 2 + frame
    return ((col == source) & (spot < PLACES)).astype(bf16)


def exchange(chunks):
    return [chunks[0]] + [flip(chunks[d], "group", d, 4) for d in range(1, 4)]


def permuted(matrix, rows):
    return matmul(matrix, rows).astype(bf16)


def permuted_back(matrix, rows):
    return outer_sum(matrix, rows).astype(bf16)


def chunks_of(rows):
    return [rows[d * CHUNK : (d + 1) * CHUNK] for d in range(4)]


def build(mesh):
    ring_size = mesh.shape["replica"]

    def on_device(tokens, out_grad, slot_mask, *shards):
        (
            time_norm_gain, time_norm_shift, time_qkv, time_qv_bias, time_proj, time_proj_bias,
            time_fc, time_fc_bias, space_norm_gain, space_norm_shift, space_qkv, space_qv_bias,
            space_proj, space_proj_bias, mlp_norm_gain, mlp_norm_shift, mlp_in, mlp_in_bias,
            mlp_out, mlp_out_bias,
        ) = shards
        group_at = lax.axis_index("group")
        replica_at = lax.axis_index("replica")
        place = (group_at, replica_at % 2, ring_size)
        vectors = [
            time_norm_gain, time_norm_shift, time_qv_bias, time_proj_bias, time_fc_bias,
            space_norm_gain, space_norm_shift, space_qv_bias, space_proj_bias, mlp_norm_gain,
            mlp_norm_shift, mlp_in_bias, mlp_out_bias,
        ]
        widths = [v.shape[0] for v in vectors]
        flat = jnp.concatenate(vectors)
        extra = jnp.pad(flat, (0, 16 * D - flat.shape[0])).reshape(16, D)

        token_pieces = tokens[0].transpose(1, 0, 2).reshape(4, 49, 2, D)
        got = exchange([pick(token_pieces, group_at ^ d) for d in range(4)])
        place_tokens = jnp.concatenate(got, axis=1).reshape(PLACE_ROWS, D)

        full_a = gather_shard(
            jnp.concatenate([pack_weight(time_qkv), time_proj, time_fc, extra], 0), place
        )
        full_b = gather_shard(jnp.concatenate([pack_weight(space_qkv), space_proj], 0), place)
        full_c = gather_shard(jnp.concatenate([pack_weight(mlp_in), mlp_out], 0), place)
        w_time_qkv = unpack_weight(full_a, 0, 3)
        w_time_proj = unpack_weight(full_a, 3, 1)
        w_time_fc = unpack_weight(full_a, 4, 1)
        w_space_qkv = unpack_weight(full_b, 0, 3)
        w_space_proj = unpack_weight(full_b, 3, 1)
        w_mlp_in = unpack_weight(full_c, 0, 4)
        w_mlp_out = full_c[:, 4 * BLOCK :].reshape(4 * D, D)
        flat_full = full_a[:, 5 * BLOCK :].reshape(4, 16 * D)
        vecs = []
        start = 0
        for width in widths:
            vecs.append(flat_full[:, start : start + width].reshape(-1).astype(f32))
            start += width
        (
            g_time_norm, s_time_norm, b_time_qv, b_time_proj, b_time_fc, g_space_norm,
            s_space_norm, b_space_qv, b_space_proj, g_mlp_norm, s_mlp_norm, b_mlp_in, b_mlp_out,
        ) = vecs

        live = slot_mask.astype(f32)[0]
        pads = ((0, 0), (0, FRAME_PAD - PLACES), (0, 0))
        frame_tokens = jnp.pad(tokens[0], pads).reshape(FRAME_ROWS, D)
        frame_grad = jnp.pad(out_grad[0], pads).reshape(FRAME_ROWS, D)
        to_send = place_to_send()
        to_frame = recv_to_frame(group_at)
        live_keys = (lax.broadcasted_iota(jnp.int32, (1, 1, 1, FRAME_PAD), 3) < PLACES)

        place_x = place_tokens.astype(f32)
        normal1, unused = norm_parts(place_x)
        h1 = (normal1 * g_time_norm + s_time_norm).astype(bf16)
        qkv1 = (matmul(h1, w_time_qkv) + bias_row(b_time_qv)).astype(bf16)
        a1, probs1 = attend(qkv1.reshape(49, 8, 3 * D), None)
        a1 = a1.reshape(PLACE_ROWS, D)
        o1 = (matmul(a1, w_time_proj) + b_time_proj).astype(bf16)
        frame_o1 = permuted(
            to_frame, jnp.concatenate(exchange(chunks_of(permuted(to_send, o1))), 0)
        )
        x1 = frame_tokens.astype(f32) + (matmul(frame_o1, w_time_fc) + b_time_fc)
        normal2, unused = norm_parts(x1)
        h2 = (normal2 * g_space_norm + s_space_norm).astype(bf16)
        qkv2 = (matmul(h2, w_space_qkv) + bias_row(b_space_qv)).astype(bf16)
        a2, probs2 = attend(qkv2.reshape(2, FRAME_PAD, 3 * D), live_keys)
        a2 = a2.reshape(FRAME_ROWS, D)
        x2 = x1 + (matmul(a2, w_space_proj) + b_space_proj)
        normal3, unused = norm_parts(x2)
        h3 = (normal3 * g_mlp_norm + s_mlp_norm).astype(bf16)
        pre_act = matmul(h3, w_mlp_in) + b_mlp_in
        cdf = 0.5 * (1.0 + lax.erf(pre_act * (0.5**0.5)))
        act = (pre_act * cdf).astype(bf16)
        x3 = x2 + (matmul(act, w_mlp_out) + b_mlp_out)
        layer_out = (live * x3).astype(bf16).reshape(2, FRAME_PAD, D)[None, :, :PLACES]
        e3 = live * frame_grad.astype(f32)
        dm = e3.astype(bf16)
        d_mlp_out = outer_sum(act, dm)
        slope = cdf + pre_act * jnp.exp(-0.5 * pre_act * pre_act) * 0.3989422804014327
        du = (slope * times_trans(dm, w_mlp_out)).astype(bf16)
        d_mlp_in = outer_sum(h3, du)
        grad_c = jnp.concatenate(
            [pack_grad(d_mlp_in), d_mlp_out.astype(bf16).reshape(4, D, D)], 1
        )
        sum_c = reduce_chunk(grad_c, place, replica_at, ring_size)
        d_v3, dg3, ds3 = norm_back(x2, g_mlp_norm, times_trans(du, w_mlp_in))
        e2 = e3 + d_v3
        dt2 = e2.astype(bf16)
        d_space_proj = outer_sum(a2, dt2)
        da2 = times_trans(dt2, w_space_proj).astype(bf16)
        dqkv2 = attend_back(
            qkv2.reshape(2, FRAME_PAD, 3 * D), probs2, da2.reshape(2, FRAME_PAD, D)
        ).reshape(FRAME_ROWS, 3 * D)
        d_space_qkv = outer_sum(h2, dqkv2)
        sum_b = reduce_chunk(
            jnp.concatenate([pack_grad(d_space_qkv), pack_grad(d_space_proj)], 1),
            place, replica_at, ring_size,
        )
        d_v2, dg2, ds2 = norm_back(x1, g_space_norm, times_trans(dqkv2, w_space_qkv))
        e1 = e2 + d_v2
        dt1 = e1.astype(bf16)
        dt1_place = permuted_back(
            to_send, jnp.concatenate(exchange(chunks_of(permuted_back(to_frame, dt1))), 0)
        )
        d_time_fc = outer_sum(o1, dt1_place)
        do1 = times_trans(dt1_place, w_time_fc).astype(bf16)
        d_time_proj = outer_sum(a1, do1)
        da1 = times_trans(do1, w_time_proj).astype(bf16)
        dqkv1 = attend_back(
            qkv1.reshape(49, 8, 3 * D), probs1, da1.reshape(49, 8, D)
        ).reshape(PLACE_ROWS, 3 * D)
        d_time_qkv = outer_sum(h1, dqkv1)
        d_v1, dg1, ds1 = norm_back(place_x, g_time_norm, times_trans(dqkv1, w_time_qkv))
        sums1 = column_sums(dqkv1)
        sums2 = column_sums(dqkv2)
        grads = [
            dg1, ds1, jnp.concatenate([sums1[:D], sums1[2 * D :]]), column_sums(do1),
            column_sums(dt1_place), dg2, ds2, jnp.concatenate([sums2[:D], sums2[2 * D :]]),
            column_sums(dt2), dg3, ds3, column_sums(du), column_sums(dm),
        ]
        flat_grads = jnp.concatenate([v.astype(bf16).reshape(4, -1) for v in grads], 1)
        extra_rows = max(16, ring_size)
        extra_grads = jnp.pad(
            flat_grads, ((0, 0), (0, extra_rows * D - flat_grads.shape[1]))
        ).reshape(4, extra_rows, D)
        sum_a = reduce_chunk(
            jnp.concatenate(
                [pack_grad(d_time_qkv), pack_grad(d_time_proj), pack_grad(d_time_fc), extra_grads],
                1,
            ),
            place, replica_at, ring_size,
        )
        back = permuted(
            to_frame,
            jnp.concatenate(exchange(chunks_of(permuted(to_send, d_v1.astype(bf16)))), 0),
        )
        tokens_grad = (e1 + back.astype(f32)).reshape(2, FRAME_PAD, D)[None, :, :PLACES]
        flat_sums = sum_a[5 * BLOCK :].reshape(-1)
        outs = []
        start = 0
        for width in widths:
            outs.append(flat_sums[start : start + width])
            start += width
        (
            o_dg1, o_ds1, o_qv1, o_pb, o_fb, o_dg2, o_ds2, o_qv2, o_sb, o_dg3, o_ds3, o_ib, o_ob,
        ) = outs
        return (
            layer_out, tokens_grad, o_dg1, o_ds1, unpack_grad(sum_a, 0, 3), o_qv1,
            unpack_grad(sum_a, 3, 1), o_pb, unpack_grad(sum_a, 4, 1), o_fb, o_dg2, o_ds2,
            unpack_grad(sum_b, 0, 3), o_qv2, unpack_grad(sum_b, 3, 1), o_sb, o_dg3, o_ds3,
            unpack_grad(sum_c, 0, 4), o_ib, sum_c[4 * BLOCK :], o_ob,
        )

    return on_device


def solution(mesh):
    rows = P("group", None)
    vector = P("group")
    batch = P("replica", "group", None, None)
    params = (
        vector, vector, rows, vector, rows, vector, rows, vector, vector, vector, rows, vector,
        rows, vector, vector, vector, rows, vector, rows, vector,
    )
    return jax.shard_map(
        build(mesh),
        mesh=mesh,
        in_specs=(batch, batch, P("replica")) + params,
        out_specs=(batch, batch) + params,
        check_vma=False,
    )
```

```python
import functools

import jax
import jax.numpy as jnp
from jax import lax
from jax.experimental import pallas as pl
from jax.experimental.pallas import tpu as pltpu
from jax.sharding import PartitionSpec as P

D = 768
FF = 3072
HEADS = 12
HEAD_DIM = 64
PLACES = 196
BLOCK = 192
CHUNK = 104
HALF = 208
ROWS = 416
epsilon = 1e-06
bf16 = jnp.bfloat16
f32 = jnp.float32

TIME_GAIN, TIME_SHIFT, TIME_PROJ_B, TIME_FC_B, SPACE_GAIN, SPACE_SHIFT, SPACE_PROJ_B = range(7)
MLP_GAIN, MLP_SHIFT, MLP_OUT_B = 7, 8, 9
TIME_QV, SPACE_QV, MLP_IN_B = 10, 12, 14
VECTOR_ROWS = 18
EXTRA = 64

TIME_QKV_PARTS = ((0, 0, 192, 0, 0), (0, 192, 192, 0, 1), (1, 0, 192, 0, 2))
TIME_PROJ_PARTS = ((1, 192, 192, 0, 0),)
SPACE_QKV_PARTS = ((0, 0, 192, 0, 0), (0, 192, 192, 0, 1), (1, 96, 192, 0, 2))
SPACE_PROJ_PARTS = ((1, 288, 192, 0, 0),)
TIME_FC_PARTS = ((0, 384, 96, 0, 0), (1, 0, 96, 96, 0))
MLP_IN_PARTS = ((0, 0, 192, 0, 0), (0, 192, 192, 0, 1), (1, 0, 192, 0, 2), (1, 192, 192, 0, 3))
MLP_OUT_PARTS = ((0, 0, 384, 0, 0), (1, 0, 384, 384, 0))
TIME_CHUNK, SPACE_CHUNK, IN_CHUNK, OUT_CHUNK = (0, 768), (768, 960), (1728, 768), (2496, 768)
VECTOR_AT = 3264


def nn(left, right):
    return lax.dot_general(left, right, (((1,), (0,)), ((), ())), preferred_element_type=f32)


def nt(left, right):
    return lax.dot_general(left, right, (((1,), (1,)), ((), ())), preferred_element_type=f32)


def tn(left, right):
    return lax.dot_general(left, right, (((0,), (0,)), ((), ())), preferred_element_type=f32)


def norm_parts(values):
    centred = values - jnp.mean(values, axis=-1, keepdims=True)
    inverse = lax.rsqrt(jnp.mean(centred * centred, axis=-1, keepdims=True) + epsilon)
    return centred * inverse, inverse


class Weights:
    def __init__(self, scalars, own, pieces, parts, chunk, target, sems):
        self.scalars, self.own, self.pieces, self.parts = scalars, own, pieces, parts
        self.chunk, self.target, self.sems = chunk, target, sems
        self.shard_rows = own.shape[0]

    def base(self, flipped):
        at = (self.scalars[0] ^ flipped) * self.shard_rows
        return pl.multiple_of(at, self.shard_rows)

    def copy(self, source, part, flipped, at):
        half, row, rows, block_row, column = part
        return pltpu.make_async_copy(
            source.at[pl.ds(row, rows), :],
            self.target.at[pl.ds(self.base(flipped) + block_row, rows), pl.ds(column * D, D)],
            self.sems.at[at],
        )

    def own_copy(self):
        target = self.target.at[pl.ds(self.base(0), self.shard_rows), :]
        return pltpu.make_async_copy(self.own, target, self.sems.at[0])

    def start(self):
        packed, direct, relayed, across, across_relayed = self.pieces
        self.own_copy().start()
        y = self.scalars[1]
        first, chunk_rows = self.chunk
        at = 1
        for part in self.parts:
            half, row, rows, block_row, column = part
            whole = (half, first + row + half * (chunk_rows // 2), rows, block_row, column)
            self.copy(packed, whole, 1, at).start()

            @pl.when(y == half)
            def _():
                self.copy(direct, part, 2, at + 1).start()
                self.copy(across, part, 3, at + 2).start()

            @pl.when(y != half)
            def _():
                self.copy(relayed, part, 2, at + 1).start()
                self.copy(across_relayed, part, 3, at + 2).start()

            at += 3

    def wait(self):
        direct, across = self.pieces[1], self.pieces[3]
        self.own_copy().wait()
        at = 1
        for part in self.parts:
            self.copy(direct, part, 1, at).wait()
            self.copy(direct, part, 2, at + 1).wait()
            self.copy(across, part, 3, at + 2).wait()
            at += 3


def lane_half(second):
    lane = lax.broadcasted_iota(jnp.int32, (HALF, 128), 1)
    return (lane >= 64) if second else (lane < 64)


def masked(values, second):
    return jnp.where(lane_half(second), values, jnp.zeros_like(values))


def key_mask(same_place):
    key = lax.broadcasted_iota(jnp.int32, (HALF, HALF), 0)
    query = lax.broadcasted_iota(jnp.int32, (HALF, HALF), 1)
    allowed = (key // 8 == query // 8) if same_place else (key < PLACES)
    return jnp.where(allowed, 0.0, -1e30).astype(f32)


def probs_of(key_pair, query_pair, mask, second):
    scores = nt(masked(key_pair, second), query_pair) + mask
    weights = jnp.exp(scores - jnp.max(scores, axis=0, keepdims=True))
    return weights * (1.0 / jnp.sum(weights, axis=0, keepdims=True))


def merged_rows(first, second):
    return jnp.concatenate([first[:64], second[64:]], axis=0)


def attend(qkv_ref, mask, out_ref):
    def pair_step(pair, carry):
        column = pl.multiple_of(pair * 128, 128)
        for part in range(2):
            rows = pl.ds(part * HALF, HALF)
            query = qkv_ref[rows, pl.ds(column, 128)] * bf16(HEAD_DIM**-0.5)
            key_part = qkv_ref[rows, pl.ds(D + column, 128)]
            value_part = qkv_ref[rows, pl.ds(2 * D + column, 128)]
            mixed = [
                tn(value_part, probs_of(key_part, query, mask, second).astype(bf16))
                for second in (False, True)
            ]
            out_ref[rows, pl.ds(column, 128)] = merged_rows(*mixed).T.astype(bf16)
        return carry

    lax.fori_loop(0, HEADS // 2, pair_step, 0)


def attend_back(qkv_ref, mask, grad_ref, out_ref):
    def pair_step(pair, carry):
        column = pl.multiple_of(pair * 128, 128)
        for part in range(2):
            rows = pl.ds(part * HALF, HALF)
            query = qkv_ref[rows, pl.ds(column, 128)] * bf16(HEAD_DIM**-0.5)
            key_part = qkv_ref[rows, pl.ds(D + column, 128)]
            value_part = qkv_ref[rows, pl.ds(2 * D + column, 128)]
            grad = grad_ref[rows, pl.ds(column, 128)]
            grads = ([], [], [])
            for second in (False, True):
                probs = probs_of(key_part, query, mask, second)
                grad_probs = nt(masked(value_part, second), grad)
                centre = jnp.sum(grad_probs * probs, axis=0, keepdims=True)
                grad_scores = (probs * (grad_probs - centre)).astype(bf16)
                grads[0].append(tn(key_part, grad_scores))
                grads[1].append(nn(grad_scores, query))
                grads[2].append(nn(probs.astype(bf16), grad))
            grad_query = merged_rows(*grads[0]).T * HEAD_DIM**-0.5
            out_ref[rows, pl.ds(column, 128)] = grad_query.astype(bf16)
            first = lane_half(False)
            out_ref[rows, pl.ds(D + column, 128)] = jnp.where(first, *grads[1]).astype(bf16)
            out_ref[rows, pl.ds(2 * D + column, 128)] = jnp.where(first, *grads[2]).astype(bf16)
        return carry

    lax.fori_loop(0, HEADS // 2, pair_step, 0)


def project_qkv(normed, weight, vec, qv_row, out_ref):
    for member in range(3):
        packed = nn(normed, weight[:, member * D : (member + 1) * D])
        if member != 1:
            row = qv_row + member // 2
            packed = packed + vec[row : row + 1, :]
        out_ref[:, member * D : (member + 1) * D] = packed.astype(bf16)


def place_to_send(dest):
    local = lax.broadcasted_iota(jnp.int32, (CHUNK, ROWS), 0)
    col = lax.broadcasted_iota(jnp.int32, (CHUNK, ROWS), 1)
    source = (local // 2) * 8 + dest * 2 + local % 2
    return ((col == source) & (local < 98)).astype(bf16)


def recv_to_frame(group_at, source):
    row = lax.broadcasted_iota(jnp.int32, (ROWS, CHUNK), 0)
    col = lax.broadcasted_iota(jnp.int32, (ROWS, CHUNK), 1)
    second = (row >= HALF).astype(jnp.int32)
    spot = row - second * HALF
    local = (spot - (group_at ^ source) * 49) * 2 + second
    inside = (spot >= (group_at ^ source) * 49) & (spot < ((group_at ^ source) + 1) * 49)
    return ((col == local) & inside).astype(bf16)


def place_forward_kernel(
    scalars, tokens, vec, *refs
):
    own_qkv, own_proj, *pieces = refs[:7]
    h1, qkv, mixed, o1, *rest = refs[7:]
    sends, (w_qkv, w_proj, sem_a, sem_b) = rest[:4], rest[4:]
    qkv_copy = Weights(scalars, own_qkv, pieces, TIME_QKV_PARTS, TIME_CHUNK, w_qkv, sem_a)
    proj_copy = Weights(scalars, own_proj, pieces, TIME_PROJ_PARTS, TIME_CHUNK, w_proj, sem_b)
    qkv_copy.start()
    proj_copy.start()
    normal, unused = norm_parts(tokens[...].astype(f32))
    normed = (normal * vec[TIME_GAIN : TIME_GAIN + 1, :] + vec[TIME_SHIFT : TIME_SHIFT + 1, :])
    normed = normed.astype(bf16)
    h1[...] = normed
    qkv_copy.wait()
    project_qkv(normed, w_qkv, vec, TIME_QV, qkv)
    attend(qkv, key_mask(True), mixed)
    proj_copy.wait()
    out = (nn(mixed[...], w_proj[...]) + vec[TIME_PROJ_B : TIME_PROJ_B + 1, :]).astype(bf16)
    o1[...] = out
    for dest in range(4):
        sends[dest][...] = nn(place_to_send(dest), out).astype(bf16)


def frame_forward_kernel(scalars, tokens, vec, r0, r1, r2, r3, *refs):
    own_fc, own_qkv, own_proj, *pieces = refs[:8]
    x1, h2, qkv, mixed, x2, h3 = refs[8:14]
    w_fc, w_qkv, w_proj, sem_a, sem_b, sem_c = refs[14:]
    fc_copy = Weights(scalars, own_fc, pieces, TIME_FC_PARTS, SPACE_CHUNK, w_fc, sem_a)
    qkv_copy = Weights(scalars, own_qkv, pieces, SPACE_QKV_PARTS, SPACE_CHUNK, w_qkv, sem_b)
    proj_copy = Weights(scalars, own_proj, pieces, SPACE_PROJ_PARTS, SPACE_CHUNK, w_proj, sem_c)
    fc_copy.start()
    qkv_copy.start()
    proj_copy.start()
    group_at = scalars[0]
    received = sum(
        nn(recv_to_frame(group_at, source), ref[...]) for source, ref in enumerate((r0, r1, r2, r3))
    ).astype(bf16)
    fc_copy.wait()
    branch = nn(received, w_fc[...]) + vec[TIME_FC_B : TIME_FC_B + 1, :]
    after = tokens[...].astype(f32) + branch
    x1[...] = after
    normal, unused = norm_parts(after)
    normed = normal * vec[SPACE_GAIN : SPACE_GAIN + 1, :] + vec[SPACE_SHIFT : SPACE_SHIFT + 1, :]
    normed = normed.astype(bf16)
    h2[...] = normed
    qkv_copy.wait()
    project_qkv(normed, w_qkv, vec, SPACE_QV, qkv)
    attend(qkv, key_mask(False), mixed)
    proj_copy.wait()
    after = x1[...] + (nn(mixed[...], w_proj[...]) + vec[SPACE_PROJ_B : SPACE_PROJ_B + 1, :])
    x2[...] = after
    normal, unused = norm_parts(after)
    normed = normal * vec[MLP_GAIN : MLP_GAIN + 1, :] + vec[MLP_SHIFT : MLP_SHIFT + 1, :]
    h3[...] = normed.astype(bf16)


def norm_back(values, gain, grad_normed):
    normal, inverse = norm_parts(values)
    scaled = grad_normed * gain
    mean = jnp.mean(scaled, axis=-1, keepdims=True)
    along = jnp.mean(scaled * normal, axis=-1, keepdims=True)
    grad = inverse * (scaled - mean - normal * along)
    return (
        grad,
        jnp.sum(grad_normed * normal, axis=0, keepdims=True),
        jnp.sum(grad_normed, axis=0, keepdims=True),
    )


def column_sum(values):
    return jnp.sum(values.astype(f32), axis=0, keepdims=True)


def mlp_kernel(scalars, live, vec, x2, h3, out_grad, *refs):
    own_in, own_out, *pieces = refs[:11]
    in_pieces, out_pieces = [pieces[0]] + pieces[1:5], [pieces[0]] + pieces[5:9]
    layer_out, acts, du, dm, e2, sums, w_in, w_out, sem_a, sem_b = refs[11:]
    in_copy = Weights(scalars, own_in, in_pieces, MLP_IN_PARTS, IN_CHUNK, w_in, sem_a)
    out_copy = Weights(scalars, own_out, out_pieces, MLP_OUT_PARTS, OUT_CHUNK, w_out, sem_b)
    in_copy.start()
    out_copy.start()
    e3 = live[0, 0] * out_grad[...].astype(f32)
    grad_branch = e3.astype(bf16)
    dm[...] = grad_branch
    sums[3:4, :] = column_sum(grad_branch)
    sums[4:8, :] = jnp.zeros((4, D), f32)
    normed = h3[...]
    in_copy.wait()
    out_copy.wait()
    x3 = x2[...] + vec[MLP_OUT_B : MLP_OUT_B + 1, :]
    e2[...] = x3
    back = None
    for part in range(4):
        columns = slice(part * D, (part + 1) * D)
        pre = nn(normed, w_in[:, columns]) + vec[MLP_IN_B + part : MLP_IN_B + part + 1, :]
        cdf = 0.5 * (1.0 + lax.erf(pre * (0.5**0.5)))
        act = (pre * cdf).astype(bf16)
        slope = cdf + pre * jnp.exp(-0.5 * pre * pre) * 0.3989422804014327
        acts[:, columns] = act
        grad = (slope * nt(grad_branch, w_out[columns, :])).astype(bf16)
        du[:, columns] = grad
        sums[4 + part : 5 + part, :] = column_sum(grad)
        e2[...] += nn(act, w_out[columns, :])
        piece = nt(grad, w_in[:, columns])
        back = piece if back is None else back + piece
    layer_out[...] = (live[0, 0] * e2[...]).astype(bf16)
    grad, gain_grad, shift_grad = norm_back(x2[...], vec[MLP_GAIN : MLP_GAIN + 1, :], back)
    sums[0:1, :] = gain_grad
    sums[1:2, :] = shift_grad
    sums[2:3, :] = jnp.zeros((1, D), f32)
    e2[...] = e3 + grad


def space_back_kernel(scalars, vec, e2, x1, qkv, *refs):
    own_proj, own_qkv, *pieces = refs[:7]
    dqkv, e1, dt2, sums, s0, s1, s2, s3, w_qkv, w_proj, da, sem_a, sem_b = refs[7:]
    proj_copy = Weights(scalars, own_proj, pieces, SPACE_PROJ_PARTS, SPACE_CHUNK, w_proj, sem_a)
    qkv_copy = Weights(scalars, own_qkv, pieces, SPACE_QKV_PARTS, SPACE_CHUNK, w_qkv, sem_b)
    proj_copy.start()
    qkv_copy.start()
    branch = e2[...].astype(bf16)
    dt2[...] = branch
    proj_copy.wait()
    da[...] = nt(branch, w_proj[...]).astype(bf16)
    attend_back(qkv, key_mask(False), da, dqkv)
    qkv_copy.wait()
    back = nt(dqkv[...], w_qkv[...])
    grad, gain_grad, shift_grad = norm_back(x1[...], vec[SPACE_GAIN : SPACE_GAIN + 1, :], back)
    total = e2[...] + grad
    e1[...] = total
    rounded = total.astype(bf16)
    for source, ref in enumerate((s0, s1, s2, s3)):
        ref[...] = tn(recv_to_frame(scalars[0], source), rounded).astype(bf16)
    sums[0:1, :] = gain_grad
    sums[1:2, :] = shift_grad
    sums[2:3, :] = column_sum(branch)
    sums[3:4, :] = column_sum(dqkv[:, :D])
    sums[4:5, :] = column_sum(dqkv[:, 2 * D :])
    sums[5:8, :] = jnp.zeros((3, D), f32)


def time_back_kernel(scalars, vec, tokens, qkv, r0, r1, r2, r3, *refs):
    own_fc, own_proj, own_qkv, packed, *pieces = refs[:12]
    fc_pieces, pieces = [packed] + pieces[:4], [packed] + pieces[4:]
    (
        dqkv, dt1, do1, sums, s0, s1, s2, s3, w_fc, w_proj, w_qkv, da, sem_a, sem_b, sem_c,
    ) = refs[12:]
    fc_copy = Weights(scalars, own_fc, fc_pieces, TIME_FC_PARTS, SPACE_CHUNK, w_fc, sem_a)
    proj_copy = Weights(scalars, own_proj, pieces, TIME_PROJ_PARTS, TIME_CHUNK, w_proj, sem_b)
    qkv_copy = Weights(scalars, own_qkv, pieces, TIME_QKV_PARTS, TIME_CHUNK, w_qkv, sem_c)
    fc_copy.start()
    proj_copy.start()
    qkv_copy.start()
    branch = sum(
        tn(place_to_send(source), ref[...]) for source, ref in enumerate((r0, r1, r2, r3))
    ).astype(bf16)
    dt1[...] = branch
    fc_copy.wait()
    projected = nt(branch, w_fc[...]).astype(bf16)
    do1[...] = projected
    proj_copy.wait()
    da[...] = nt(projected, w_proj[...]).astype(bf16)
    attend_back(qkv, key_mask(True), da, dqkv)
    qkv_copy.wait()
    back = nt(dqkv[...], w_qkv[...])
    grad, gain_grad, shift_grad = norm_back(
        tokens[...].astype(f32), vec[TIME_GAIN : TIME_GAIN + 1, :], back
    )
    rounded = grad.astype(bf16)
    for dest, ref in enumerate((s0, s1, s2, s3)):
        ref[...] = nn(place_to_send(dest), rounded).astype(bf16)
    sums[0:1, :] = gain_grad
    sums[1:2, :] = shift_grad
    sums[2:3, :] = column_sum(projected)
    sums[3:4, :] = column_sum(branch)
    sums[4:5, :] = column_sum(dqkv[:, :D])
    sums[5:6, :] = column_sum(dqkv[:, 2 * D :])
    sums[6:8, :] = jnp.zeros((2, D), f32)


def weight_grad_kernel(scalars, *refs, count, tables):
    inputs, (kept, sent) = refs[:-2], refs[-2:]
    core = scalars[0] % 2

    def store(shard, rows, columns, values):
        @pl.when(core == shard % 2)
        def _():
            kept[shard // 2, rows, columns] = values

        @pl.when(core != shard % 2)
        def _():
            sent[shard // 2, rows, columns] = values

    at = 0
    for index in range(count):
        left, right = inputs[2 * index : 2 * index + 2]
        shard_rows = left.shape[1] // 4
        for block in range(right.shape[1] // D):
            columns = slice(block * D, (block + 1) * D)
            total = tn(left[...], right[:, columns]).astype(bf16)
            for shard in range(4):
                values = total[shard * shard_rows : (shard + 1) * shard_rows, :]
                store(shard, slice(at, at + shard_rows), slice(0, D), values)
            at += shard_rows
    if tables:
        time, space, mlp = (ref[...] for ref in inputs[2 * count :])
        singles = jnp.concatenate([time[0:4], space[0:3], mlp[0:2], mlp[3:4]], axis=0)
        for ref in (kept, sent):
            for chip in range(2):
                ref[chip, at : at + EXTRA, :] = jnp.zeros((EXTRA, D), bf16)
        for shard in range(4):
            lanes = slice(shard * BLOCK, (shard + 1) * BLOCK)
            store(shard, slice(at, at + 10), slice(0, BLOCK), singles[:, lanes].astype(bf16))
            half = slice((shard % 2) * (D // 2), (shard % 2 + 1) * (D // 2))
            for row, pair in ((10, time[4:6]), (11, space[3:5])):
                values = pair[shard // 2 : shard // 2 + 1, half].astype(bf16)
                store(shard, slice(at + row, at + row + 1), slice(0, D // 2), values)
            values = mlp[4 + shard : 5 + shard, :].astype(bf16)
            store(shard, slice(at + 12, at + 13), slice(0, D), values)


def last_kernel(scalars, e1, r0, r1, r2, r3, out):
    total = e1[...]
    for source, ref in enumerate((r0, r1, r2, r3)):
        total = total + nn(recv_to_frame(scalars[0], source), ref[...])
    out[...] = total


def shape(rows, columns, kind):
    return jax.ShapeDtypeStruct((rows, columns), kind)


VMEM = pl.BlockSpec(memory_space=pltpu.MemorySpace.VMEM)
SMEM = pl.BlockSpec(memory_space=pltpu.MemorySpace.SMEM)
ANY = pl.BlockSpec(memory_space=pl.ANY)


def call(kernel, name, outs, specs, scratch, operands, microseconds, limit=48):
    return pl.pallas_call(
        kernel,
        name=name,
        out_shape=outs,
        in_specs=specs,
        out_specs=[VMEM] * len(outs),
        scratch_shapes=scratch,
        compiler_params=pltpu.CompilerParams(vmem_limit_bytes=limit << 20),
        cost_estimate=pl.CostEstimate(
            flops=int(microseconds * 1.1e9), transcendentals=0, bytes_accessed=1 << 20
        ),
    )(*operands)


def dma_sems(parts):
    return pltpu.SemaphoreType.DMA((1 + 3 * len(parts),))


def vmem(rows, columns, kind=bf16):
    return pltpu.VMEM((rows, columns), kind)


def place_forward(scalars, tokens, vec, owns, pieces):
    outs = [shape(ROWS, D, bf16), shape(ROWS, 3 * D, bf16), shape(ROWS, D, bf16)]
    outs += [shape(ROWS, D, bf16)] + [shape(CHUNK, D, bf16)] * 4
    return call(
        place_forward_kernel, "place_forward", outs, [SMEM, VMEM, VMEM] + [ANY] * 7,
        [vmem(D, 3 * D), vmem(D, D), dma_sems(TIME_QKV_PARTS), dma_sems(TIME_PROJ_PARTS)],
        (scalars, tokens, vec, *owns, *pieces), 11,
    )


def frame_forward(scalars, tokens, vec, received, owns, pieces):
    outs = [shape(ROWS, D, f32), shape(ROWS, D, bf16), shape(ROWS, 3 * D, bf16)]
    outs += [shape(ROWS, D, bf16), shape(ROWS, D, f32), shape(ROWS, D, bf16)]
    return call(
        frame_forward_kernel, "frame_forward", outs, [SMEM] + [VMEM] * 6 + [ANY] * 8,
        [
            vmem(D, D), vmem(D, 3 * D), vmem(D, D),
            dma_sems(TIME_FC_PARTS), dma_sems(SPACE_QKV_PARTS), dma_sems(SPACE_PROJ_PARTS),
        ],
        (scalars, tokens, vec, *received, *owns, *pieces), 13,
    )


def mlp_both(scalars, live, vec, x2, h3, out_grad, owns, in_pieces, out_pieces):
    outs = [
        shape(ROWS, D, bf16), shape(ROWS, FF, bf16), shape(ROWS, FF, bf16),
        shape(ROWS, D, bf16), shape(ROWS, D, f32), shape(8, D, f32),
    ]
    return call(
        mlp_kernel, "mlp_both", outs, [SMEM, SMEM] + [VMEM] * 4 + [ANY] * 11,
        [vmem(D, FF), vmem(FF, D), dma_sems(MLP_IN_PARTS), dma_sems(MLP_OUT_PARTS)],
        (scalars, live, vec, x2, h3, out_grad, *owns, *in_pieces, *out_pieces[1:]), 18, 56,
    )


def space_back(scalars, vec, e2, x1, qkv, owns, pieces):
    outs = [shape(ROWS, 3 * D, bf16), shape(ROWS, D, f32), shape(ROWS, D, bf16)]
    outs += [shape(8, D, f32)] + [shape(CHUNK, D, bf16)] * 4
    return call(
        space_back_kernel, "space_back", outs, [SMEM] + [VMEM] * 4 + [ANY] * 7,
        [
            vmem(D, 3 * D), vmem(D, D), vmem(ROWS, D),
            dma_sems(SPACE_PROJ_PARTS), dma_sems(SPACE_QKV_PARTS),
        ],
        (scalars, vec, e2, x1, qkv, *owns, *pieces), 20,
    )


def time_back(scalars, vec, tokens, qkv, received, owns, fc_pieces, pieces):
    outs = [shape(ROWS, 3 * D, bf16), shape(ROWS, D, bf16), shape(ROWS, D, bf16)]
    outs += [shape(8, D, f32)] + [shape(CHUNK, D, bf16)] * 4
    return call(
        time_back_kernel, "time_back", outs, [SMEM] + [VMEM] * 7 + [ANY] * 12,
        [
            vmem(D, D), vmem(D, D), vmem(D, 3 * D), vmem(ROWS, D),
            dma_sems(TIME_FC_PARTS), dma_sems(TIME_PROJ_PARTS), dma_sems(TIME_QKV_PARTS),
        ],
        (scalars, vec, tokens, qkv, *received, *owns, *fc_pieces, *pieces[1:]), 21,
    )


def weight_grads(name, scalars, groups, tables=()):
    rows = sum(g[0].shape[1] // 4 * (g[1].shape[1] // D) for g in groups)
    flat = [array for group in groups for array in group] + list(tables)
    rows += EXTRA if tables else 0
    kernel = functools.partial(weight_grad_kernel, count=len(groups), tables=len(tables))
    return call(
        kernel, name, [jax.ShapeDtypeStruct((2, rows, D), bf16)] * 2, [SMEM] + [VMEM] * len(flat),
        [], (scalars, *flat), rows / 128,
    )


def last_sum(scalars, e1, received):
    return call(
        last_kernel, "last_sum", [shape(ROWS, D, f32)], [SMEM] + [VMEM] * 5, [],
        (scalars, e1, *received), 2,
    )[0]


def flip(array, axis, bit, size):
    return lax.ppermute(array, axis, [(at, at ^ bit) for at in range(size)])


def pick(array, at):
    return lax.dynamic_index_in_dim(array, at, 0, keepdims=False)


def add_rounded(left, right):
    return (left.astype(f32) + right.astype(f32)).astype(bf16)


def after(value, *others):
    return lax.optimization_barrier((value,) + others)[0]


def halves_of(own, half_at):
    return lax.dynamic_slice_in_dim(own, half_at * (own.shape[0] // 2), own.shape[0] // 2, 0)


class Reduce:
    def __init__(self, parts, order, group_at, replica_at, ring_size):
        self.kept, sent = parts
        self.group_at, self.replica_at = group_at, replica_at
        self.ring_size = ring_size
        self.steps = [("sum", -1)] + [("sum", bit) for bit in order]
        self.steps += [("gather", bit) for bit in reversed(order) if bit]
        self.flying = flip(sent, "group", 1, 4)

    def place(self, bit):
        return (self.replica_at // bit) % 2

    def start(self, *others):
        kind, bit = self.steps[0]
        if kind == "gather":
            sent = self.current
        elif bit == 0:
            chip = self.group_at // 2
            sent, self.kept = pick(self.current, 1 - chip), pick(self.current, chip)
        else:
            rows = self.current.shape[-2] // 2
            mine = self.place(bit)
            sent = lax.dynamic_slice_in_dim(self.current, (1 - mine) * rows, rows, -2 % self.current.ndim)
            self.kept = lax.dynamic_slice_in_dim(self.current, mine * rows, rows, -2 % self.current.ndim)
        if others:
            sent = after(sent, *others)
        axis = ("group", 2, 4) if bit == 0 else ("replica", bit, self.ring_size)
        self.flying = flip(sent, *axis)

    def finish(self, *others):
        kind, bit = self.steps.pop(0)
        got = after(self.flying, *others) if others else self.flying
        if kind == "sum":
            self.current = add_rounded(self.kept, got)
        else:
            mine = self.place(bit)
            self.current = jnp.where(
                mine == 0,
                jnp.concatenate([self.current, got], 0),
                jnp.concatenate([got, self.current], 0),
            )
        return self.current

    def advance(self, *others):
        result = self.finish(*others)
        if self.steps:
            self.start()
        return result


def block(array, at):
    return array[:, at * D : (at + 1) * D]


def unpack_grad(summed, blocks):
    return summed.reshape(blocks, BLOCK, D).transpose(1, 0, 2).reshape(BLOCK, blocks * D).astype(f32)


def exchange(chunks):
    return [chunks[0]] + [flip(chunks[d], "group", d, 4) for d in range(1, 4)]


def build(mesh):
    ring_size = mesh.shape["replica"]

    def on_device(tokens, out_grad, slot_mask, *shards):
        (
            time_norm_gain, time_norm_shift, time_qkv, time_qv_bias, time_proj, time_proj_bias,
            time_fc, time_fc_bias, space_norm_gain, space_norm_shift, space_qkv, space_qv_bias,
            space_proj, space_proj_bias, mlp_norm_gain, mlp_norm_shift, mlp_in, mlp_in_bias,
            mlp_out, mlp_out_bias,
        ) = shards
        group_at = lax.axis_index("group")
        replica_at = lax.axis_index("replica")
        half_at = replica_at % 2
        scalars = jnp.stack([group_at, half_at]).astype(jnp.int32)
        live = slot_mask.astype(f32).reshape(1, 1)
        vectors = [
            time_norm_gain, time_norm_shift, time_proj_bias, time_fc_bias, space_norm_gain,
            space_norm_shift, space_proj_bias, mlp_norm_gain, mlp_norm_shift, mlp_out_bias,
            time_qv_bias, space_qv_bias, mlp_in_bias,
        ]
        cross = functools.partial(flip, axis="group", bit=2, size=4)
        near = functools.partial(flip, axis="group", bit=1, size=4)
        relay = functools.partial(flip, axis="replica", bit=1, size=ring_size)
        flat = jnp.pad(jnp.concatenate(vectors), (0, 8 * D - VECTOR_ROWS * BLOCK)).reshape(8, D)
        time_half = jnp.where(
            half_at == 0,
            jnp.concatenate([block(time_qkv, 0), block(time_qkv, 1), flat]),
            jnp.concatenate([block(time_qkv, 2), time_proj, flat]),
        )
        time_direct = cross(time_half)
        token_pieces = tokens[0].transpose(1, 0, 2).reshape(4, 49, 2, D)
        got = exchange([pick(token_pieces, group_at ^ d) for d in range(4)])
        place_tokens = jnp.pad(jnp.concatenate(got, axis=1), ((0, 3), (0, 0), (0, 0)))
        place_tokens = place_tokens.reshape(ROWS, D)

        packed = jnp.concatenate(
            [
                block(time_qkv, 0), block(time_qkv, 1), block(time_qkv, 2), time_proj,
                block(space_qkv, 0), block(space_qkv, 1), time_fc, block(space_qkv, 2), space_proj,
                block(mlp_in, 0), block(mlp_in, 1), block(mlp_in, 2), block(mlp_in, 3), mlp_out,
                flat,
            ]
        )

        def half_of(chunk):
            first, rows = chunk
            return lax.dynamic_slice_in_dim(packed, first + half_at * (rows // 2), rows // 2, 0)

        partner = near(packed)
        time_across = near(time_direct)
        time_relayed = relay(time_direct)
        time_pieces = (partner, time_direct, time_relayed, time_across, near(time_relayed))
        space_direct = cross(after(half_of(SPACE_CHUNK), time_direct, got[2], got[3]))
        in_direct = cross(after(half_of(IN_CHUNK), space_direct))
        out_direct = cross(after(half_of(OUT_CHUNK), in_direct))

        held = [flat, partner[VECTOR_AT:], time_direct[384:], time_across[384:]]
        held = jnp.stack(held).reshape(4, 8 * D)[:, : VECTOR_ROWS * BLOCK]
        tables = jnp.stack([pick(held, group_at ^ shard) for shard in range(4)]).astype(f32)
        tables = tables.reshape(4, VECTOR_ROWS, BLOCK)
        vec = jnp.concatenate(
            [
                tables[:, :10].transpose(1, 0, 2).reshape(10, D),
                tables[:, 10:12].reshape(2, D),
                tables[:, 12:14].reshape(2, D),
                tables[:, 14:18].reshape(4, D),
                jnp.zeros((6, D), f32),
            ]
        )
        pads = ((0, 0), (0, HALF - PLACES), (0, 0))
        frame_tokens = jnp.pad(tokens[0], pads).reshape(ROWS, D)
        frame_grad = jnp.pad(out_grad[0], pads).reshape(ROWS, D)

        h1, qkv1, a1, o1, *sends = place_forward(
            scalars, after(place_tokens, space_direct), vec, (time_qkv, time_proj), time_pieces
        )
        received = exchange(sends)
        space_relayed = relay(space_direct)
        space_pieces = (
            partner, space_direct, space_relayed, near(space_direct),
            near(after(space_relayed, o1)),
        )
        x1, h2, qkv2, a2, x2, h3 = frame_forward(
            scalars, after(frame_tokens, in_direct), vec, received,
            (time_fc, space_qkv, space_proj), space_pieces,
        )
        in_relayed = relay(in_direct)
        in_pieces = (
            partner, in_direct, in_relayed, near(after(in_direct, x2)), near(after(in_relayed, x2)),
        )
        out_direct = after(out_direct, x2)
        out_relayed = relay(out_direct)
        out_pieces = (partner, out_direct, out_relayed, near(out_direct), near(out_relayed))
        layer_out, act, du, dm, e2, sums3 = mlp_both(
            scalars, live, vec, x2, h3, frame_grad, (mlp_in, mlp_out), in_pieces, out_pieces
        )
        layer_out = layer_out.reshape(2, HALF, D)[None, :, :PLACES]

        chunk = functools.partial(
            Reduce, group_at=group_at, replica_at=replica_at, ring_size=ring_size
        )
        bits = [1 << at for at in range(ring_size.bit_length() - 1)]
        along = [0] + bits
        first_y = bits[:1] + [0] + bits[1:]
        first_z = bits[1:2] + [0] + bits[:1] + bits[2:]

        way_out = chunk(weight_grads("mlp_out_grad", scalars, [(act, dm)]), along)
        way_in = chunk(
            weight_grads("mlp_in_grad", scalars, [(h3, after(du, way_out.kept))]), first_y
        )
        one = way_out.advance(way_in.kept)
        two = way_in.advance(one)
        dqkv2, e1, dt2, sums2, *sends = space_back(
            scalars, vec, after(e2, one, two), x1, qkv2, (space_proj, space_qkv), space_pieces
        )
        received = exchange(sends)
        one = way_out.advance(e1)
        two = way_in.advance(one)
        way_space = chunk(
            weight_grads("space_grad", scalars, [(h2, after(dqkv2, two)), (a2, dt2)]), first_z
        )
        three = way_space.advance(two)
        dqkv1, dt1, do1, sums1, *sends = time_back(
            scalars, vec, after(place_tokens, three), qkv1, received,
            (time_fc, time_proj, time_qkv), space_pieces, time_pieces,
        )
        received = exchange(sends)
        one = way_out.advance(dqkv1)
        two = way_in.advance(one)
        three = way_space.advance(two)
        way_time = chunk(weight_grads("time_grad", scalars, [(h1, after(dqkv1, three))]), along)
        way_small = chunk(
            weight_grads(
                "time_small_grad", scalars, [(a1, after(do1, way_time.kept)), (o1, dt1)],
                (sums1, sums2, sums3),
            ),
            first_y,
        )
        last = way_time.advance(way_small.kept)
        last = way_small.advance(last)
        tokens_grad = last_sum(scalars, after(e1, last), received)
        last = tokens_grad
        tokens_grad = tokens_grad.reshape(2, HALF, D)[None, :, :PLACES]
        ways = [way_out, way_in, way_space, way_time, way_small]
        while any(way.steps for way in ways):
            for way in ways:
                if way.steps:
                    last = way.advance(last)
        sum_out, sum_in, sum_space, sum_time, sum_small = (way.current for way in ways)
        vectors = sum_small[384:].astype(f32)
        ones = vectors[:10, :BLOCK]
        return (
            layer_out, tokens_grad, ones[0], ones[1], unpack_grad(sum_time, 3),
            vectors[10, : D // 2], sum_small[:192].astype(f32), ones[2],
            sum_small[192:384].astype(f32), ones[3],
            ones[4], ones[5], unpack_grad(sum_space[:576], 3), vectors[11, : D // 2],
            sum_space[576:768].astype(f32), ones[6], ones[7], ones[8], unpack_grad(sum_in, 4),
            vectors[12], sum_out.astype(f32), ones[9],
        )

    return on_device


def solution(mesh):
    rows = P("group", None)
    vector = P("group")
    batch = P("replica", "group", None, None)
    params = (
        vector, vector, rows, vector, rows, vector, rows, vector, vector, vector, rows, vector,
        rows, vector, vector, vector, rows, vector, rows, vector,
    )
    return jax.shard_map(
        build(mesh),
        mesh=mesh,
        in_specs=(batch, batch, P("replica")) + params,
        out_specs=(batch, batch) + params,
        check_vma=False,
    )
```

```python
import functools

import jax
import jax.numpy as jnp
from jax import lax
from jax.experimental import pallas as pl
from jax.experimental.pallas import tpu as pltpu
from jax.sharding import PartitionSpec as P

D = 768
FF = 3072
HEADS = 12
HEAD_DIM = 64
PLACES = 196
BLOCK = 192
CHUNK = 104
HALF = 208
ROWS = 416
epsilon = 1e-06
bf16 = jnp.bfloat16
f32 = jnp.float32

TIME_GAIN, TIME_SHIFT, TIME_PROJ_B, TIME_FC_B, SPACE_GAIN, SPACE_SHIFT, SPACE_PROJ_B = range(7)
MLP_GAIN, MLP_SHIFT, MLP_OUT_B = 7, 8, 9
TIME_QV, SPACE_QV, MLP_IN_B = 10, 12, 14
VECTOR_ROWS = 18
EXTRA = 64
LIMITS = {
    "place_forward": 10, "frame_forward": 14, "mlp_both": 28, "space_back": 19, "time_back": 13,
    "mlp_out_grad": 8, "mlp_in_grad": 8, "space_grad": 7, "pack_rest": 8, "time_projections": 6,
}
ORDERS = {"o": "xyuw", "i": "yuxw", "s": "uxyw", "p": "yxuw", "t": "yxuw"}
SCHEDULE = ("oi", "", "oi", "spi", "", "iptosip", "oistposi" + "tpotsop" + "tsptst")

TIME_QKV_PARTS = ((0, 0, 192, 0, 0), (0, 192, 192, 0, 1), (1, 0, 192, 0, 2))
TIME_PROJ_PARTS = ((1, 192, 192, 0, 0),)
SPACE_QKV_PARTS = ((0, 0, 192, 0, 0), (0, 192, 192, 0, 1), (1, 96, 192, 0, 2))
SPACE_PROJ_PARTS = ((1, 288, 192, 0, 0),)
TIME_FC_PARTS = ((0, 384, 96, 0, 0), (1, 0, 96, 96, 0))
MLP_IN_PARTS = ((0, 0, 192, 0, 0), (0, 192, 192, 0, 1), (1, 0, 192, 0, 2), (1, 192, 192, 0, 3))
MLP_OUT_PARTS = ((0, 0, 384, 0, 0), (1, 0, 384, 384, 0))
TIME_CHUNK, SPACE_CHUNK, IN_CHUNK, OUT_CHUNK = (0, 768), (768, 960), (1728, 768), (2496, 768)
VECTOR_AT = 3264


def nn(left, right):
    return lax.dot_general(left, right, (((1,), (0,)), ((), ())), preferred_element_type=f32)


def nt(left, right):
    return lax.dot_general(left, right, (((1,), (1,)), ((), ())), preferred_element_type=f32)


def tn(left, right):
    return lax.dot_general(left, right, (((0,), (0,)), ((), ())), preferred_element_type=f32)


def norm_parts(values):
    centred = values - jnp.mean(values, axis=-1, keepdims=True)
    inverse = lax.rsqrt(jnp.mean(centred * centred, axis=-1, keepdims=True) + epsilon)
    return centred * inverse, inverse


class Weights:
    def __init__(self, scalars, own, pieces, parts, chunk, target, sems):
        self.scalars, self.own, self.pieces, self.parts = scalars, own, pieces, parts
        self.chunk, self.target, self.sems = chunk, target, sems
        self.shard_rows = own.shape[0]

    def base(self, flipped):
        at = (self.scalars[0] ^ flipped) * self.shard_rows
        return pl.multiple_of(at, self.shard_rows)

    def copy(self, source, part, flipped, at):
        half, row, rows, block_row, column = part
        return pltpu.make_async_copy(
            source.at[pl.ds(row, rows), :],
            self.target.at[pl.ds(self.base(flipped) + block_row, rows), pl.ds(column * D, D)],
            self.sems.at[at],
        )

    def own_copy(self):
        target = self.target.at[pl.ds(self.base(0), self.shard_rows), :]
        return pltpu.make_async_copy(self.own, target, self.sems.at[0])

    def start(self):
        packed, direct, relayed, across, across_relayed = self.pieces
        self.own_copy().start()
        y = self.scalars[1]
        first, chunk_rows = self.chunk
        at = 1
        for part in self.parts:
            half, row, rows, block_row, column = part
            whole = (half, first + row + half * (chunk_rows // 2), rows, block_row, column)
            self.copy(packed, whole, 1, at).start()

            @pl.when(y == half)
            def _():
                self.copy(direct, part, 2, at + 1).start()
                self.copy(across, part, 3, at + 2).start()

            @pl.when(y != half)
            def _():
                self.copy(relayed, part, 2, at + 1).start()
                self.copy(across_relayed, part, 3, at + 2).start()

            at += 3

    def wait(self):
        direct, across = self.pieces[1], self.pieces[3]
        self.own_copy().wait()
        at = 1
        for part in self.parts:
            self.copy(direct, part, 1, at).wait()
            self.copy(direct, part, 2, at + 1).wait()
            self.copy(across, part, 3, at + 2).wait()
            at += 3


def lane_half(second):
    lane = lax.broadcasted_iota(jnp.int32, (HALF, 128), 1)
    return (lane >= 64) if second else (lane < 64)


def masked(values, second):
    return jnp.where(lane_half(second), values, jnp.zeros_like(values))


def key_mask(same_place):
    key = lax.broadcasted_iota(jnp.int32, (HALF, HALF), 0)
    query = lax.broadcasted_iota(jnp.int32, (HALF, HALF), 1)
    allowed = (key // 8 == query // 8) if same_place else (key < PLACES)
    return jnp.where(allowed, 0.0, -1e30).astype(f32)


def both_heads(pair):
    return jnp.concatenate([masked(pair, False), masked(pair, True)], axis=0)


def probs_of(keys, query_pair, mask):
    scores = nt(keys, query_pair).reshape(2, HALF, HALF) + mask[None]
    weights = jnp.exp(scores - jnp.max(scores, axis=1, keepdims=True))
    return weights * (1.0 / jnp.sum(weights, axis=1, keepdims=True))


def flat_heads(values):
    return values.astype(bf16).reshape(2 * HALF, HALF)


def attend(qkv_ref, mask, out_ref):
    def pair_step(pair, carry):
        column = pl.multiple_of(pair * 128, 128)
        for part in range(2):
            rows = pl.ds(part * HALF, HALF)
            query = qkv_ref[rows, pl.ds(column, 128)] * bf16(HEAD_DIM**-0.5)
            key_part = qkv_ref[rows, pl.ds(D + column, 128)]
            value_part = qkv_ref[rows, pl.ds(2 * D + column, 128)]
            mixed = []
            for second in (False, True):
                scores = nt(masked(key_part, second), query) + mask
                weights = jnp.exp(scores - jnp.max(scores, axis=0, keepdims=True))
                probs = weights * (1.0 / jnp.sum(weights, axis=0, keepdims=True))
                mixed.append(tn(value_part, probs.astype(bf16)))
            mixed = jnp.concatenate([mixed[0][:64], mixed[1][64:]], axis=0)
            out_ref[rows, pl.ds(column, 128)] = mixed.T.astype(bf16)
        return carry

    lax.fori_loop(0, HEADS // 2, pair_step, 0)


def attend_back(qkv_ref, mask, grad_ref, out_ref):
    first = lane_half(False)

    def pair_step(pair, carry):
        column = pl.multiple_of(pair * 128, 128)
        for part in range(2):
            rows = pl.ds(part * HALF, HALF)
            query = qkv_ref[rows, pl.ds(column, 128)] * bf16(HEAD_DIM**-0.5)
            keys = both_heads(qkv_ref[rows, pl.ds(D + column, 128)])
            values = both_heads(qkv_ref[rows, pl.ds(2 * D + column, 128)])
            grad = grad_ref[rows, pl.ds(column, 128)]
            probs = probs_of(keys, query, mask)
            grad_probs = nt(values, grad).reshape(2, HALF, HALF)
            centre = jnp.sum(grad_probs * probs, axis=1, keepdims=True)
            grad_scores = flat_heads(probs * (grad_probs - centre))
            grad_query = tn(keys, grad_scores).T * HEAD_DIM**-0.5
            out_ref[rows, pl.ds(column, 128)] = grad_query.astype(bf16)
            grad_key = nn(grad_scores, query)
            grad_key = jnp.where(first, grad_key[:HALF], grad_key[HALF:])
            out_ref[rows, pl.ds(D + column, 128)] = grad_key.astype(bf16)
            grad_value = nn(flat_heads(probs), grad)
            grad_value = jnp.where(first, grad_value[:HALF], grad_value[HALF:])
            out_ref[rows, pl.ds(2 * D + column, 128)] = grad_value.astype(bf16)
        return carry

    lax.fori_loop(0, HEADS // 2, pair_step, 0)


def project_qkv(normed, weight, vec, qv_row, out_ref):
    for member in range(3):
        packed = nn(normed, weight[:, member * D : (member + 1) * D])
        if member != 1:
            row = qv_row + member // 2
            packed = packed + vec[row : row + 1, :]
        out_ref[:, member * D : (member + 1) * D] = packed.astype(bf16)


def place_to_send(dest):
    local = lax.broadcasted_iota(jnp.int32, (CHUNK, ROWS), 0)
    col = lax.broadcasted_iota(jnp.int32, (CHUNK, ROWS), 1)
    source = (local // 2) * 8 + dest * 2 + local % 2
    return ((col == source) & (local < 98)).astype(bf16)


def recv_to_frame(group_at, source):
    row = lax.broadcasted_iota(jnp.int32, (ROWS, CHUNK), 0)
    col = lax.broadcasted_iota(jnp.int32, (ROWS, CHUNK), 1)
    second = (row >= HALF).astype(jnp.int32)
    spot = row - second * HALF
    local = (spot - (group_at ^ source) * 49) * 2 + second
    inside = (spot >= (group_at ^ source) * 49) & (spot < ((group_at ^ source) + 1) * 49)
    return ((col == local) & inside).astype(bf16)


def place_forward_kernel(
    scalars, tokens, vec, *refs
):
    own_qkv, own_proj, *pieces = refs[:7]
    h1, qkv, mixed, o1, *rest = refs[7:]
    sends, (w_qkv, w_proj, sem_a, sem_b) = rest[:4], rest[4:]
    qkv_copy = Weights(scalars, own_qkv, pieces, TIME_QKV_PARTS, TIME_CHUNK, w_qkv, sem_a)
    proj_copy = Weights(scalars, own_proj, pieces, TIME_PROJ_PARTS, TIME_CHUNK, w_proj, sem_b)
    qkv_copy.start()
    proj_copy.start()
    normal, unused = norm_parts(tokens[...].astype(f32))
    normed = (normal * vec[TIME_GAIN : TIME_GAIN + 1, :] + vec[TIME_SHIFT : TIME_SHIFT + 1, :])
    normed = normed.astype(bf16)
    h1[...] = normed
    qkv_copy.wait()
    project_qkv(normed, w_qkv, vec, TIME_QV, qkv)
    attend(qkv, key_mask(True), mixed)
    proj_copy.wait()
    out = (nn(mixed[...], w_proj[...]) + vec[TIME_PROJ_B : TIME_PROJ_B + 1, :]).astype(bf16)
    o1[...] = out
    for dest in range(4):
        sends[dest][...] = nn(place_to_send(dest), out).astype(bf16)


def frame_forward_kernel(scalars, tokens, vec, r0, r1, r2, r3, *refs):
    own_fc, own_qkv, own_proj, *pieces = refs[:8]
    x1, h2, qkv, mixed, x2, h3 = refs[8:14]
    w_fc, w_qkv, w_proj, sem_a, sem_b, sem_c = refs[14:]
    fc_copy = Weights(scalars, own_fc, pieces, TIME_FC_PARTS, SPACE_CHUNK, w_fc, sem_a)
    qkv_copy = Weights(scalars, own_qkv, pieces, SPACE_QKV_PARTS, SPACE_CHUNK, w_qkv, sem_b)
    proj_copy = Weights(scalars, own_proj, pieces, SPACE_PROJ_PARTS, SPACE_CHUNK, w_proj, sem_c)
    fc_copy.start()
    qkv_copy.start()
    proj_copy.start()
    group_at = scalars[0]
    received = sum(
        nn(recv_to_frame(group_at, source), ref[...]) for source, ref in enumerate((r0, r1, r2, r3))
    ).astype(bf16)
    fc_copy.wait()
    branch = nn(received, w_fc[...]) + vec[TIME_FC_B : TIME_FC_B + 1, :]
    after = tokens[...].astype(f32) + branch
    x1[...] = after
    normal, unused = norm_parts(after)
    normed = normal * vec[SPACE_GAIN : SPACE_GAIN + 1, :] + vec[SPACE_SHIFT : SPACE_SHIFT + 1, :]
    normed = normed.astype(bf16)
    h2[...] = normed
    qkv_copy.wait()
    project_qkv(normed, w_qkv, vec, SPACE_QV, qkv)
    attend(qkv, key_mask(False), mixed)
    proj_copy.wait()
    after = x1[...] + (nn(mixed[...], w_proj[...]) + vec[SPACE_PROJ_B : SPACE_PROJ_B + 1, :])
    x2[...] = after
    normal, unused = norm_parts(after)
    normed = normal * vec[MLP_GAIN : MLP_GAIN + 1, :] + vec[MLP_SHIFT : MLP_SHIFT + 1, :]
    h3[...] = normed.astype(bf16)


def norm_back(values, gain, grad_normed):
    normal, inverse = norm_parts(values)
    scaled = grad_normed * gain
    mean = jnp.mean(scaled, axis=-1, keepdims=True)
    along = jnp.mean(scaled * normal, axis=-1, keepdims=True)
    grad = inverse * (scaled - mean - normal * along)
    return (
        grad,
        jnp.sum(grad_normed * normal, axis=0, keepdims=True),
        jnp.sum(grad_normed, axis=0, keepdims=True),
    )


def column_sum(values):
    return jnp.sum(values.astype(f32), axis=0, keepdims=True)


def mlp_kernel(scalars, live, vec, x2, h3, out_grad, *refs):
    own_in, own_out, *pieces = refs[:11]
    in_pieces, out_pieces = [pieces[0]] + pieces[1:5], [pieces[0]] + pieces[5:9]
    layer_out, acts, du, dm, e2, sums, w_in, w_out, sem_a, sem_b = refs[11:]
    in_copy = Weights(scalars, own_in, in_pieces, MLP_IN_PARTS, IN_CHUNK, w_in, sem_a)
    out_copy = Weights(scalars, own_out, out_pieces, MLP_OUT_PARTS, OUT_CHUNK, w_out, sem_b)
    in_copy.start()
    out_copy.start()
    e3 = live[0, 0] * out_grad[...].astype(f32)
    grad_branch = e3.astype(bf16)
    dm[...] = grad_branch
    sums[3:4, :] = column_sum(grad_branch)
    sums[4:8, :] = jnp.zeros((4, D), f32)
    normed = h3[...]
    in_copy.wait()
    out_copy.wait()
    x3 = x2[...] + vec[MLP_OUT_B : MLP_OUT_B + 1, :]
    e2[...] = x3
    back = None
    for part in range(4):
        columns = slice(part * D, (part + 1) * D)
        pre = nn(normed, w_in[:, columns]) + vec[MLP_IN_B + part : MLP_IN_B + part + 1, :]
        cdf = 0.5 * (1.0 + lax.erf(pre * (0.5**0.5)))
        act = (pre * cdf).astype(bf16)
        slope = cdf + pre * jnp.exp(-0.5 * pre * pre) * 0.3989422804014327
        acts[:, columns] = act
        grad = (slope * nt(grad_branch, w_out[columns, :])).astype(bf16)
        du[:, columns] = grad
        sums[4 + part : 5 + part, :] = column_sum(grad)
        e2[...] += nn(act, w_out[columns, :])
        piece = nt(grad, w_in[:, columns])
        back = piece if back is None else back + piece
    layer_out[...] = (live[0, 0] * e2[...]).astype(bf16)
    grad, gain_grad, shift_grad = norm_back(x2[...], vec[MLP_GAIN : MLP_GAIN + 1, :], back)
    sums[0:1, :] = gain_grad
    sums[1:2, :] = shift_grad
    sums[2:3, :] = jnp.zeros((1, D), f32)
    e2[...] = e3 + grad


def space_back_kernel(scalars, vec, e2, x1, qkv, *refs):
    own_proj, own_qkv, *pieces = refs[:7]
    dqkv, e1, dt2, sums, s0, s1, s2, s3, w_qkv, w_proj, da, sem_a, sem_b = refs[7:]
    proj_copy = Weights(scalars, own_proj, pieces, SPACE_PROJ_PARTS, SPACE_CHUNK, w_proj, sem_a)
    qkv_copy = Weights(scalars, own_qkv, pieces, SPACE_QKV_PARTS, SPACE_CHUNK, w_qkv, sem_b)
    proj_copy.start()
    qkv_copy.start()
    branch = e2[...].astype(bf16)
    dt2[...] = branch
    proj_copy.wait()
    da[...] = nt(branch, w_proj[...]).astype(bf16)
    attend_back(qkv, key_mask(False), da, dqkv)
    qkv_copy.wait()
    back = nt(dqkv[...], w_qkv[...])
    grad, gain_grad, shift_grad = norm_back(x1[...], vec[SPACE_GAIN : SPACE_GAIN + 1, :], back)
    total = e2[...] + grad
    e1[...] = total
    rounded = total.astype(bf16)
    for source, ref in enumerate((s0, s1, s2, s3)):
        ref[...] = tn(recv_to_frame(scalars[0], source), rounded).astype(bf16)
    sums[0:1, :] = gain_grad
    sums[1:2, :] = shift_grad
    sums[2:3, :] = column_sum(branch)
    sums[3:4, :] = column_sum(dqkv[:, :D])
    sums[4:5, :] = column_sum(dqkv[:, 2 * D :])
    sums[5:8, :] = jnp.zeros((3, D), f32)


def time_projections_kernel(scalars, r0, r1, r2, r3, *refs):
    own_fc, own_proj, packed, *pieces = refs[:11]
    dt1, do1, da1, sums, w_fc, w_proj, sem_a, sem_b = refs[11:]
    fc_pieces, pieces = [packed] + pieces[:4], [packed] + pieces[4:]
    fc_copy = Weights(scalars, own_fc, fc_pieces, TIME_FC_PARTS, SPACE_CHUNK, w_fc, sem_a)
    proj_copy = Weights(scalars, own_proj, pieces, TIME_PROJ_PARTS, TIME_CHUNK, w_proj, sem_b)
    fc_copy.start()
    proj_copy.start()
    branch = sum(
        tn(place_to_send(source), ref[...]) for source, ref in enumerate((r0, r1, r2, r3))
    ).astype(bf16)
    dt1[...] = branch
    fc_copy.wait()
    projected = nt(branch, w_fc[...]).astype(bf16)
    do1[...] = projected
    proj_copy.wait()
    da1[...] = nt(projected, w_proj[...]).astype(bf16)
    sums[0:1, :] = column_sum(projected)
    sums[1:2, :] = column_sum(branch)
    sums[2:8, :] = jnp.zeros((6, D), f32)


def time_back_kernel(scalars, vec, tokens, qkv, da1, early_sums, own_qkv, *refs):
    pieces, (dqkv, sums, s0, s1, s2, s3, w_qkv, sem) = refs[:5], refs[5:]
    qkv_copy = Weights(scalars, own_qkv, pieces, TIME_QKV_PARTS, TIME_CHUNK, w_qkv, sem)
    qkv_copy.start()
    attend_back(qkv, key_mask(True), da1, dqkv)
    qkv_copy.wait()
    back = nt(dqkv[...], w_qkv[...])
    grad, gain_grad, shift_grad = norm_back(
        tokens[...].astype(f32), vec[TIME_GAIN : TIME_GAIN + 1, :], back
    )
    rounded = grad.astype(bf16)
    for dest, ref in enumerate((s0, s1, s2, s3)):
        ref[...] = nn(place_to_send(dest), rounded).astype(bf16)
    sums[0:1, :] = gain_grad
    sums[1:2, :] = shift_grad
    sums[2:4, :] = early_sums[0:2, :]
    sums[4:5, :] = column_sum(dqkv[:, :D])
    sums[5:6, :] = column_sum(dqkv[:, 2 * D :])
    sums[6:8, :] = jnp.zeros((2, D), f32)


def weight_grad_kernel(scalars, *refs, count, tables):
    inputs, (kept, sent, turned, ordered) = refs[:-4], refs[-4:]
    core = scalars[0] % 2

    def store(shard, rows, columns, values):
        @pl.when(core == shard % 2)
        def _():
            kept[shard // 2, rows, columns] = values

        @pl.when(core != shard % 2)
        def _():
            sent[shard // 2, rows, columns] = values

    at = 0
    for index in range(count):
        left, right = inputs[2 * index : 2 * index + 2]
        width = left.shape[1]
        shard_rows = width // 4
        if shard_rows % 128 == 0:
            for spot in range(4):
                shard = 2 * (spot % 2) + (core if spot < 2 else 1 - core)
                source = pl.ds(pl.multiple_of(shard * shard_rows, shard_rows), shard_rows)
                target = kept if spot < 2 else sent
                for block in range(right.shape[1] // D):
                    total = tn(left[:, source], right[:, block * D : (block + 1) * D])
                    rows = slice(at + block * shard_rows, at + (block + 1) * shard_rows)
                    target[spot % 2, rows, :] = total.astype(bf16)
            at += shard_rows * (right.shape[1] // D)
            continue
        turned[0:width, :] = left[...].T
        for spot in range(4):
            shard = 2 * (spot % 2) + (core if spot < 2 else 1 - core)
            source = pl.ds(pl.multiple_of(shard * shard_rows, shard_rows), shard_rows)
            ordered[spot * shard_rows : (spot + 1) * shard_rows, :] = turned[source, :]
        for block in range(right.shape[1] // D):
            columns = slice(block * D, (block + 1) * D)
            total = nn(ordered[...], right[:, columns]).astype(bf16)
            for spot in range(4):
                target = kept if spot < 2 else sent
                target[spot % 2, at : at + shard_rows, :] = total[
                    spot * shard_rows : (spot + 1) * shard_rows, :
                ]
            at += shard_rows
    if tables:
        time, space, mlp = (ref[...] for ref in inputs[2 * count :])
        singles = jnp.concatenate([time[0:4], space[0:3], mlp[0:2], mlp[3:4]], axis=0)
        for ref in (kept, sent):
            for chip in range(2):
                ref[chip, at : at + EXTRA, :] = jnp.zeros((EXTRA, D), bf16)
        for shard in range(4):
            lanes = slice(shard * BLOCK, (shard + 1) * BLOCK)
            store(shard, slice(at, at + 10), slice(0, BLOCK), singles[:, lanes].astype(bf16))
            half = slice((shard % 2) * (D // 2), (shard % 2 + 1) * (D // 2))
            for row, pair in ((10, time[4:6]), (11, space[3:5])):
                values = pair[shard // 2 : shard // 2 + 1, half].astype(bf16)
                store(shard, slice(at + row, at + row + 1), slice(0, D // 2), values)
            values = mlp[4 + shard : 5 + shard, :].astype(bf16)
            store(shard, slice(at + 12, at + 13), slice(0, D), values)


def last_kernel(scalars, e1, r0, r1, r2, r3, out):
    total = e1[...]
    for source, ref in enumerate((r0, r1, r2, r3)):
        total = total + nn(recv_to_frame(scalars[0], source), ref[...])
    out[...] = total


def shape(rows, columns, kind):
    return jax.ShapeDtypeStruct((rows, columns), kind)


VMEM = pl.BlockSpec(memory_space=pltpu.MemorySpace.VMEM)
SMEM = pl.BlockSpec(memory_space=pltpu.MemorySpace.SMEM)
ANY = pl.BlockSpec(memory_space=pltpu.MemorySpace.HBM)


def call(kernel, name, outs, specs, scratch, operands, microseconds):
    return pl.pallas_call(
        kernel,
        name=name,
        out_shape=outs,
        in_specs=specs,
        out_specs=[VMEM] * len(outs),
        scratch_shapes=scratch,
        compiler_params=pltpu.CompilerParams(vmem_limit_bytes=LIMITS.get(name, 5) << 20),
        cost_estimate=pl.CostEstimate(
            flops=int(microseconds * 1.1e9), transcendentals=0, bytes_accessed=1 << 20
        ),
    )(*operands)


def dma_sems(parts):
    return pltpu.SemaphoreType.DMA((1 + 3 * len(parts),))


def vmem(rows, columns, kind=bf16):
    return pltpu.VMEM((rows, columns), kind)


def place_forward(scalars, tokens, vec, owns, pieces):
    outs = [shape(ROWS, D, bf16), shape(ROWS, 3 * D, bf16), shape(ROWS, D, bf16)]
    outs += [shape(ROWS, D, bf16)] + [shape(CHUNK, D, bf16)] * 4
    return call(
        place_forward_kernel, "place_forward", outs, [SMEM, VMEM, VMEM] + [ANY] * 7,
        [vmem(D, 3 * D), vmem(D, D), dma_sems(TIME_QKV_PARTS), dma_sems(TIME_PROJ_PARTS)],
        (scalars, tokens, vec, *owns, *pieces), 11,
    )


def frame_forward(scalars, tokens, vec, received, owns, pieces):
    outs = [shape(ROWS, D, f32), shape(ROWS, D, bf16), shape(ROWS, 3 * D, bf16)]
    outs += [shape(ROWS, D, bf16), shape(ROWS, D, f32), shape(ROWS, D, bf16)]
    return call(
        frame_forward_kernel, "frame_forward", outs, [SMEM] + [VMEM] * 6 + [ANY] * 8,
        [
            vmem(D, D), vmem(D, 3 * D), vmem(D, D),
            dma_sems(TIME_FC_PARTS), dma_sems(SPACE_QKV_PARTS), dma_sems(SPACE_PROJ_PARTS),
        ],
        (scalars, tokens, vec, *received, *owns, *pieces), 13,
    )


def mlp_both(scalars, live, vec, x2, h3, out_grad, owns, in_pieces, out_pieces):
    outs = [
        shape(ROWS, D, bf16), shape(ROWS, FF, bf16), shape(ROWS, FF, bf16),
        shape(ROWS, D, bf16), shape(ROWS, D, f32), shape(8, D, f32),
    ]
    return call(
        mlp_kernel, "mlp_both", outs, [SMEM, SMEM] + [VMEM] * 4 + [ANY] * 11,
        [vmem(D, FF), vmem(FF, D), dma_sems(MLP_IN_PARTS), dma_sems(MLP_OUT_PARTS)],
        (scalars, live, vec, x2, h3, out_grad, *owns, *in_pieces, *out_pieces[1:]), 18,
    )


def space_back(scalars, vec, e2, x1, qkv, owns, pieces):
    outs = [shape(ROWS, 3 * D, bf16), shape(ROWS, D, f32), shape(ROWS, D, bf16)]
    outs += [shape(8, D, f32)] + [shape(CHUNK, D, bf16)] * 4
    return call(
        space_back_kernel, "space_back", outs, [SMEM] + [VMEM] * 4 + [ANY] * 7,
        [
            vmem(D, 3 * D), vmem(D, D), vmem(ROWS, D),
            dma_sems(SPACE_PROJ_PARTS), dma_sems(SPACE_QKV_PARTS),
        ],
        (scalars, vec, e2, x1, qkv, *owns, *pieces), 20,
    )


def time_projections(scalars, received, owns, fc_pieces, pieces):
    outs = [shape(ROWS, D, bf16)] * 3 + [shape(8, D, f32)]
    return call(
        time_projections_kernel, "time_projections", outs, [SMEM] + [VMEM] * 4 + [ANY] * 11,
        [vmem(D, D), vmem(D, D), dma_sems(TIME_FC_PARTS), dma_sems(TIME_PROJ_PARTS)],
        (scalars, *received, *owns, *fc_pieces, *pieces[1:]), 4,
    )


def time_back(scalars, vec, tokens, qkv, da1, early_sums, own, pieces):
    outs = [shape(ROWS, 3 * D, bf16), shape(8, D, f32)] + [shape(CHUNK, D, bf16)] * 4
    return call(
        time_back_kernel, "time_back", outs, [SMEM] + [VMEM] * 5 + [ANY] * 6,
        [vmem(D, 3 * D), dma_sems(TIME_QKV_PARTS)],
        (scalars, vec, tokens, qkv, da1, early_sums, own, *pieces), 16,
    )


def weight_grads(name, scalars, groups, tables=()):
    rows = sum(g[0].shape[1] // 4 * (g[1].shape[1] // D) for g in groups)
    flat = [array for group in groups for array in group] + list(tables)
    rows += EXTRA if tables else 0
    kernel = functools.partial(weight_grad_kernel, count=len(groups), tables=len(tables))
    return call(
        kernel, name, [jax.ShapeDtypeStruct((2, rows, D), bf16)] * 2, [SMEM] + [VMEM] * len(flat),
        [vmem(D, ROWS)] * 2, (scalars, *flat), rows / 150,
    )


def copy_all(copies):
    for copy in copies:
        copy.start()
    for copy in copies:
        copy.wait()


def columns_of(ref, at):
    return ref.at[:, pl.ds(pl.multiple_of(at * D, D), D)]


def pack_time_kernel(scalars, time_qkv, time_proj, vectors, out, sems):
    first, second = out.at[pl.ds(0, BLOCK), :], out.at[pl.ds(BLOCK, BLOCK), :]
    tail = pltpu.make_async_copy(vectors, out.at[pl.ds(2 * BLOCK, 8), :], sems.at[2])
    tail.start()

    @pl.when(scalars[1] == 0)
    def _():
        pltpu.make_async_copy(columns_of(time_qkv, 0), first, sems.at[0]).start()
        pltpu.make_async_copy(columns_of(time_qkv, 1), second, sems.at[1]).start()

    @pl.when(scalars[1] != 0)
    def _():
        pltpu.make_async_copy(columns_of(time_qkv, 2), first, sems.at[0]).start()
        pltpu.make_async_copy(time_proj, second, sems.at[1]).start()

    pltpu.make_async_copy(time_proj, first, sems.at[0]).wait()
    pltpu.make_async_copy(time_proj, second, sems.at[1]).wait()
    tail.wait()


def pack_rest_kernel(
    scalars, time_qkv, time_proj, time_fc, space_qkv, space_proj, mlp_in, mlp_out, vectors,
    packed, space_half, in_half, out_half, sems,
):
    half = scalars[1]
    copies = []

    def add(source, target, row, rows):
        target = target.at[pl.ds(row, rows), :]
        copies.append(pltpu.make_async_copy(source, target, sems.at[len(copies)]))

    halves = pl.ds(pl.multiple_of(half * 2 * BLOCK, 2 * BLOCK), 2 * BLOCK)
    add(columns_of(mlp_in, 2 * half), in_half, 0, BLOCK)
    add(columns_of(mlp_in, 2 * half + 1), in_half, BLOCK, BLOCK)
    add(mlp_out.at[halves, :], out_half, 0, 2 * BLOCK)
    blocks = [columns_of(time_qkv, at) for at in range(3)] + [time_proj]
    blocks += [columns_of(space_qkv, 0), columns_of(space_qkv, 1), time_fc]
    blocks += [columns_of(space_qkv, 2), space_proj]
    blocks += [columns_of(mlp_in, at) for at in range(4)]
    for at, source in enumerate(blocks):
        add(source, packed, at * BLOCK, BLOCK)
    add(mlp_out, packed, 13 * BLOCK, 4 * BLOCK)
    add(vectors, packed, VECTOR_AT, 8)
    at = len(copies)
    middle = BLOCK // 2

    def space(source, row, rows, sem):
        return pltpu.make_async_copy(source, space_half.at[pl.ds(row, rows), :], sems.at[sem])

    @pl.when(half == 0)
    def _():
        space(columns_of(space_qkv, 0), 0, BLOCK, at).start()
        space(columns_of(space_qkv, 1), BLOCK, BLOCK, at + 1).start()
        space(time_fc.at[pl.ds(0, middle), :], 2 * BLOCK, middle, at + 2).start()

    @pl.when(half != 0)
    def _():
        space(time_fc.at[pl.ds(middle, middle), :], 0, middle, at + 2).start()
        space(columns_of(space_qkv, 2), middle, BLOCK, at).start()
        space(space_proj, BLOCK + middle, BLOCK, at + 1).start()

    copy_all(copies)
    space(space_proj, 0, BLOCK, at).wait()
    space(space_proj, BLOCK, BLOCK, at + 1).wait()
    space(time_fc.at[pl.ds(0, middle), :], 2 * BLOCK, middle, at + 2).wait()


def pack_time(*operands):
    return pl.pallas_call(
        pack_time_kernel, name="pack_time",
        compiler_params=pltpu.CompilerParams(vmem_limit_bytes=LIMITS.get("pack_time", 5) << 20), out_shape=shape(392, D, bf16),
        in_specs=[SMEM, ANY, ANY, ANY], out_specs=VMEM,
        scratch_shapes=[pltpu.SemaphoreType.DMA((3,))],
        cost_estimate=pl.CostEstimate(flops=10**9, transcendentals=0, bytes_accessed=1 << 20),
    )(*operands)


def pack_rest(*operands):
    return pl.pallas_call(
        pack_rest_kernel, name="pack_rest",
        compiler_params=pltpu.CompilerParams(vmem_limit_bytes=LIMITS.get("pack_rest", 5) << 20),
        out_shape=[
            shape(VECTOR_AT + 8, D, bf16), shape(480, D, bf16), shape(384, D, bf16),
            shape(384, D, bf16),
        ],
        in_specs=[SMEM] + [ANY] * 8, out_specs=[VMEM] * 4,
        scratch_shapes=[pltpu.SemaphoreType.DMA((21,))],
        cost_estimate=pl.CostEstimate(flops=3 * 10**9, transcendentals=0, bytes_accessed=1 << 20),
    )(*operands)


def unpack_kernel(scalars, mine, other, *outs, bit, parts):
    own_first = (scalars[2] // bit) % 2 == 0
    for half, row, rows, index, out_row, column in parts:
        rows = pl.ds(row, rows)
        near, far = mine[rows, :], other[rows, :]
        pair = (near, far) if half == 0 else (far, near)
        outs[index][out_row : out_row + rows.size, column * D : (column + 1) * D] = jnp.where(
            own_first, *pair
        ).astype(f32)


def unpack(scalars, mine, other, bit, parts, outs):
    kernel = functools.partial(unpack_kernel, bit=bit, parts=parts)
    return call(
        kernel, "unpack", [shape(*out, f32) for out in outs], [SMEM, VMEM, VMEM], [],
        (scalars, mine, other), 2,
    )


OUT_PARTS = ((0, 0, 384, 0, 0, 0), (1, 0, 384, 0, 384, 0))
IN_PARTS = (
    (0, 0, 192, 0, 0, 0), (0, 192, 192, 0, 0, 1), (1, 0, 192, 0, 0, 2), (1, 192, 192, 0, 0, 3),
)
SPACE_PARTS = (
    (0, 0, 192, 0, 0, 0), (0, 192, 192, 0, 0, 1), (1, 0, 192, 0, 0, 2), (1, 192, 192, 1, 0, 0),
)
SMALL_PARTS = ((0, 0, 192, 0, 0, 0), (1, 0, 192, 1, 0, 0))
TIME_PARTS = (
    (0, 0, 192, 0, 0, 0), (0, 192, 128, 0, 0, 1), (1, 0, 64, 0, 128, 1), (1, 64, 192, 0, 0, 2),
    (1, 256, 16, 1, 0, 0),
)


def last_sum(scalars, e1, received):
    return call(
        last_kernel, "last_sum", [shape(ROWS, D, f32)], [SMEM] + [VMEM] * 5, [],
        (scalars, e1, *received), 2,
    )[0]


def flip(array, axis, bit, size):
    return lax.ppermute(array, axis, [(at, at ^ bit) for at in range(size)])


def pick(array, at):
    return lax.dynamic_index_in_dim(array, at, 0, keepdims=False)


def add_rounded(left, right):
    return (left.astype(f32) + right.astype(f32)).astype(bf16)


def after(value, *others):
    return lax.optimization_barrier((value,) + others)[0]


def halves_of(own, half_at):
    return lax.dynamic_slice_in_dim(own, half_at * (own.shape[0] // 2), own.shape[0] // 2, 0)


def step_rows(rows):
    return next(step for step in (96, 80, 48, 16) if rows % step == 0)


def sum_split_kernel(scalars, kept, got, keep, send, *, bit):
    rows = keep.shape[-2]
    step = step_rows(rows)
    if bit == 0:
        mine = scalars[0] // 2
    else:
        mine = (scalars[2] // bit) % 2
    for target, at in ((keep, mine), (send, 1 - mine)):

        def body(index, carry, target=target, at=at):
            row = pl.multiple_of(index * step, 16)
            if bit == 0:
                total = kept[at, pl.ds(row, step), :].astype(f32)
                total = total + got[at, pl.ds(row, step), :].astype(f32)
                target[pl.ds(row, step), :] = total.astype(bf16)
            else:
                source = pl.ds(pl.multiple_of(at * rows + row, 16), step)
                for chip in range(2) if len(keep.shape) == 3 else [None]:
                    here = (source, slice(None)) if chip is None else (chip, source, slice(None))
                    there = (pl.ds(row, step), slice(None))
                    there = there if chip is None else (chip,) + there
                    total = kept[here].astype(f32) + got[here].astype(f32)
                    target[there] = total.astype(bf16)
            return carry

        lax.fori_loop(0, rows // step, body, 0)


def sum_split(scalars, kept, got, bit):
    dims = kept.shape
    out = dims[1:] if bit == 0 else dims[:-2] + (dims[-2] // 2, D)
    kernel = functools.partial(sum_split_kernel, bit=bit)
    outs = [jax.ShapeDtypeStruct(out, bf16)] * 2
    return call(kernel, "sum_split", outs, [SMEM, VMEM, VMEM], [], (scalars, kept, got), 1.5)


def join_kernel(scalars, mine, other, out, *, bit):
    rows = mine.shape[0]
    at = (scalars[2] // bit) % 2
    out[pl.ds(pl.multiple_of(at * rows, 16), rows), :] = mine[...]
    out[pl.ds(pl.multiple_of((1 - at) * rows, 16), rows), :] = other[...]


def join(scalars, mine, other, bit):
    kernel = functools.partial(join_kernel, bit=bit)
    outs = [shape(2 * mine.shape[0], D, bf16)]
    return call(kernel, "join", outs, [SMEM, VMEM, VMEM], [], (scalars, mine, other), 1)[0]


class Reduce:
    def __init__(self, parts, order, scalars, replica_at, ring_size):
        self.kept, sent = parts
        self.scalars, self.replica_at, self.ring_size = scalars, replica_at, ring_size
        self.steps = [("sum", bit) for bit in order]
        self.steps += [("gather", bit) for bit in reversed(order) if bit]
        self.flying = flip(sent, "group", 1, 4)
        self.halve = lambda array: array

    def split(self, bit):
        if bit == 0:
            chip = self.scalars[0] // 2
            return (lambda a: pick(a, chip)), (lambda a: pick(a, 1 - chip))
        mine = (self.replica_at // bit) % 2

        def half(at):
            def take(array):
                rows = array.shape[-2] // 2
                return lax.dynamic_slice_in_dim(array, at * rows, rows, array.ndim - 2)

            return take

        return half(mine), half(1 - mine)

    def flip(self, array, bit):
        axis = ("group", 2, 4) if bit == 0 else ("replica", bit, self.ring_size)
        return flip(array, *axis)

    def advance(self, *others):
        got = after(self.flying, *others) if others else self.flying
        if self.kept is not None:
            if self.steps[0][0] == "sum":
                bit = self.steps.pop(0)[1]
                if self.kept.shape[-2] % 32 == 0:
                    self.kept, sent = sum_split(self.scalars, self.kept, got, bit)
                else:
                    keep, send = self.split(bit)
                    sent = add_rounded(send(self.kept), send(got))
                    self.kept = add_rounded(keep(self.kept), keep(got))
            else:
                sent = self.current = add_rounded(self.kept, got)
                self.kept = None
                bit = self.steps[0][1]
        else:
            bit = self.steps.pop(0)[1]
            mine = (self.replica_at // bit) % 2
            if not self.steps:
                self.got, self.bit = got, bit
                return got
            if got.shape[0] % 16 == 0:
                self.current = join(self.scalars, self.current, got, bit)
            else:
                self.current = jnp.where(
                    mine == 0,
                    jnp.concatenate([self.current, got], 0),
                    jnp.concatenate([got, self.current], 0),
                )
            sent = self.current
            bit = self.steps[0][1]
        self.flying = self.flip(sent, bit)
        return sent

    def unpacked(self, parts, outs):
        return unpack(self.scalars, self.current, self.got, self.bit, parts, outs)


def block(array, at):
    return array[:, at * D : (at + 1) * D]


def unpack_grad(summed, blocks):
    return summed.reshape(blocks, BLOCK, D).transpose(1, 0, 2).reshape(BLOCK, blocks * D).astype(f32)


def exchange(chunks):
    return [chunks[0]] + [flip(chunks[d], "group", d, 4) for d in range(1, 4)]


def build(mesh):
    ring_size = mesh.shape["replica"]

    def on_device(tokens, out_grad, slot_mask, *shards):
        (
            time_norm_gain, time_norm_shift, time_qkv, time_qv_bias, time_proj, time_proj_bias,
            time_fc, time_fc_bias, space_norm_gain, space_norm_shift, space_qkv, space_qv_bias,
            space_proj, space_proj_bias, mlp_norm_gain, mlp_norm_shift, mlp_in, mlp_in_bias,
            mlp_out, mlp_out_bias,
        ) = shards
        group_at = lax.axis_index("group")
        replica_at = lax.axis_index("replica")
        half_at = replica_at % 2
        scalars = jnp.stack([group_at, half_at, replica_at]).astype(jnp.int32)
        live = slot_mask.astype(f32).reshape(1, 1)
        vectors = [
            time_norm_gain, time_norm_shift, time_proj_bias, time_fc_bias, space_norm_gain,
            space_norm_shift, space_proj_bias, mlp_norm_gain, mlp_norm_shift, mlp_out_bias,
            time_qv_bias, space_qv_bias, mlp_in_bias,
        ]
        cross = functools.partial(flip, axis="group", bit=2, size=4)
        near = functools.partial(flip, axis="group", bit=1, size=4)
        relay = functools.partial(flip, axis="replica", bit=1, size=ring_size)
        ends = [sum(v.shape[0] for v in vectors[: at + 1]) for at in range(len(vectors))]
        flat = sum(jnp.pad(v, (at - v.shape[0], 8 * D - at)) for v, at in zip(vectors, ends))
        flat = flat.reshape(8, D)
        time_half = pack_time(scalars, time_qkv, time_proj, flat)
        time_direct = cross(time_half)
        token_pieces = after(tokens[0], time_half).transpose(1, 0, 2).reshape(4, 49, 2, D)
        got = exchange([pick(token_pieces, group_at ^ d) for d in range(4)])
        place_tokens = jnp.pad(jnp.concatenate(got, axis=1), ((0, 3), (0, 0), (0, 0)))
        place_tokens = place_tokens.reshape(ROWS, D)

        packed, space_half, in_half, out_half = pack_rest(
            scalars, time_qkv, time_proj, time_fc, space_qkv, space_proj, mlp_in, mlp_out,
            after(flat, got[1]),
        )
        partner = near(packed)
        time_direct, space_half = lax.optimization_barrier((time_direct, space_half))
        time_across = near(time_direct)
        time_relayed = relay(time_direct)
        time_pieces = (partner, time_direct, time_relayed, time_across, near(time_relayed))
        space_direct = cross(after(space_half, got[2], got[3]))
        in_direct = cross(after(in_half, space_direct))
        out_direct = cross(after(out_half, space_direct))

        held = [flat, partner[VECTOR_AT:], time_direct[384:], time_across[384:]]
        held = jnp.stack(held).reshape(4, 8 * D)[:, : VECTOR_ROWS * BLOCK]
        tables = jnp.stack([pick(held, group_at ^ shard) for shard in range(4)]).astype(f32)
        tables = tables.reshape(4, VECTOR_ROWS, BLOCK)
        vec = jnp.concatenate(
            [
                tables[:, :10].transpose(1, 0, 2).reshape(10, D),
                tables[:, 10:12].reshape(2, D),
                tables[:, 12:14].reshape(2, D),
                tables[:, 14:18].reshape(4, D),
                jnp.zeros((6, D), f32),
            ]
        )
        pads = ((0, 0), (0, HALF - PLACES), (0, 0))
        frame_tokens = jnp.pad(tokens[0], pads).reshape(ROWS, D)
        frame_grad = jnp.pad(out_grad[0], pads).reshape(ROWS, D)

        h1, qkv1, a1, o1, *sends = place_forward(
            scalars, after(place_tokens, space_direct), vec, (time_qkv, time_proj), time_pieces
        )
        received = exchange(sends)
        space_relayed = relay(space_direct)
        space_pieces = (
            partner, space_direct, space_relayed, near(space_direct),
            near(after(space_relayed, o1)),
        )
        x1, h2, qkv2, a2, x2, h3 = frame_forward(
            scalars, after(frame_tokens, in_direct, out_direct), vec, received,
            (time_fc, space_qkv, space_proj), space_pieces,
        )
        in_relayed = relay(in_direct)
        in_pieces = (
            partner, in_direct, in_relayed, near(after(in_direct, x2)), near(after(in_relayed, x2)),
        )
        out_relayed = relay(out_direct)
        out_pieces = (
            partner, out_direct, out_relayed, near(after(out_direct, x2)),
            near(after(out_relayed, x2)),
        )
        layer_out, act, du, dm, e2, sums3 = mlp_both(
            scalars, live, vec, x2, h3, frame_grad, (mlp_in, mlp_out), in_pieces, out_pieces
        )
        layer_out = layer_out.reshape(2, HALF, D)[None, :, :PLACES]

        chunk = functools.partial(
            Reduce, scalars=scalars, replica_at=replica_at, ring_size=ring_size
        )
        bits = [1 << at for at in range(ring_size.bit_length() - 1)]
        along = [0] + bits
        names = {"x": 0, "y": bits[0], "u": bits[1], "w": bits[2]}

        def way(parts, order):
            return chunk(parts, [names[name] for name in order] + bits[3:])

        ways = {}
        last = ()

        def advance(steps):
            nonlocal last
            for name in steps:
                if ways[name].steps:
                    last = (ways[name].advance(*last),)

        ways["o"] = way(weight_grads("mlp_out_grad", scalars, [(act, dm)]), ORDERS["o"])
        ways["i"] = way(
            weight_grads("mlp_in_grad", scalars, [(h3, after(du, ways["o"].kept))]), ORDERS["i"]
        )
        last = (ways["i"].kept,)
        advance(SCHEDULE[0])
        dqkv2, e1, dt2, sums2, *sends = space_back(
            scalars, vec, after(e2, *last), x1, qkv2, (space_proj, space_qkv), space_pieces
        )
        received = exchange(sends)
        last = (e1,)
        advance(SCHEDULE[1])
        ways["s"] = way(
            weight_grads("space_grad", scalars, [(h2, after(dqkv2, *last)), (a2, dt2)]),
            ORDERS["s"],
        )
        last = (ways["s"].kept,)
        advance(SCHEDULE[2])
        dt1, do1, da1, early = time_projections(
            scalars, [after(received[0], *last)] + received[1:], (time_fc, time_proj),
            space_pieces, time_pieces,
        )
        ways["p"] = way(
            weight_grads("time_small_grad", scalars, [(a1, do1), (o1, dt1)]), ORDERS["p"]
        )
        last = (ways["p"].kept,)
        advance(SCHEDULE[3])
        dqkv1, sums1, *sends = time_back(
            scalars, vec, place_tokens, qkv1, after(da1, *last), early, time_qkv, time_pieces
        )
        received = exchange(sends)
        last = (dqkv1,)
        advance(SCHEDULE[4])
        ways["t"] = way(
            weight_grads(
                "time_grad", scalars, [(h1, after(dqkv1, *last))], (sums1, sums2, sums3)
            ),
            ORDERS["t"],
        )
        last = (ways["t"].kept,)
        advance(SCHEDULE[5])
        tokens_grad = last_sum(scalars, after(e1, *last), received)
        last = (tokens_grad,)
        tokens_grad = tokens_grad.reshape(2, HALF, D)[None, :, :PLACES]
        advance(SCHEDULE[6])
        while any(each.steps for each in ways.values()):
            advance([name for name in ways])
        way_out, way_in, way_space, way_small, way_time = (ways[name] for name in "oispt")
        (d_out,) = way_out.unpacked(OUT_PARTS, [(D, D)])
        (d_in,) = way_in.unpacked(IN_PARTS, [(BLOCK, FF)])
        d_space_qkv, d_space_proj = way_space.unpacked(SPACE_PARTS, [(BLOCK, 3 * D), (BLOCK, D)])
        d_proj, d_fc = way_small.unpacked(SMALL_PARTS, [(BLOCK, D), (BLOCK, D)])
        d_time_qkv, vectors = way_time.unpacked(TIME_PARTS, [(BLOCK, 3 * D), (16, D)])
        ones = vectors[:10, :BLOCK]
        return (
            layer_out, tokens_grad, ones[0], ones[1], d_time_qkv, vectors[10, : D // 2],
            d_proj, ones[2], d_fc, ones[3], ones[4], ones[5], d_space_qkv,
            vectors[11, : D // 2], d_space_proj, ones[6], ones[7], ones[8], d_in, vectors[12],
            d_out, ones[9],
        )

    return on_device


def solution(mesh):
    rows = P("group", None)
    vector = P("group")
    batch = P("replica", "group", None, None)
    params = (
        vector, vector, rows, vector, rows, vector, rows, vector, vector, vector, rows, vector,
        rows, vector, vector, vector, rows, vector, rows, vector,
    )
    return jax.shard_map(
        build(mesh),
        mesh=mesh,
        in_specs=(batch, batch, P("replica")) + params,
        out_specs=(batch, batch) + params,
        check_vma=False,
    )
```

```python
import functools

import jax
import jax.numpy as jnp
from jax import lax
from jax.experimental import pallas as pl
from jax.experimental.pallas import tpu as pltpu
from jax.sharding import PartitionSpec as P

D = 768
FF = 3072
HEADS = 12
HEAD_DIM = 64
PLACES = 196
BLOCK = 192
CHUNK = 104
HALF = 208
ROWS = 416
epsilon = 1e-06
bf16 = jnp.bfloat16
f32 = jnp.float32

TIME_GAIN, TIME_SHIFT, TIME_PROJ_B, TIME_FC_B, SPACE_GAIN, SPACE_SHIFT, SPACE_PROJ_B = range(7)
MLP_GAIN, MLP_SHIFT, MLP_OUT_B = 7, 8, 9
TIME_QV, SPACE_QV, MLP_IN_B = 10, 12, 14
VECTOR_ROWS = 18
EXTRA = 64
LIMITS = {
    "place_forward": 10, "frame_forward": 14, "mlp_both": 28, "space_back": 19, "time_back": 13,
    "mlp_out_grad": 8, "mlp_in_grad": 8, "space_grad": 7, "pack_rest": 8, "time_projections": 6,
}
ORDERS = {"o": "uyxw", "i": "yuxw", "s": "xyuw", "p": "uyxw", "t": "xyuw"}
SCHEDULE = ("", "", "io", "", "s", "", "i", "opisotiospispotipsitptsipotpsatapoatasot")

TIME_QKV_PARTS = ((0, 0, 192, 0, 0), (0, 192, 192, 0, 1), (1, 0, 192, 0, 2))
TIME_PROJ_PARTS = ((1, 192, 192, 0, 0),)
SPACE_QKV_PARTS = ((0, 0, 192, 0, 0), (0, 192, 192, 0, 1), (1, 96, 192, 0, 2))
SPACE_PROJ_PARTS = ((1, 288, 192, 0, 0),)
TIME_FC_PARTS = ((0, 384, 96, 0, 0), (1, 0, 96, 96, 0))
MLP_IN_PARTS = ((0, 0, 192, 0, 0), (0, 192, 192, 0, 1), (1, 0, 192, 0, 2), (1, 192, 192, 0, 3))
MLP_OUT_PARTS = ((0, 0, 384, 0, 0), (1, 0, 384, 384, 0))
TIME_CHUNK, SPACE_CHUNK, IN_CHUNK, OUT_CHUNK = (0, 768), (768, 960), (1728, 768), (2496, 768)
VECTOR_AT = 3264
VECTOR_PAD = 24


def nn(left, right):
    return lax.dot_general(left, right, (((1,), (0,)), ((), ())), preferred_element_type=f32)


def nt(left, right):
    return lax.dot_general(left, right, (((1,), (1,)), ((), ())), preferred_element_type=f32)


def tn(left, right):
    return lax.dot_general(left, right, (((0,), (0,)), ((), ())), preferred_element_type=f32)


def norm_parts(values):
    centred = values - jnp.mean(values, axis=-1, keepdims=True)
    inverse = lax.rsqrt(jnp.mean(centred * centred, axis=-1, keepdims=True) + epsilon)
    return centred * inverse, inverse


class Weights:
    def __init__(self, scalars, own, pieces, parts, chunk, target, sems):
        self.scalars, self.own, self.pieces, self.parts = scalars, own, pieces, parts
        self.chunk, self.target, self.sems = chunk, target, sems
        self.shard_rows = own.shape[0]

    def base(self, flipped):
        at = (self.scalars[0] ^ flipped) * self.shard_rows
        return pl.multiple_of(at, self.shard_rows)

    def copy(self, source, part, flipped, at):
        half, row, rows, block_row, column = part
        return pltpu.make_async_copy(
            source.at[pl.ds(row, rows), :],
            self.target.at[pl.ds(self.base(flipped) + block_row, rows), pl.ds(column * D, D)],
            self.sems.at[at],
        )

    def own_copy(self):
        target = self.target.at[pl.ds(self.base(0), self.shard_rows), :]
        return pltpu.make_async_copy(self.own, target, self.sems.at[0])

    def start(self):
        packed, direct, relayed, across, across_relayed = self.pieces
        self.own_copy().start()
        y = self.scalars[1]
        first, chunk_rows = self.chunk
        at = 1
        for part in self.parts:
            half, row, rows, block_row, column = part
            whole = (half, first + row + half * (chunk_rows // 2), rows, block_row, column)
            self.copy(packed, whole, 1, at).start()

            @pl.when(y == half)
            def _():
                self.copy(direct, part, 2, at + 1).start()
                self.copy(across, part, 3, at + 2).start()

            @pl.when(y != half)
            def _():
                self.copy(relayed, part, 2, at + 1).start()
                self.copy(across_relayed, part, 3, at + 2).start()

            at += 3

    def wait(self):
        direct, across = self.pieces[1], self.pieces[3]
        self.own_copy().wait()
        at = 1
        for part in self.parts:
            self.copy(direct, part, 1, at).wait()
            self.copy(direct, part, 2, at + 1).wait()
            self.copy(across, part, 3, at + 2).wait()
            at += 3


def lane_half(second):
    lane = lax.broadcasted_iota(jnp.int32, (HALF, 128), 1)
    return (lane >= 64) if second else (lane < 64)


def masked(values, second):
    return jnp.where(lane_half(second), values, jnp.zeros_like(values))


def key_mask(same_place):
    key = lax.broadcasted_iota(jnp.int32, (HALF, HALF), 0)
    query = lax.broadcasted_iota(jnp.int32, (HALF, HALF), 1)
    allowed = (key // 8 == query // 8) if same_place else (key < PLACES)
    return jnp.where(allowed, 0.0, -1e30).astype(f32)


def both_heads(pair):
    return jnp.concatenate([masked(pair, False), masked(pair, True)], axis=0)


def probs_of(keys, query_pair, mask):
    scores = nt(keys, query_pair).reshape(2, HALF, HALF) + mask[None]
    weights = jnp.exp(scores - jnp.max(scores, axis=1, keepdims=True))
    return weights * (1.0 / jnp.sum(weights, axis=1, keepdims=True))


def flat_heads(values):
    return values.astype(bf16).reshape(2 * HALF, HALF)


def attend(qkv_ref, mask, out_ref):
    def pair_step(pair, carry):
        column = pl.multiple_of(pair * 128, 128)
        for part in range(2):
            rows = pl.ds(part * HALF, HALF)
            query = qkv_ref[rows, pl.ds(column, 128)] * bf16(HEAD_DIM**-0.5)
            key_part = qkv_ref[rows, pl.ds(D + column, 128)]
            value_part = qkv_ref[rows, pl.ds(2 * D + column, 128)]
            mixed = []
            for second in (False, True):
                scores = nt(masked(key_part, second), query) + mask
                weights = jnp.exp(scores - jnp.max(scores, axis=0, keepdims=True))
                probs = weights * (1.0 / jnp.sum(weights, axis=0, keepdims=True))
                mixed.append(tn(value_part, probs.astype(bf16)))
            mixed = jnp.concatenate([mixed[0][:64], mixed[1][64:]], axis=0)
            out_ref[rows, pl.ds(column, 128)] = mixed.T.astype(bf16)
        return carry

    lax.fori_loop(0, HEADS // 2, pair_step, 0)


def attend_back(qkv_ref, mask, grad_ref, out_ref):
    first = lane_half(False)

    def pair_step(pair, carry):
        column = pl.multiple_of(pair * 128, 128)
        for part in range(2):
            rows = pl.ds(part * HALF, HALF)
            query = qkv_ref[rows, pl.ds(column, 128)] * bf16(HEAD_DIM**-0.5)
            keys = both_heads(qkv_ref[rows, pl.ds(D + column, 128)])
            values = both_heads(qkv_ref[rows, pl.ds(2 * D + column, 128)])
            grad = grad_ref[rows, pl.ds(column, 128)]
            probs = probs_of(keys, query, mask)
            grad_probs = nt(values, grad).reshape(2, HALF, HALF)
            centre = jnp.sum(grad_probs * probs, axis=1, keepdims=True)
            grad_scores = flat_heads(probs * (grad_probs - centre))
            grad_query = tn(keys, grad_scores).T * HEAD_DIM**-0.5
            out_ref[rows, pl.ds(column, 128)] = grad_query.astype(bf16)
            grad_key = nn(grad_scores, query)
            grad_key = jnp.where(first, grad_key[:HALF], grad_key[HALF:])
            out_ref[rows, pl.ds(D + column, 128)] = grad_key.astype(bf16)
            grad_value = nn(flat_heads(probs), grad)
            grad_value = jnp.where(first, grad_value[:HALF], grad_value[HALF:])
            out_ref[rows, pl.ds(2 * D + column, 128)] = grad_value.astype(bf16)
        return carry

    lax.fori_loop(0, HEADS // 2, pair_step, 0)


def project_qkv(normed, weight, vec, qv_row, out_ref):
    for member in range(3):
        packed = nn(normed, weight[:, member * D : (member + 1) * D])
        if member != 1:
            row = qv_row + member // 2
            packed = packed + vec[row : row + 1, :]
        out_ref[:, member * D : (member + 1) * D] = packed.astype(bf16)


def place_to_send(dest):
    local = lax.broadcasted_iota(jnp.int32, (CHUNK, ROWS), 0)
    col = lax.broadcasted_iota(jnp.int32, (CHUNK, ROWS), 1)
    source = (local // 2) * 8 + dest * 2 + local % 2
    return ((col == source) & (local < 98)).astype(bf16)


def recv_to_frame(group_at, source):
    row = lax.broadcasted_iota(jnp.int32, (ROWS, CHUNK), 0)
    col = lax.broadcasted_iota(jnp.int32, (ROWS, CHUNK), 1)
    second = (row >= HALF).astype(jnp.int32)
    spot = row - second * HALF
    local = (spot - (group_at ^ source) * 49) * 2 + second
    inside = (spot >= (group_at ^ source) * 49) & (spot < ((group_at ^ source) + 1) * 49)
    return ((col == local) & inside).astype(bf16)


def place_forward_kernel(
    scalars, tokens, vec, *refs
):
    own_qkv, own_proj, *pieces = refs[:7]
    h1, qkv, mixed, o1, *rest = refs[7:]
    sends, (w_qkv, w_proj, sem_a, sem_b) = rest[:4], rest[4:]
    qkv_copy = Weights(scalars, own_qkv, pieces, TIME_QKV_PARTS, TIME_CHUNK, w_qkv, sem_a)
    proj_copy = Weights(scalars, own_proj, pieces, TIME_PROJ_PARTS, TIME_CHUNK, w_proj, sem_b)
    qkv_copy.start()
    proj_copy.start()
    normal, unused = norm_parts(tokens[...].astype(f32))
    normed = (normal * vec[TIME_GAIN : TIME_GAIN + 1, :] + vec[TIME_SHIFT : TIME_SHIFT + 1, :])
    normed = normed.astype(bf16)
    h1[...] = normed
    qkv_copy.wait()
    project_qkv(normed, w_qkv, vec, TIME_QV, qkv)
    attend(qkv, key_mask(True), mixed)
    proj_copy.wait()
    out = (nn(mixed[...], w_proj[...]) + vec[TIME_PROJ_B : TIME_PROJ_B + 1, :]).astype(bf16)
    o1[...] = out
    for dest in range(4):
        sends[dest][...] = nn(place_to_send(dest), out).astype(bf16)


def frame_forward_kernel(scalars, tokens, vec, r0, r1, r2, r3, *refs):
    own_fc, own_qkv, own_proj, *pieces = refs[:8]
    x1, h2, qkv, mixed, x2, h3 = refs[8:14]
    w_fc, w_qkv, w_proj, sem_a, sem_b, sem_c = refs[14:]
    fc_copy = Weights(scalars, own_fc, pieces, TIME_FC_PARTS, SPACE_CHUNK, w_fc, sem_a)
    qkv_copy = Weights(scalars, own_qkv, pieces, SPACE_QKV_PARTS, SPACE_CHUNK, w_qkv, sem_b)
    proj_copy = Weights(scalars, own_proj, pieces, SPACE_PROJ_PARTS, SPACE_CHUNK, w_proj, sem_c)
    fc_copy.start()
    qkv_copy.start()
    proj_copy.start()
    group_at = scalars[0]
    received = sum(
        nn(recv_to_frame(group_at, source), ref[...]) for source, ref in enumerate((r0, r1, r2, r3))
    ).astype(bf16)
    fc_copy.wait()
    branch = nn(received, w_fc[...]) + vec[TIME_FC_B : TIME_FC_B + 1, :]
    after = tokens[...].astype(f32) + branch
    x1[...] = after
    normal, unused = norm_parts(after)
    normed = normal * vec[SPACE_GAIN : SPACE_GAIN + 1, :] + vec[SPACE_SHIFT : SPACE_SHIFT + 1, :]
    normed = normed.astype(bf16)
    h2[...] = normed
    qkv_copy.wait()
    project_qkv(normed, w_qkv, vec, SPACE_QV, qkv)
    attend(qkv, key_mask(False), mixed)
    proj_copy.wait()
    after = x1[...] + (nn(mixed[...], w_proj[...]) + vec[SPACE_PROJ_B : SPACE_PROJ_B + 1, :])
    x2[...] = after
    normal, unused = norm_parts(after)
    normed = normal * vec[MLP_GAIN : MLP_GAIN + 1, :] + vec[MLP_SHIFT : MLP_SHIFT + 1, :]
    h3[...] = normed.astype(bf16)


def norm_back(values, gain, grad_normed):
    normal, inverse = norm_parts(values)
    scaled = grad_normed * gain
    mean = jnp.mean(scaled, axis=-1, keepdims=True)
    along = jnp.mean(scaled * normal, axis=-1, keepdims=True)
    grad = inverse * (scaled - mean - normal * along)
    return (
        grad,
        jnp.sum(grad_normed * normal, axis=0, keepdims=True),
        jnp.sum(grad_normed, axis=0, keepdims=True),
    )


def column_sum(values):
    return jnp.sum(values.astype(f32), axis=0, keepdims=True)


def mlp_kernel(scalars, live, vec, x2, h3, out_grad, *refs):
    own_in, own_out, *pieces = refs[:11]
    in_pieces, out_pieces = [pieces[0]] + pieces[1:5], [pieces[0]] + pieces[5:9]
    layer_out, acts, du, dm, e2, sums, w_in, w_out, sem_a, sem_b = refs[11:]
    in_copy = Weights(scalars, own_in, in_pieces, MLP_IN_PARTS, IN_CHUNK, w_in, sem_a)
    out_copy = Weights(scalars, own_out, out_pieces, MLP_OUT_PARTS, OUT_CHUNK, w_out, sem_b)
    in_copy.start()
    out_copy.start()
    e3 = live[0, 0] * out_grad[...].astype(f32)
    grad_branch = e3.astype(bf16)
    dm[...] = grad_branch
    sums[3:4, :] = column_sum(grad_branch)
    sums[4:8, :] = jnp.zeros((4, D), f32)
    normed = h3[...]
    in_copy.wait()
    out_copy.wait()
    x3 = x2[...] + vec[MLP_OUT_B : MLP_OUT_B + 1, :]
    e2[...] = x3
    back = None
    for part in range(4):
        columns = slice(part * D, (part + 1) * D)
        pre = nn(normed, w_in[:, columns]) + vec[MLP_IN_B + part : MLP_IN_B + part + 1, :]
        cdf = 0.5 * (1.0 + lax.erf(pre * (0.5**0.5)))
        act = (pre * cdf).astype(bf16)
        slope = cdf + pre * jnp.exp(-0.5 * pre * pre) * 0.3989422804014327
        acts[:, columns] = act
        grad = (slope * nt(grad_branch, w_out[columns, :])).astype(bf16)
        du[:, columns] = grad
        sums[4 + part : 5 + part, :] = column_sum(grad)
        e2[...] += nn(act, w_out[columns, :])
        piece = nt(grad, w_in[:, columns])
        back = piece if back is None else back + piece
    layer_out[...] = (live[0, 0] * e2[...]).astype(bf16)
    grad, gain_grad, shift_grad = norm_back(x2[...], vec[MLP_GAIN : MLP_GAIN + 1, :], back)
    sums[0:1, :] = gain_grad
    sums[1:2, :] = shift_grad
    sums[2:3, :] = jnp.zeros((1, D), f32)
    e2[...] = e3 + grad


def space_back_kernel(scalars, vec, e2, x1, qkv, *refs):
    own_proj, own_qkv, *pieces = refs[:7]
    dqkv, e1, dt2, sums, s0, s1, s2, s3, w_qkv, w_proj, da, sem_a, sem_b = refs[7:]
    proj_copy = Weights(scalars, own_proj, pieces, SPACE_PROJ_PARTS, SPACE_CHUNK, w_proj, sem_a)
    qkv_copy = Weights(scalars, own_qkv, pieces, SPACE_QKV_PARTS, SPACE_CHUNK, w_qkv, sem_b)
    proj_copy.start()
    qkv_copy.start()
    branch = e2[...].astype(bf16)
    dt2[...] = branch
    proj_copy.wait()
    da[...] = nt(branch, w_proj[...]).astype(bf16)
    attend_back(qkv, key_mask(False), da, dqkv)
    qkv_copy.wait()
    back = nt(dqkv[...], w_qkv[...])
    grad, gain_grad, shift_grad = norm_back(x1[...], vec[SPACE_GAIN : SPACE_GAIN + 1, :], back)
    total = e2[...] + grad
    e1[...] = total
    rounded = total.astype(bf16)
    for source, ref in enumerate((s0, s1, s2, s3)):
        ref[...] = tn(recv_to_frame(scalars[0], source), rounded).astype(bf16)
    sums[0:1, :] = gain_grad
    sums[1:2, :] = shift_grad
    sums[2:3, :] = column_sum(branch)
    sums[3:4, :] = column_sum(dqkv[:, :D])
    sums[4:5, :] = column_sum(dqkv[:, 2 * D :])
    sums[5:8, :] = jnp.zeros((3, D), f32)


def time_projections_kernel(scalars, r0, r1, r2, r3, *refs):
    own_fc, own_proj, packed, *pieces = refs[:11]
    dt1, do1, da1, sums, w_fc, w_proj, sem_a, sem_b = refs[11:]
    fc_pieces, pieces = [packed] + pieces[:4], [packed] + pieces[4:]
    fc_copy = Weights(scalars, own_fc, fc_pieces, TIME_FC_PARTS, SPACE_CHUNK, w_fc, sem_a)
    proj_copy = Weights(scalars, own_proj, pieces, TIME_PROJ_PARTS, TIME_CHUNK, w_proj, sem_b)
    fc_copy.start()
    proj_copy.start()
    branch = sum(
        tn(place_to_send(source), ref[...]) for source, ref in enumerate((r0, r1, r2, r3))
    ).astype(bf16)
    dt1[...] = branch
    fc_copy.wait()
    projected = nt(branch, w_fc[...]).astype(bf16)
    do1[...] = projected
    proj_copy.wait()
    da1[...] = nt(projected, w_proj[...]).astype(bf16)
    sums[0:1, :] = column_sum(projected)
    sums[1:2, :] = column_sum(branch)
    sums[2:8, :] = jnp.zeros((6, D), f32)


def time_back_kernel(scalars, vec, tokens, qkv, da1, early_sums, own_qkv, *refs):
    pieces, (dqkv, sums, s0, s1, s2, s3, w_qkv, sem) = refs[:5], refs[5:]
    qkv_copy = Weights(scalars, own_qkv, pieces, TIME_QKV_PARTS, TIME_CHUNK, w_qkv, sem)
    qkv_copy.start()
    attend_back(qkv, key_mask(True), da1, dqkv)
    qkv_copy.wait()
    back = nt(dqkv[...], w_qkv[...])
    grad, gain_grad, shift_grad = norm_back(
        tokens[...].astype(f32), vec[TIME_GAIN : TIME_GAIN + 1, :], back
    )
    rounded = grad.astype(bf16)
    for dest, ref in enumerate((s0, s1, s2, s3)):
        ref[...] = nn(place_to_send(dest), rounded).astype(bf16)
    sums[0:1, :] = gain_grad
    sums[1:2, :] = shift_grad
    sums[2:4, :] = early_sums[0:2, :]
    sums[4:5, :] = column_sum(dqkv[:, :D])
    sums[5:6, :] = column_sum(dqkv[:, 2 * D :])
    sums[6:8, :] = jnp.zeros((2, D), f32)


def weight_grad_kernel(scalars, *refs, count, tables):
    inputs, (kept, sent, turned, ordered) = refs[:-4], refs[-4:]
    core = scalars[0] % 2

    def store(shard, rows, columns, values):
        @pl.when(core == shard % 2)
        def _():
            kept[shard // 2, rows, columns] = values

        @pl.when(core != shard % 2)
        def _():
            sent[shard // 2, rows, columns] = values

    at = 0
    for index in range(count):
        left, right = inputs[2 * index : 2 * index + 2]
        width = left.shape[1]
        shard_rows = width // 4
        if shard_rows % 128 == 0:
            for spot in range(4):
                shard = 2 * (spot % 2) + (core if spot < 2 else 1 - core)
                source = pl.ds(pl.multiple_of(shard * shard_rows, shard_rows), shard_rows)
                target = kept if spot < 2 else sent
                for block in range(right.shape[1] // D):
                    total = tn(left[:, source], right[:, block * D : (block + 1) * D])
                    rows = slice(at + block * shard_rows, at + (block + 1) * shard_rows)
                    target[spot % 2, rows, :] = total.astype(bf16)
            at += shard_rows * (right.shape[1] // D)
            continue
        turned[0:width, :] = left[...].T
        for spot in range(4):
            shard = 2 * (spot % 2) + (core if spot < 2 else 1 - core)
            source = pl.ds(pl.multiple_of(shard * shard_rows, shard_rows), shard_rows)
            ordered[spot * shard_rows : (spot + 1) * shard_rows, :] = turned[source, :]
        for block in range(right.shape[1] // D):
            columns = slice(block * D, (block + 1) * D)
            total = nn(ordered[...], right[:, columns]).astype(bf16)
            for spot in range(4):
                target = kept if spot < 2 else sent
                target[spot % 2, at : at + shard_rows, :] = total[
                    spot * shard_rows : (spot + 1) * shard_rows, :
                ]
            at += shard_rows
    if tables:
        time, space, mlp = (ref[...] for ref in inputs[2 * count :])
        singles = jnp.concatenate([time[0:4], space[0:3], mlp[0:2], mlp[3:4]], axis=0)
        for ref in (kept, sent):
            for chip in range(2):
                ref[chip, at : at + EXTRA, :] = jnp.zeros((EXTRA, D), bf16)
        for shard in range(4):
            lanes = slice(shard * BLOCK, (shard + 1) * BLOCK)
            store(shard, slice(at, at + 10), slice(0, BLOCK), singles[:, lanes].astype(bf16))
            half = slice((shard % 2) * (D // 2), (shard % 2 + 1) * (D // 2))
            for row, pair in ((10, time[4:6]), (11, space[3:5])):
                values = pair[shard // 2 : shard // 2 + 1, half].astype(bf16)
                store(shard, slice(at + row, at + row + 1), slice(0, D // 2), values)
            values = mlp[4 + shard : 5 + shard, :].astype(bf16)
            store(shard, slice(at + 12, at + 13), slice(0, D), values)


def last_kernel(scalars, e1, r0, r1, r2, r3, out):
    total = e1[...]
    for source, ref in enumerate((r0, r1, r2, r3)):
        total = total + nn(recv_to_frame(scalars[0], source), ref[...])
    out[...] = total


def shape(rows, columns, kind):
    return jax.ShapeDtypeStruct((rows, columns), kind)


VMEM = pl.BlockSpec(memory_space=pltpu.MemorySpace.VMEM)
SMEM = pl.BlockSpec(memory_space=pltpu.MemorySpace.SMEM)
ANY = pl.BlockSpec(memory_space=pltpu.MemorySpace.HBM)


def in_hbm(array):
    return pltpu.with_memory_space_constraint(array, pltpu.MemorySpace.HBM)


def call(kernel, name, outs, specs, scratch, operands, microseconds):
    return pl.pallas_call(
        kernel,
        name=name,
        out_shape=outs,
        in_specs=specs,
        out_specs=[VMEM] * len(outs),
        scratch_shapes=scratch,
        compiler_params=pltpu.CompilerParams(vmem_limit_bytes=LIMITS.get(name, 5) << 20),
        cost_estimate=pl.CostEstimate(
            flops=int((microseconds + 10) * 1.1e9), transcendentals=0,
            bytes_accessed=1024,
        ),
    )(*operands)


def dma_sems(parts):
    return pltpu.SemaphoreType.DMA((1 + 3 * len(parts),))


def vmem(rows, columns, kind=bf16):
    return pltpu.VMEM((rows, columns), kind)


def place_forward(scalars, tokens, vec, owns, pieces):
    outs = [shape(ROWS, D, bf16), shape(ROWS, 3 * D, bf16), shape(ROWS, D, bf16)]
    outs += [shape(ROWS, D, bf16)] + [shape(CHUNK, D, bf16)] * 4
    return call(
        place_forward_kernel, "place_forward", outs, [SMEM, VMEM, VMEM] + [ANY] * 7,
        [vmem(D, 3 * D), vmem(D, D), dma_sems(TIME_QKV_PARTS), dma_sems(TIME_PROJ_PARTS)],
        (scalars, tokens, vec, *owns, *pieces), 11,
    )


def frame_forward(scalars, tokens, vec, received, owns, pieces):
    outs = [shape(ROWS, D, f32), shape(ROWS, D, bf16), shape(ROWS, 3 * D, bf16)]
    outs += [shape(ROWS, D, bf16), shape(ROWS, D, f32), shape(ROWS, D, bf16)]
    return call(
        frame_forward_kernel, "frame_forward", outs, [SMEM] + [VMEM] * 6 + [ANY] * 8,
        [
            vmem(D, D), vmem(D, 3 * D), vmem(D, D),
            dma_sems(TIME_FC_PARTS), dma_sems(SPACE_QKV_PARTS), dma_sems(SPACE_PROJ_PARTS),
        ],
        (scalars, tokens, vec, *received, *owns, *pieces), 13,
    )


def mlp_both(scalars, live, vec, x2, h3, out_grad, owns, in_pieces, out_pieces):
    outs = [
        shape(ROWS, D, bf16), shape(ROWS, FF, bf16), shape(ROWS, FF, bf16),
        shape(ROWS, D, bf16), shape(ROWS, D, f32), shape(8, D, f32),
    ]
    return call(
        mlp_kernel, "mlp_both", outs, [SMEM, SMEM] + [VMEM] * 4 + [ANY] * 11,
        [vmem(D, FF), vmem(FF, D), dma_sems(MLP_IN_PARTS), dma_sems(MLP_OUT_PARTS)],
        (scalars, live, vec, x2, h3, out_grad, *owns, *in_pieces, *out_pieces[1:]), 18,
    )


def space_back(scalars, vec, e2, x1, qkv, owns, pieces):
    outs = [shape(ROWS, 3 * D, bf16), shape(ROWS, D, f32), shape(ROWS, D, bf16)]
    outs += [shape(8, D, f32)] + [shape(CHUNK, D, bf16)] * 4
    return call(
        space_back_kernel, "space_back", outs, [SMEM] + [VMEM] * 4 + [ANY] * 7,
        [
            vmem(D, 3 * D), vmem(D, D), vmem(ROWS, D),
            dma_sems(SPACE_PROJ_PARTS), dma_sems(SPACE_QKV_PARTS),
        ],
        (scalars, vec, e2, x1, qkv, *owns, *pieces), 20,
    )


def time_projections(scalars, received, owns, fc_pieces, pieces):
    outs = [shape(ROWS, D, bf16)] * 3 + [shape(8, D, f32)]
    return call(
        time_projections_kernel, "time_projections", outs, [SMEM] + [VMEM] * 4 + [ANY] * 11,
        [vmem(D, D), vmem(D, D), dma_sems(TIME_FC_PARTS), dma_sems(TIME_PROJ_PARTS)],
        (scalars, *received, *owns, *fc_pieces, *pieces[1:]), 4,
    )


def time_back(scalars, vec, tokens, qkv, da1, early_sums, own, pieces):
    outs = [shape(ROWS, 3 * D, bf16), shape(8, D, f32)] + [shape(CHUNK, D, bf16)] * 4
    return call(
        time_back_kernel, "time_back", outs, [SMEM] + [VMEM] * 5 + [ANY] * 6,
        [vmem(D, 3 * D), dma_sems(TIME_QKV_PARTS)],
        (scalars, vec, tokens, qkv, da1, early_sums, own, *pieces), 16,
    )


def weight_grads(name, scalars, groups, tables=()):
    rows = sum(g[0].shape[1] // 4 * (g[1].shape[1] // D) for g in groups)
    flat = [array for group in groups for array in group] + list(tables)
    rows += EXTRA if tables else 0
    kernel = functools.partial(weight_grad_kernel, count=len(groups), tables=len(tables))
    return call(
        kernel, name, [jax.ShapeDtypeStruct((2, rows, D), bf16)] * 2, [SMEM] + [VMEM] * len(flat),
        [vmem(D, ROWS)] * 2, (scalars, *flat), rows / 150,
    )


def copy_all(copies):
    for copy in copies:
        copy.start()
    for copy in copies:
        copy.wait()


def columns_of(ref, at):
    return ref.at[:, pl.ds(pl.multiple_of(at * D, D), D)]


def pack_time_kernel(scalars, time_qkv, time_proj, vectors, out, sems):
    first, second = out.at[pl.ds(0, BLOCK), :], out.at[pl.ds(BLOCK, BLOCK), :]
    tail = pltpu.make_async_copy(vectors, out.at[pl.ds(2 * BLOCK, VECTOR_PAD), :], sems.at[2])
    tail.start()

    @pl.when(scalars[1] == 0)
    def _():
        pltpu.make_async_copy(columns_of(time_qkv, 0), first, sems.at[0]).start()
        pltpu.make_async_copy(columns_of(time_qkv, 1), second, sems.at[1]).start()

    @pl.when(scalars[1] != 0)
    def _():
        pltpu.make_async_copy(columns_of(time_qkv, 2), first, sems.at[0]).start()
        pltpu.make_async_copy(time_proj, second, sems.at[1]).start()

    pltpu.make_async_copy(time_proj, first, sems.at[0]).wait()
    pltpu.make_async_copy(time_proj, second, sems.at[1]).wait()
    tail.wait()


def pack_rest_kernel(
    scalars, time_qkv, time_proj, time_fc, space_qkv, space_proj, mlp_in, mlp_out, vectors,
    packed, space_half, in_half, out_half, sems,
):
    half = scalars[1]
    copies = []

    def add(source, target, row, rows):
        target = target.at[pl.ds(row, rows), :]
        copies.append(pltpu.make_async_copy(source, target, sems.at[len(copies)]))

    halves = pl.ds(pl.multiple_of(half * 2 * BLOCK, 2 * BLOCK), 2 * BLOCK)
    add(columns_of(mlp_in, 2 * half), in_half, 0, BLOCK)
    add(columns_of(mlp_in, 2 * half + 1), in_half, BLOCK, BLOCK)
    add(mlp_out.at[halves, :], out_half, 0, 2 * BLOCK)
    blocks = [columns_of(time_qkv, at) for at in range(3)] + [time_proj]
    blocks += [columns_of(space_qkv, 0), columns_of(space_qkv, 1), time_fc]
    blocks += [columns_of(space_qkv, 2), space_proj]
    blocks += [columns_of(mlp_in, at) for at in range(4)]
    for at, source in enumerate(blocks):
        add(source, packed, at * BLOCK, BLOCK)
    add(mlp_out, packed, 13 * BLOCK, 4 * BLOCK)
    add(vectors, packed, VECTOR_AT, VECTOR_PAD)
    at = len(copies)
    middle = BLOCK // 2

    def space(source, row, rows, sem):
        return pltpu.make_async_copy(source, space_half.at[pl.ds(row, rows), :], sems.at[sem])

    @pl.when(half == 0)
    def _():
        space(columns_of(space_qkv, 0), 0, BLOCK, at).start()
        space(columns_of(space_qkv, 1), BLOCK, BLOCK, at + 1).start()
        space(time_fc.at[pl.ds(0, middle), :], 2 * BLOCK, middle, at + 2).start()

    @pl.when(half != 0)
    def _():
        space(time_fc.at[pl.ds(middle, middle), :], 0, middle, at + 2).start()
        space(columns_of(space_qkv, 2), middle, BLOCK, at).start()
        space(space_proj, BLOCK + middle, BLOCK, at + 1).start()

    copy_all(copies)
    space(space_proj, 0, BLOCK, at).wait()
    space(space_proj, BLOCK, BLOCK, at + 1).wait()
    space(time_fc.at[pl.ds(0, middle), :], 2 * BLOCK, middle, at + 2).wait()


def pack_time(*operands):
    operands = [operands[0], *map(in_hbm, operands[1:])]
    return pl.pallas_call(
        pack_time_kernel, name="pack_time",
        compiler_params=pltpu.CompilerParams(vmem_limit_bytes=LIMITS.get("pack_time", 5) << 20), out_shape=shape(2 * BLOCK + VECTOR_PAD, D, bf16),
        in_specs=[SMEM, ANY, ANY, ANY], out_specs=VMEM,
        scratch_shapes=[pltpu.SemaphoreType.DMA((3,))],
        cost_estimate=pl.CostEstimate(flops=11 * 10**9, transcendentals=0, bytes_accessed=1024),
    )(*operands)


def pack_rest(*operands):
    operands = [operands[0], *map(in_hbm, operands[1:])]
    return pl.pallas_call(
        pack_rest_kernel, name="pack_rest",
        compiler_params=pltpu.CompilerParams(vmem_limit_bytes=LIMITS.get("pack_rest", 5) << 20),
        out_shape=[
            shape(VECTOR_AT + VECTOR_PAD, D, bf16), shape(480, D, bf16), shape(384, D, bf16),
            shape(384, D, bf16),
        ],
        in_specs=[SMEM] + [ANY] * 8, out_specs=[VMEM] * 4,
        scratch_shapes=[pltpu.SemaphoreType.DMA((21,))],
        cost_estimate=pl.CostEstimate(flops=11 * 10**9, transcendentals=0, bytes_accessed=1024),
    )(*operands)


def table_kernel(scalars, own, packed, direct, across, out, pieces, sems):
    copies = [
        pltpu.make_async_copy(source.at[pl.ds(row, VECTOR_PAD), :], pieces.at[at], sems.at[at])
        for at, (source, row) in enumerate(
            ((own, 0), (packed, VECTOR_AT), (direct, 2 * BLOCK), (across, 2 * BLOCK))
        )
    ]
    copy_all(copies)
    group_at = scalars[0]
    out[...] = jnp.zeros((VECTOR_PAD, D), f32)
    for shard in range(4):
        rows = pieces[group_at ^ shard].astype(f32)[:, :BLOCK]
        lanes = slice(shard * BLOCK, (shard + 1) * BLOCK)
        out[0:10, lanes] = rows[0:10]
        for row in range(2):
            lanes = slice((shard % 2) * 384 + row * BLOCK, (shard % 2) * 384 + (row + 1) * BLOCK)
            for first in (TIME_QV, SPACE_QV):
                source = rows[first + row : first + row + 1]
                out[first + shard // 2 : first + shard // 2 + 1, lanes] = source
        for row in range(4):
            lanes = slice(row * BLOCK, (row + 1) * BLOCK)
            source = rows[MLP_IN_B + row : MLP_IN_B + row + 1]
            out[MLP_IN_B + shard : MLP_IN_B + shard + 1, lanes] = source


def vector_table(*operands):
    return call(
        table_kernel, "table", [shape(VECTOR_PAD, D, f32)], [SMEM] + [ANY] * 4,
        [pltpu.VMEM((4, VECTOR_PAD, D), bf16), pltpu.SemaphoreType.DMA((4,))], operands, 1,
    )[0]


def unpack_kernel(scalars, mine, other, *outs, bit, parts):
    own_first = (scalars[2] // bit) % 2 == 0
    for half, row, rows, index, out_row, column in parts:
        rows = pl.ds(row, rows)
        near, far = mine[rows, :], other[rows, :]
        pair = (near, far) if half == 0 else (far, near)
        outs[index][out_row : out_row + rows.size, column * D : (column + 1) * D] = jnp.where(
            own_first, *pair
        ).astype(f32)


def unpack(scalars, mine, other, bit, parts, outs):
    kernel = functools.partial(unpack_kernel, bit=bit, parts=parts)
    return call(
        kernel, "unpack", [shape(*out, f32) for out in outs], [SMEM, VMEM, VMEM], [],
        (scalars, mine, other), 2,
    )


OUT_PARTS = ((0, 0, 384, 0, 0, 0), (1, 0, 384, 0, 384, 0))
IN_PARTS = (
    (0, 0, 192, 0, 0, 0), (0, 192, 192, 0, 0, 1), (1, 0, 192, 0, 0, 2), (1, 192, 192, 0, 0, 3),
)
SPACE_PARTS = (
    (0, 0, 192, 0, 0, 0), (0, 192, 192, 0, 0, 1), (1, 0, 192, 0, 0, 2), (1, 192, 192, 1, 0, 0),
)
SMALL_PARTS = ((0, 0, 192, 0, 0, 0), (1, 0, 192, 1, 0, 0))
TIME_PARTS = (
    (0, 0, 192, 0, 0, 0), (0, 192, 128, 0, 0, 1), (1, 0, 64, 0, 128, 1), (1, 64, 192, 0, 0, 2),
    (1, 256, 16, 1, 0, 0),
)


def last_sum(scalars, e1, received):
    return call(
        last_kernel, "last_sum", [shape(ROWS, D, f32)], [SMEM] + [VMEM] * 5, [],
        (scalars, e1, *received), 2,
    )[0]


def flip(array, axis, bit, size):
    return lax.ppermute(array, axis, [(at, at ^ bit) for at in range(size)])


def pick(array, at):
    return lax.dynamic_index_in_dim(array, at, 0, keepdims=False)


def add_rounded(left, right):
    return (left.astype(f32) + right.astype(f32)).astype(bf16)


def after(value, *others):
    return lax.optimization_barrier((value,) + others)[0]


def halves_of(own, half_at):
    return lax.dynamic_slice_in_dim(own, half_at * (own.shape[0] // 2), own.shape[0] // 2, 0)


def step_rows(rows):
    return next(step for step in (96, 80, 48, 16) if rows % step == 0)


def sum_split_kernel(scalars, kept, got, keep, send, *, bit):
    rows = keep.shape[-2]
    step = step_rows(rows)
    if bit == 0:
        mine = scalars[0] // 2
    else:
        mine = (scalars[2] // bit) % 2
    for target, at in ((keep, mine), (send, 1 - mine)):

        def body(index, carry, target=target, at=at):
            row = pl.multiple_of(index * step, 16)
            if bit == 0:
                total = kept[at, pl.ds(row, step), :].astype(f32)
                total = total + got[at, pl.ds(row, step), :].astype(f32)
                target[pl.ds(row, step), :] = total.astype(bf16)
            else:
                source = pl.ds(pl.multiple_of(at * rows + row, 16), step)
                for chip in range(2) if len(keep.shape) == 3 else [None]:
                    here = (source, slice(None)) if chip is None else (chip, source, slice(None))
                    there = (pl.ds(row, step), slice(None))
                    there = there if chip is None else (chip,) + there
                    total = kept[here].astype(f32) + got[here].astype(f32)
                    target[there] = total.astype(bf16)
            return carry

        lax.fori_loop(0, rows // step, body, 0)


def sum_split(scalars, kept, got, bit):
    dims = kept.shape
    out = dims[1:] if bit == 0 else dims[:-2] + (dims[-2] // 2, D)
    kernel = functools.partial(sum_split_kernel, bit=bit)
    outs = [jax.ShapeDtypeStruct(out, bf16)] * 2
    return call(kernel, "sum_split", outs, [SMEM, VMEM, VMEM], [], (scalars, kept, got), 0)


def join_kernel(scalars, mine, other, out, *, bit):
    rows = mine.shape[0]
    at = (scalars[2] // bit) % 2
    out[pl.ds(pl.multiple_of(at * rows, 16), rows), :] = mine[...]
    out[pl.ds(pl.multiple_of((1 - at) * rows, 16), rows), :] = other[...]


def join(scalars, mine, other, bit):
    kernel = functools.partial(join_kernel, bit=bit)
    outs = [shape(2 * mine.shape[0], D, bf16)]
    return call(kernel, "join", outs, [SMEM, VMEM, VMEM], [], (scalars, mine, other), 0)[0]


class Reduce:
    def __init__(self, parts, order, scalars, replica_at, ring_size):
        self.kept, sent = parts
        self.scalars, self.replica_at, self.ring_size = scalars, replica_at, ring_size
        self.steps = [("sum", bit) for bit in order]
        self.steps += [("gather", bit) for bit in reversed(order) if bit]
        self.flying = flip(sent, "group", 1, 4)
        self.halve = lambda array: array

    def split(self, bit):
        if bit == 0:
            chip = self.scalars[0] // 2
            return (lambda a: pick(a, chip)), (lambda a: pick(a, 1 - chip))
        mine = (self.replica_at // bit) % 2

        def half(at):
            def take(array):
                rows = array.shape[-2] // 2
                return lax.dynamic_slice_in_dim(array, at * rows, rows, array.ndim - 2)

            return take

        return half(mine), half(1 - mine)

    def flip(self, array, bit):
        axis = ("group", 2, 4) if bit == 0 else ("replica", bit, self.ring_size)
        return flip(array, *axis)

    def advance(self, *others):
        got = after(self.flying, *others) if others else self.flying
        if self.kept is not None:
            if self.steps[0][0] == "sum":
                bit = self.steps.pop(0)[1]
                if self.kept.shape[-2] % 32 == 0:
                    self.kept, sent = sum_split(self.scalars, self.kept, got, bit)
                else:
                    keep, send = self.split(bit)
                    sent = add_rounded(send(self.kept), send(got))
                    self.kept = add_rounded(keep(self.kept), keep(got))
            else:
                sent = self.current = add_rounded(self.kept, got)
                self.kept = None
                bit = self.steps[0][1]
        else:
            bit = self.steps.pop(0)[1]
            mine = (self.replica_at // bit) % 2
            if not self.steps:
                self.got, self.bit = got, bit
                return got
            if got.shape[0] % 16 == 0:
                self.current = join(self.scalars, self.current, got, bit)
            else:
                self.current = jnp.where(
                    mine == 0,
                    jnp.concatenate([self.current, got], 0),
                    jnp.concatenate([got, self.current], 0),
                )
            sent = self.current
            bit = self.steps[0][1]
        self.flying = self.flip(sent, bit)
        return sent

    def unpacked(self, parts, outs):
        return unpack(self.scalars, self.current, self.got, self.bit, parts, outs)


def block(array, at):
    return array[:, at * D : (at + 1) * D]


def unpack_grad(summed, blocks):
    return summed.reshape(blocks, BLOCK, D).transpose(1, 0, 2).reshape(BLOCK, blocks * D).astype(f32)


def exchange(chunks):
    return [chunks[0]] + [flip(chunks[d], "group", d, 4) for d in range(1, 4)]


def build(mesh):
    ring_size = mesh.shape["replica"]

    def on_device(tokens, out_grad, slot_mask, *shards):
        (
            time_norm_gain, time_norm_shift, time_qkv, time_qv_bias, time_proj, time_proj_bias,
            time_fc, time_fc_bias, space_norm_gain, space_norm_shift, space_qkv, space_qv_bias,
            space_proj, space_proj_bias, mlp_norm_gain, mlp_norm_shift, mlp_in, mlp_in_bias,
            mlp_out, mlp_out_bias,
        ) = shards
        group_at = lax.axis_index("group")
        replica_at = lax.axis_index("replica")
        half_at = replica_at % 2
        scalars = jnp.stack([group_at, half_at, replica_at]).astype(jnp.int32)
        live = slot_mask.astype(f32).reshape(1, 1)
        vectors = [
            time_norm_gain, time_norm_shift, time_proj_bias, time_fc_bias, space_norm_gain,
            space_norm_shift, space_proj_bias, mlp_norm_gain, mlp_norm_shift, mlp_out_bias,
            time_qv_bias, space_qv_bias, mlp_in_bias,
        ]
        cross = functools.partial(flip, axis="group", bit=2, size=4)
        near = functools.partial(flip, axis="group", bit=1, size=4)
        relay = functools.partial(flip, axis="replica", bit=1, size=ring_size)
        ends = [sum(v.shape[0] for v in vectors[: at + 1]) for at in range(len(vectors))]
        room = VECTOR_PAD * BLOCK
        flat = sum(jnp.pad(v, (at - v.shape[0], room - at)) for v, at in zip(vectors, ends))
        flat = jnp.pad(flat.reshape(VECTOR_PAD, BLOCK), ((0, 0), (0, D - BLOCK)))
        token_pieces = tokens[0].transpose(1, 0, 2).reshape(4, 49, 2, D)
        token_pieces = [pick(token_pieces, group_at ^ d) for d in range(4)]
        got = exchange(token_pieces)
        time_half = pack_time(scalars, time_qkv, time_proj, after(flat, *token_pieces))
        time_direct = cross(after(time_half, *got[1:]))
        place_tokens = jnp.pad(jnp.concatenate(got, axis=1), ((0, 3), (0, 0), (0, 0)))
        place_tokens = place_tokens.reshape(ROWS, D)

        packed, space_half, in_half, out_half = pack_rest(
            scalars, time_qkv, time_proj, time_fc, space_qkv, space_proj, mlp_in, mlp_out,
            after(flat, *got[1:]),
        )
        partner = near(packed)
        time_across = near(time_direct)
        time_relayed = relay(time_direct)
        space_direct = cross(after(space_half, time_direct))
        in_direct = cross(after(in_half, space_direct))
        out_direct = cross(after(out_half, space_direct))

        vec = vector_table(scalars, flat, partner, time_direct, time_across)
        time_pieces = (
            partner, time_direct, time_relayed, time_across, near(after(time_relayed, vec)),
        )
        pads = ((0, 0), (0, HALF - PLACES), (0, 0))
        frame_tokens = jnp.pad(tokens[0], pads).reshape(ROWS, D)
        frame_grad = jnp.pad(out_grad[0], pads).reshape(ROWS, D)

        space_across = near(space_direct)
        h1, qkv1, a1, o1, *sends = place_forward(
            scalars, after(place_tokens, space_direct), vec, (time_qkv, time_proj), time_pieces
        )
        received = exchange(sends)
        space_relayed = relay(space_direct)
        space_pieces = (
            partner, space_direct, space_relayed, space_across,
            near(after(space_relayed, o1)),
        )
        x1, h2, qkv2, a2, x2, h3 = frame_forward(
            scalars, after(frame_tokens, in_direct, out_direct), vec, received,
            (time_fc, space_qkv, space_proj), space_pieces,
        )
        in_relayed = relay(in_direct)
        in_pieces = (
            partner, in_direct, in_relayed, near(in_direct), near(after(in_relayed, x2)),
        )
        out_relayed = relay(out_direct)
        out_pieces = (
            partner, out_direct, out_relayed, near(after(out_direct, x2)),
            near(after(out_relayed, x2)),
        )
        layer_out, act, du, dm, e2, sums3 = mlp_both(
            scalars, live, vec, x2, h3, frame_grad, (mlp_in, mlp_out), in_pieces, out_pieces
        )
        layer_out = layer_out.reshape(2, HALF, D)[None, :, :PLACES]

        chunk = functools.partial(
            Reduce, scalars=scalars, replica_at=replica_at, ring_size=ring_size
        )
        bits = [1 << at for at in range(ring_size.bit_length() - 1)]
        along = [0] + bits
        names = {"x": 0, "y": bits[0], "u": bits[1], "w": bits[2]}

        def way(parts, order):
            return chunk(parts, [names[name] for name in order] + bits[3:])

        ways = {}
        last = ()

        back = {"sent": None, "got": [], "flying": None, "out": None}

        def move_back():
            nonlocal last
            sends, got = back["sent"], back["got"]
            if back["flying"] is not None:
                got.append(after(back["flying"], *last))
                last = (got[-1],)
            at = len(got) + 1
            if at < 4:
                back["flying"] = flip(after(sends[at], *last), "group", at, 4)
            else:
                back["out"] = last_sum(scalars, e1, [sends[0]] + got)
                back["flying"] = None
                last = (back["out"],)

        def advance(steps):
            nonlocal last
            for name in steps:
                if name == "a":
                    move_back()
                elif ways[name].steps:
                    last = (ways[name].advance(*last),)

        ways["o"] = way(weight_grads("mlp_out_grad", scalars, [(act, dm)]), ORDERS["o"])
        last = (ways["o"].kept,)
        advance(SCHEDULE[0])
        ways["i"] = way(
            weight_grads("mlp_in_grad", scalars, [(h3, after(du, *last))]), ORDERS["i"]
        )
        last = (ways["i"].kept,)
        advance(SCHEDULE[1])
        dqkv2, e1, dt2, sums2, *sends = space_back(
            scalars, vec, after(e2, *last), x1, qkv2, (space_proj, space_qkv), space_pieces
        )
        received = exchange(sends)
        last = (e1,)
        advance(SCHEDULE[2])
        ways["s"] = way(
            weight_grads("space_grad", scalars, [(h2, after(dqkv2, *last)), (a2, dt2)]),
            ORDERS["s"],
        )
        last = (ways["s"].kept,)
        advance(SCHEDULE[3])
        dt1, do1, da1, early = time_projections(
            scalars, [after(received[0], *last)] + received[1:], (time_fc, time_proj),
            space_pieces, time_pieces,
        )
        last = (do1,)
        advance(SCHEDULE[4])
        ways["p"] = way(
            weight_grads("time_small_grad", scalars, [(a1, after(do1, *last)), (o1, dt1)]),
            ORDERS["p"],
        )
        last = (ways["p"].kept,)
        advance(SCHEDULE[5])
        dqkv1, sums1, *sends = time_back(
            scalars, vec, place_tokens, qkv1, after(da1, *last), early, time_qkv, time_pieces
        )
        back["sent"] = sends
        last = (dqkv1,)
        advance(SCHEDULE[6])
        ways["t"] = way(
            weight_grads(
                "time_grad", scalars, [(h1, after(dqkv1, *last))], (sums1, sums2, sums3)
            ),
            ORDERS["t"],
        )
        last = (ways["t"].kept,)
        advance(SCHEDULE[7])
        while back["out"] is None:
            move_back()
        tokens_grad = back["out"].reshape(2, HALF, D)[None, :, :PLACES]
        while any(each.steps for each in ways.values()):
            advance([name for name in ways])
        way_out, way_in, way_space, way_small, way_time = (ways[name] for name in "oispt")
        (d_out,) = way_out.unpacked(OUT_PARTS, [(D, D)])
        (d_in,) = way_in.unpacked(IN_PARTS, [(BLOCK, FF)])
        d_space_qkv, d_space_proj = way_space.unpacked(SPACE_PARTS, [(BLOCK, 3 * D), (BLOCK, D)])
        d_proj, d_fc = way_small.unpacked(SMALL_PARTS, [(BLOCK, D), (BLOCK, D)])
        d_time_qkv, vectors = way_time.unpacked(TIME_PARTS, [(BLOCK, 3 * D), (16, D)])
        ones = vectors[:10, :BLOCK]
        return (
            layer_out, tokens_grad, ones[0], ones[1], d_time_qkv, vectors[10, : D // 2],
            d_proj, ones[2], d_fc, ones[3], ones[4], ones[5], d_space_qkv,
            vectors[11, : D // 2], d_space_proj, ones[6], ones[7], ones[8], d_in, vectors[12],
            d_out, ones[9],
        )

    return on_device


def solution(mesh):
    rows = P("group", None)
    vector = P("group")
    batch = P("replica", "group", None, None)
    params = (
        vector, vector, rows, vector, rows, vector, rows, vector, vector, vector, rows, vector,
        rows, vector, vector, vector, rows, vector, rows, vector,
    )
    return jax.shard_map(
        build(mesh),
        mesh=mesh,
        in_specs=(batch, batch, P("replica")) + params,
        out_specs=(batch, batch) + params,
        check_vma=False,
    )
```

```python
import functools

import jax
import jax.numpy as jnp
from jax import lax
from jax.experimental import pallas as pl
from jax.experimental.pallas import tpu as pltpu
from jax.sharding import PartitionSpec as P

D = 768
FF = 3072
HEADS = 12
HEAD_DIM = 64
PLACES = 196
BLOCK = 192
CHUNK = 104
HALF = 208
ROWS = 416
epsilon = 1e-06
bf16 = jnp.bfloat16
f32 = jnp.float32

TIME_GAIN, TIME_SHIFT, TIME_PROJ_B, TIME_FC_B, SPACE_GAIN, SPACE_SHIFT, SPACE_PROJ_B = range(7)
MLP_GAIN, MLP_SHIFT, MLP_OUT_B = 7, 8, 9
TIME_QV, SPACE_QV, MLP_IN_B = 10, 12, 14
VECTOR_ROWS = 18
EXTRA = 64
LIMITS = {
    "place_forward": 10, "frame_forward": 14, "mlp_both": 28, "space_back": 19, "time_back": 13,
    "mlp_out_grad": 8, "mlp_in_grad": 8, "space_grad": 7, "pack_rest": 8, "time_projections": 6,
}
ORDERS = {"o": "yuxw", "i": "uxyw", "s": "xyuw", "p": "yxuw", "t": "xyuw"}
SCHEDULE = ('', '', '', 'ois', '', '', 'ois', 'potsoisoitpostipotsiptoaspatapitspaitp')

TIME_QKV_PARTS = ((0, 0, 192, 0, 0), (0, 192, 192, 0, 1), (1, 0, 192, 0, 2))
TIME_PROJ_PARTS = ((1, 192, 192, 0, 0),)
SPACE_QKV_PARTS = ((0, 0, 192, 0, 0), (0, 192, 192, 0, 1), (1, 96, 192, 0, 2))
SPACE_PROJ_PARTS = ((1, 288, 192, 0, 0),)
TIME_FC_PARTS = ((0, 384, 96, 0, 0), (1, 0, 96, 96, 0))
MLP_IN_PARTS = ((0, 0, 192, 0, 0), (0, 192, 192, 0, 1), (1, 0, 192, 0, 2), (1, 192, 192, 0, 3))
MLP_OUT_PARTS = ((0, 0, 384, 0, 0), (1, 0, 384, 384, 0))
TIME_CHUNK, SPACE_CHUNK, IN_CHUNK, OUT_CHUNK = (0, 768), (768, 960), (1728, 768), (2496, 768)
VECTOR_AT = 3264
VECTOR_PAD = 24


def nn(left, right):
    return lax.dot_general(left, right, (((1,), (0,)), ((), ())), preferred_element_type=f32)


def nt(left, right):
    return lax.dot_general(left, right, (((1,), (1,)), ((), ())), preferred_element_type=f32)


def tn(left, right):
    return lax.dot_general(left, right, (((0,), (0,)), ((), ())), preferred_element_type=f32)


def norm_parts(values):
    centred = values - jnp.mean(values, axis=-1, keepdims=True)
    inverse = lax.rsqrt(jnp.mean(centred * centred, axis=-1, keepdims=True) + epsilon)
    return centred * inverse, inverse


class Weights:
    def __init__(self, scalars, own, pieces, parts, chunk, target, sems, half_at=1):
        self.half_at = half_at
        self.scalars, self.own, self.pieces, self.parts = scalars, own, pieces, parts
        self.chunk, self.target, self.sems = chunk, target, sems
        self.shard_rows = own.shape[0]

    def base(self, flipped):
        at = (self.scalars[0] ^ flipped) * self.shard_rows
        return pl.multiple_of(at, self.shard_rows)

    def copy(self, source, part, flipped, at):
        half, row, rows, block_row, column = part
        return pltpu.make_async_copy(
            source.at[pl.ds(row, rows), :],
            self.target.at[pl.ds(self.base(flipped) + block_row, rows), pl.ds(column * D, D)],
            self.sems.at[at],
        )

    def own_copy(self):
        target = self.target.at[pl.ds(self.base(0), self.shard_rows), :]
        return pltpu.make_async_copy(self.own, target, self.sems.at[0])

    def start(self):
        packed, direct, relayed, across, across_relayed = self.pieces
        self.own_copy().start()
        y = self.scalars[self.half_at]
        first, chunk_rows = self.chunk
        at = 1
        for part in self.parts:
            half, row, rows, block_row, column = part
            whole = (half, first + row + half * (chunk_rows // 2), rows, block_row, column)
            self.copy(packed, whole, 1, at).start()

            @pl.when(y == half)
            def _():
                self.copy(direct, part, 2, at + 1).start()
                self.copy(across, part, 3, at + 2).start()

            @pl.when(y != half)
            def _():
                self.copy(relayed, part, 2, at + 1).start()
                self.copy(across_relayed, part, 3, at + 2).start()

            at += 3

    def wait(self):
        direct, across = self.pieces[1], self.pieces[3]
        self.own_copy().wait()
        at = 1
        for part in self.parts:
            self.copy(direct, part, 1, at).wait()
            self.copy(direct, part, 2, at + 1).wait()
            self.copy(across, part, 3, at + 2).wait()
            at += 3


def lane_half(second):
    lane = lax.broadcasted_iota(jnp.int32, (HALF, 128), 1)
    return (lane >= 64) if second else (lane < 64)


def masked(values, second):
    return jnp.where(lane_half(second), values, jnp.zeros_like(values))


def key_mask(same_place):
    key = lax.broadcasted_iota(jnp.int32, (HALF, HALF), 0)
    query = lax.broadcasted_iota(jnp.int32, (HALF, HALF), 1)
    allowed = (key // 8 == query // 8) if same_place else (key < PLACES)
    return jnp.where(allowed, 0.0, -1e30).astype(f32)


def both_heads(pair):
    return jnp.concatenate([masked(pair, False), masked(pair, True)], axis=0)


def probs_of(keys, query_pair, mask):
    scores = nt(keys, query_pair).reshape(2, HALF, HALF) + mask[None]
    weights = jnp.exp(scores - jnp.max(scores, axis=1, keepdims=True))
    return weights * (1.0 / jnp.sum(weights, axis=1, keepdims=True))


def flat_heads(values):
    return values.astype(bf16).reshape(2 * HALF, HALF)


def attend(qkv_ref, mask, out_ref):
    def pair_step(pair, carry):
        column = pl.multiple_of(pair * 128, 128)
        for part in range(2):
            rows = pl.ds(part * HALF, HALF)
            query = qkv_ref[rows, pl.ds(column, 128)] * bf16(HEAD_DIM**-0.5)
            key_part = qkv_ref[rows, pl.ds(D + column, 128)]
            value_part = qkv_ref[rows, pl.ds(2 * D + column, 128)]
            mixed = []
            for second in (False, True):
                scores = nt(masked(key_part, second), query) + mask
                weights = jnp.exp(scores - jnp.max(scores, axis=0, keepdims=True))
                probs = weights * (1.0 / jnp.sum(weights, axis=0, keepdims=True))
                mixed.append(tn(value_part, probs.astype(bf16)))
            mixed = jnp.concatenate([mixed[0][:64], mixed[1][64:]], axis=0)
            out_ref[rows, pl.ds(column, 128)] = mixed.T.astype(bf16)
        return carry

    lax.fori_loop(0, HEADS // 2, pair_step, 0)


def attend_back(qkv_ref, mask, grad_ref, out_ref):
    first = lane_half(False)

    def pair_step(pair, carry):
        column = pl.multiple_of(pair * 128, 128)
        for part in range(2):
            rows = pl.ds(part * HALF, HALF)
            query = qkv_ref[rows, pl.ds(column, 128)] * bf16(HEAD_DIM**-0.5)
            keys = both_heads(qkv_ref[rows, pl.ds(D + column, 128)])
            values = both_heads(qkv_ref[rows, pl.ds(2 * D + column, 128)])
            grad = grad_ref[rows, pl.ds(column, 128)]
            probs = probs_of(keys, query, mask)
            grad_probs = nt(values, grad).reshape(2, HALF, HALF)
            centre = jnp.sum(grad_probs * probs, axis=1, keepdims=True)
            grad_scores = flat_heads(probs * (grad_probs - centre))
            grad_query = tn(keys, grad_scores).T * HEAD_DIM**-0.5
            out_ref[rows, pl.ds(column, 128)] = grad_query.astype(bf16)
            grad_key = nn(grad_scores, query)
            grad_key = jnp.where(first, grad_key[:HALF], grad_key[HALF:])
            out_ref[rows, pl.ds(D + column, 128)] = grad_key.astype(bf16)
            grad_value = nn(flat_heads(probs), grad)
            grad_value = jnp.where(first, grad_value[:HALF], grad_value[HALF:])
            out_ref[rows, pl.ds(2 * D + column, 128)] = grad_value.astype(bf16)
        return carry

    lax.fori_loop(0, HEADS // 2, pair_step, 0)


def project_qkv(normed, weight, vec, qv_row, out_ref):
    for member in range(3):
        packed = nn(normed, weight[:, member * D : (member + 1) * D])
        if member != 1:
            row = qv_row + member // 2
            packed = packed + vec[row : row + 1, :]
        out_ref[:, member * D : (member + 1) * D] = packed.astype(bf16)


def place_to_send(dest):
    local = lax.broadcasted_iota(jnp.int32, (CHUNK, ROWS), 0)
    col = lax.broadcasted_iota(jnp.int32, (CHUNK, ROWS), 1)
    source = (local // 2) * 8 + dest * 2 + local % 2
    return ((col == source) & (local < 98)).astype(bf16)


def recv_to_frame(group_at, source):
    row = lax.broadcasted_iota(jnp.int32, (ROWS, CHUNK), 0)
    col = lax.broadcasted_iota(jnp.int32, (ROWS, CHUNK), 1)
    second = (row >= HALF).astype(jnp.int32)
    spot = row - second * HALF
    local = (spot - (group_at ^ source) * 49) * 2 + second
    inside = (spot >= (group_at ^ source) * 49) & (spot < ((group_at ^ source) + 1) * 49)
    return ((col == local) & inside).astype(bf16)


def place_forward_kernel(
    scalars, tokens, vec, *refs
):
    own_qkv, own_proj, *pieces = refs[:7]
    h1, qkv, mixed, o1, *rest = refs[7:]
    sends, (w_qkv, w_proj, sem_a, sem_b) = rest[:4], rest[4:]
    qkv_copy = Weights(scalars, own_qkv, pieces, TIME_QKV_PARTS, TIME_CHUNK, w_qkv, sem_a)
    proj_copy = Weights(scalars, own_proj, pieces, TIME_PROJ_PARTS, TIME_CHUNK, w_proj, sem_b)
    qkv_copy.start()
    proj_copy.start()
    normal, unused = norm_parts(tokens[...].astype(f32))
    normed = (normal * vec[TIME_GAIN : TIME_GAIN + 1, :] + vec[TIME_SHIFT : TIME_SHIFT + 1, :])
    normed = normed.astype(bf16)
    h1[...] = normed
    qkv_copy.wait()
    project_qkv(normed, w_qkv, vec, TIME_QV, qkv)
    attend(qkv, key_mask(True), mixed)
    proj_copy.wait()
    out = (nn(mixed[...], w_proj[...]) + vec[TIME_PROJ_B : TIME_PROJ_B + 1, :]).astype(bf16)
    o1[...] = out
    for dest in range(4):
        sends[dest][...] = nn(place_to_send(dest), out).astype(bf16)


def frame_forward_kernel(scalars, tokens, vec, r0, r1, r2, r3, *refs):
    own_fc, own_qkv, own_proj, *pieces = refs[:8]
    x1, h2, qkv, mixed, x2, h3 = refs[8:14]
    w_fc, w_qkv, w_proj, sem_a, sem_b, sem_c = refs[14:]
    fc_copy = Weights(scalars, own_fc, pieces, TIME_FC_PARTS, SPACE_CHUNK, w_fc, sem_a)
    qkv_copy = Weights(scalars, own_qkv, pieces, SPACE_QKV_PARTS, SPACE_CHUNK, w_qkv, sem_b)
    proj_copy = Weights(scalars, own_proj, pieces, SPACE_PROJ_PARTS, SPACE_CHUNK, w_proj, sem_c)
    fc_copy.start()
    qkv_copy.start()
    proj_copy.start()
    group_at = scalars[0]
    received = sum(
        nn(recv_to_frame(group_at, source), ref[...]) for source, ref in enumerate((r0, r1, r2, r3))
    ).astype(bf16)
    fc_copy.wait()
    branch = nn(received, w_fc[...]) + vec[TIME_FC_B : TIME_FC_B + 1, :]
    after = tokens[...].astype(f32) + branch
    x1[...] = after
    normal, unused = norm_parts(after)
    normed = normal * vec[SPACE_GAIN : SPACE_GAIN + 1, :] + vec[SPACE_SHIFT : SPACE_SHIFT + 1, :]
    normed = normed.astype(bf16)
    h2[...] = normed
    qkv_copy.wait()
    project_qkv(normed, w_qkv, vec, SPACE_QV, qkv)
    attend(qkv, key_mask(False), mixed)
    proj_copy.wait()
    after = x1[...] + (nn(mixed[...], w_proj[...]) + vec[SPACE_PROJ_B : SPACE_PROJ_B + 1, :])
    x2[...] = after
    normal, unused = norm_parts(after)
    normed = normal * vec[MLP_GAIN : MLP_GAIN + 1, :] + vec[MLP_SHIFT : MLP_SHIFT + 1, :]
    h3[...] = normed.astype(bf16)


def norm_back(values, gain, grad_normed):
    normal, inverse = norm_parts(values)
    scaled = grad_normed * gain
    mean = jnp.mean(scaled, axis=-1, keepdims=True)
    along = jnp.mean(scaled * normal, axis=-1, keepdims=True)
    grad = inverse * (scaled - mean - normal * along)
    return (
        grad,
        jnp.sum(grad_normed * normal, axis=0, keepdims=True),
        jnp.sum(grad_normed, axis=0, keepdims=True),
    )


def column_sum(values):
    return jnp.sum(values.astype(f32), axis=0, keepdims=True)


def mlp_kernel(scalars, live, vec, x2, h3, out_grad, *refs):
    own_in, own_out, *pieces = refs[:11]
    in_pieces, out_pieces = [pieces[0]] + pieces[1:5], [pieces[0]] + pieces[5:9]
    layer_out, acts, du, dm, e2, sums, w_in, w_out, sem_a, sem_b = refs[11:]
    in_copy = Weights(scalars, own_in, in_pieces, MLP_IN_PARTS, IN_CHUNK, w_in, sem_a)
    out_copy = Weights(scalars, own_out, out_pieces, MLP_OUT_PARTS, OUT_CHUNK, w_out, sem_b, 3)
    in_copy.start()
    out_copy.start()
    e3 = live[0, 0] * out_grad[...].astype(f32)
    grad_branch = e3.astype(bf16)
    dm[...] = grad_branch
    sums[3:4, :] = column_sum(grad_branch)
    sums[4:8, :] = jnp.zeros((4, D), f32)
    normed = h3[...]
    in_copy.wait()
    out_copy.wait()
    x3 = x2[...] + vec[MLP_OUT_B : MLP_OUT_B + 1, :]
    e2[...] = x3
    back = None
    for part in range(4):
        columns = slice(part * D, (part + 1) * D)
        pre = nn(normed, w_in[:, columns]) + vec[MLP_IN_B + part : MLP_IN_B + part + 1, :]
        cdf = 0.5 * (1.0 + lax.erf(pre * (0.5**0.5)))
        act = (pre * cdf).astype(bf16)
        slope = cdf + pre * jnp.exp(-0.5 * pre * pre) * 0.3989422804014327
        acts[:, columns] = act
        grad = (slope * nt(grad_branch, w_out[columns, :])).astype(bf16)
        du[:, columns] = grad
        sums[4 + part : 5 + part, :] = column_sum(grad)
        e2[...] += nn(act, w_out[columns, :])
        piece = nt(grad, w_in[:, columns])
        back = piece if back is None else back + piece
    layer_out[...] = (live[0, 0] * e2[...]).astype(bf16)
    grad, gain_grad, shift_grad = norm_back(x2[...], vec[MLP_GAIN : MLP_GAIN + 1, :], back)
    sums[0:1, :] = gain_grad
    sums[1:2, :] = shift_grad
    sums[2:3, :] = jnp.zeros((1, D), f32)
    e2[...] = e3 + grad


def space_back_kernel(scalars, vec, e2, x1, qkv, *refs):
    own_proj, own_qkv, *pieces = refs[:7]
    dqkv, e1, dt2, sums, s0, s1, s2, s3, w_qkv, w_proj, da, sem_a, sem_b = refs[7:]
    proj_copy = Weights(scalars, own_proj, pieces, SPACE_PROJ_PARTS, SPACE_CHUNK, w_proj, sem_a)
    qkv_copy = Weights(scalars, own_qkv, pieces, SPACE_QKV_PARTS, SPACE_CHUNK, w_qkv, sem_b)
    proj_copy.start()
    qkv_copy.start()
    branch = e2[...].astype(bf16)
    dt2[...] = branch
    proj_copy.wait()
    da[...] = nt(branch, w_proj[...]).astype(bf16)
    attend_back(qkv, key_mask(False), da, dqkv)
    qkv_copy.wait()
    back = nt(dqkv[...], w_qkv[...])
    grad, gain_grad, shift_grad = norm_back(x1[...], vec[SPACE_GAIN : SPACE_GAIN + 1, :], back)
    total = e2[...] + grad
    e1[...] = total
    rounded = total.astype(bf16)
    for source, ref in enumerate((s0, s1, s2, s3)):
        ref[...] = tn(recv_to_frame(scalars[0], source), rounded).astype(bf16)
    sums[0:1, :] = gain_grad
    sums[1:2, :] = shift_grad
    sums[2:3, :] = column_sum(branch)
    sums[3:4, :] = column_sum(dqkv[:, :D])
    sums[4:5, :] = column_sum(dqkv[:, 2 * D :])
    sums[5:8, :] = jnp.zeros((3, D), f32)


def time_projections_kernel(scalars, r0, r1, r2, r3, *refs):
    own_fc, own_proj, packed, *pieces = refs[:11]
    dt1, do1, da1, sums, w_fc, w_proj, sem_a, sem_b = refs[11:]
    fc_pieces, pieces = [packed] + pieces[:4], [packed] + pieces[4:]
    fc_copy = Weights(scalars, own_fc, fc_pieces, TIME_FC_PARTS, SPACE_CHUNK, w_fc, sem_a)
    proj_copy = Weights(scalars, own_proj, pieces, TIME_PROJ_PARTS, TIME_CHUNK, w_proj, sem_b)
    fc_copy.start()
    proj_copy.start()
    branch = sum(
        tn(place_to_send(source), ref[...]) for source, ref in enumerate((r0, r1, r2, r3))
    ).astype(bf16)
    dt1[...] = branch
    fc_copy.wait()
    projected = nt(branch, w_fc[...]).astype(bf16)
    do1[...] = projected
    proj_copy.wait()
    da1[...] = nt(projected, w_proj[...]).astype(bf16)
    sums[0:1, :] = column_sum(projected)
    sums[1:2, :] = column_sum(branch)
    sums[2:8, :] = jnp.zeros((6, D), f32)


def time_back_kernel(scalars, vec, tokens, qkv, da1, early_sums, own_qkv, *refs):
    pieces, (dqkv, sums, s0, s1, s2, s3, w_qkv, sem) = refs[:5], refs[5:]
    qkv_copy = Weights(scalars, own_qkv, pieces, TIME_QKV_PARTS, TIME_CHUNK, w_qkv, sem)
    qkv_copy.start()
    attend_back(qkv, key_mask(True), da1, dqkv)
    qkv_copy.wait()
    back = nt(dqkv[...], w_qkv[...])
    grad, gain_grad, shift_grad = norm_back(
        tokens[...].astype(f32), vec[TIME_GAIN : TIME_GAIN + 1, :], back
    )
    rounded = grad.astype(bf16)
    for dest, ref in enumerate((s0, s1, s2, s3)):
        ref[...] = nn(place_to_send(dest), rounded).astype(bf16)
    sums[0:1, :] = gain_grad
    sums[1:2, :] = shift_grad
    sums[2:4, :] = early_sums[0:2, :]
    sums[4:5, :] = column_sum(dqkv[:, :D])
    sums[5:6, :] = column_sum(dqkv[:, 2 * D :])
    sums[6:8, :] = jnp.zeros((2, D), f32)


def weight_grad_kernel(scalars, *refs, count, tables):
    inputs, (kept, sent, turned, ordered) = refs[:-4], refs[-4:]
    core = scalars[0] % 2

    def store(shard, rows, columns, values):
        @pl.when(core == shard % 2)
        def _():
            kept[shard // 2, rows, columns] = values

        @pl.when(core != shard % 2)
        def _():
            sent[shard // 2, rows, columns] = values

    at = 0
    for index in range(count):
        left, right = inputs[2 * index : 2 * index + 2]
        width = left.shape[1]
        shard_rows = width // 4
        if shard_rows % 128 == 0:
            for spot in range(4):
                shard = 2 * (spot % 2) + (core if spot < 2 else 1 - core)
                source = pl.ds(pl.multiple_of(shard * shard_rows, shard_rows), shard_rows)
                target = kept if spot < 2 else sent
                for block in range(right.shape[1] // D):
                    total = tn(left[:, source], right[:, block * D : (block + 1) * D])
                    rows = slice(at + block * shard_rows, at + (block + 1) * shard_rows)
                    target[spot % 2, rows, :] = total.astype(bf16)
            at += shard_rows * (right.shape[1] // D)
            continue
        turned[0:width, :] = left[...].T
        for spot in range(4):
            shard = 2 * (spot % 2) + (core if spot < 2 else 1 - core)
            source = pl.ds(pl.multiple_of(shard * shard_rows, shard_rows), shard_rows)
            ordered[spot * shard_rows : (spot + 1) * shard_rows, :] = turned[source, :]
        for block in range(right.shape[1] // D):
            columns = slice(block * D, (block + 1) * D)
            total = nn(ordered[...], right[:, columns]).astype(bf16)
            for spot in range(4):
                target = kept if spot < 2 else sent
                target[spot % 2, at : at + shard_rows, :] = total[
                    spot * shard_rows : (spot + 1) * shard_rows, :
                ]
            at += shard_rows
    if tables:
        time, space, mlp = (ref[...] for ref in inputs[2 * count :])
        singles = jnp.concatenate([time[0:4], space[0:3], mlp[0:2], mlp[3:4]], axis=0)
        for ref in (kept, sent):
            for chip in range(2):
                ref[chip, at : at + EXTRA, :] = jnp.zeros((EXTRA, D), bf16)
        for shard in range(4):
            lanes = slice(shard * BLOCK, (shard + 1) * BLOCK)
            store(shard, slice(at, at + 10), slice(0, BLOCK), singles[:, lanes].astype(bf16))
            half = slice((shard % 2) * (D // 2), (shard % 2 + 1) * (D // 2))
            for row, pair in ((10, time[4:6]), (11, space[3:5])):
                values = pair[shard // 2 : shard // 2 + 1, half].astype(bf16)
                store(shard, slice(at + row, at + row + 1), slice(0, D // 2), values)
            values = mlp[4 + shard : 5 + shard, :].astype(bf16)
            store(shard, slice(at + 12, at + 13), slice(0, D), values)


def last_kernel(scalars, e1, r0, r1, r2, r3, out):
    total = e1[...]
    for source, ref in enumerate((r0, r1, r2, r3)):
        total = total + nn(recv_to_frame(scalars[0], source), ref[...])
    out[...] = total


def shape(rows, columns, kind):
    return jax.ShapeDtypeStruct((rows, columns), kind)


VMEM = pl.BlockSpec(memory_space=pltpu.MemorySpace.VMEM)
SMEM = pl.BlockSpec(memory_space=pltpu.MemorySpace.SMEM)
ANY = pl.BlockSpec(memory_space=pltpu.MemorySpace.HBM)


def in_hbm(array):
    return pltpu.with_memory_space_constraint(array, pltpu.MemorySpace.HBM)


def call(kernel, name, outs, specs, scratch, operands, microseconds):
    return pl.pallas_call(
        kernel,
        name=name,
        out_shape=outs,
        in_specs=specs,
        out_specs=[VMEM] * len(outs),
        scratch_shapes=scratch,
        compiler_params=pltpu.CompilerParams(vmem_limit_bytes=LIMITS.get(name, 5) << 20),
        cost_estimate=pl.CostEstimate(
            flops=int((microseconds + 10) * 1.1e9), transcendentals=0,
            bytes_accessed=1024,
        ),
    )(*operands)


def dma_sems(parts):
    return pltpu.SemaphoreType.DMA((1 + 3 * len(parts),))


def vmem(rows, columns, kind=bf16):
    return pltpu.VMEM((rows, columns), kind)


def place_forward(scalars, tokens, vec, owns, pieces):
    outs = [shape(ROWS, D, bf16), shape(ROWS, 3 * D, bf16), shape(ROWS, D, bf16)]
    outs += [shape(ROWS, D, bf16)] + [shape(CHUNK, D, bf16)] * 4
    return call(
        place_forward_kernel, "place_forward", outs, [SMEM, VMEM, VMEM] + [ANY] * 7,
        [vmem(D, 3 * D), vmem(D, D), dma_sems(TIME_QKV_PARTS), dma_sems(TIME_PROJ_PARTS)],
        (scalars, tokens, vec, *owns, *pieces), 11,
    )


def frame_forward(scalars, tokens, vec, received, owns, pieces):
    outs = [shape(ROWS, D, f32), shape(ROWS, D, bf16), shape(ROWS, 3 * D, bf16)]
    outs += [shape(ROWS, D, bf16), shape(ROWS, D, f32), shape(ROWS, D, bf16)]
    return call(
        frame_forward_kernel, "frame_forward", outs, [SMEM] + [VMEM] * 6 + [ANY] * 8,
        [
            vmem(D, D), vmem(D, 3 * D), vmem(D, D),
            dma_sems(TIME_FC_PARTS), dma_sems(SPACE_QKV_PARTS), dma_sems(SPACE_PROJ_PARTS),
        ],
        (scalars, tokens, vec, *received, *owns, *pieces), 13,
    )


def mlp_both(scalars, live, vec, x2, h3, out_grad, owns, in_pieces, out_pieces):
    outs = [
        shape(ROWS, D, bf16), shape(ROWS, FF, bf16), shape(ROWS, FF, bf16),
        shape(ROWS, D, bf16), shape(ROWS, D, f32), shape(8, D, f32),
    ]
    return call(
        mlp_kernel, "mlp_both", outs, [SMEM, SMEM] + [VMEM] * 4 + [ANY] * 11,
        [vmem(D, FF), vmem(FF, D), dma_sems(MLP_IN_PARTS), dma_sems(MLP_OUT_PARTS)],
        (scalars, live, vec, x2, h3, out_grad, *owns, *in_pieces, *out_pieces[1:]), 18,
    )


def space_back(scalars, vec, e2, x1, qkv, owns, pieces):
    outs = [shape(ROWS, 3 * D, bf16), shape(ROWS, D, f32), shape(ROWS, D, bf16)]
    outs += [shape(8, D, f32)] + [shape(CHUNK, D, bf16)] * 4
    return call(
        space_back_kernel, "space_back", outs, [SMEM] + [VMEM] * 4 + [ANY] * 7,
        [
            vmem(D, 3 * D), vmem(D, D), vmem(ROWS, D),
            dma_sems(SPACE_PROJ_PARTS), dma_sems(SPACE_QKV_PARTS),
        ],
        (scalars, vec, e2, x1, qkv, *owns, *pieces), 20,
    )


def time_projections(scalars, received, owns, fc_pieces, pieces):
    outs = [shape(ROWS, D, bf16)] * 3 + [shape(8, D, f32)]
    return call(
        time_projections_kernel, "time_projections", outs, [SMEM] + [VMEM] * 4 + [ANY] * 11,
        [vmem(D, D), vmem(D, D), dma_sems(TIME_FC_PARTS), dma_sems(TIME_PROJ_PARTS)],
        (scalars, *received, *owns, *fc_pieces, *pieces[1:]), 4,
    )


def time_back(scalars, vec, tokens, qkv, da1, early_sums, own, pieces):
    outs = [shape(ROWS, 3 * D, bf16), shape(8, D, f32)] + [shape(CHUNK, D, bf16)] * 4
    return call(
        time_back_kernel, "time_back", outs, [SMEM] + [VMEM] * 5 + [ANY] * 6,
        [vmem(D, 3 * D), dma_sems(TIME_QKV_PARTS)],
        (scalars, vec, tokens, qkv, da1, early_sums, own, *pieces), 16,
    )


def weight_grads(name, scalars, groups, tables=()):
    rows = sum(g[0].shape[1] // 4 * (g[1].shape[1] // D) for g in groups)
    flat = [array for group in groups for array in group] + list(tables)
    rows += EXTRA if tables else 0
    kernel = functools.partial(weight_grad_kernel, count=len(groups), tables=len(tables))
    return call(
        kernel, name, [jax.ShapeDtypeStruct((2, rows, D), bf16)] * 2, [SMEM] + [VMEM] * len(flat),
        [vmem(D, ROWS)] * 2, (scalars, *flat), rows / 150,
    )


def copy_all(copies):
    for copy in copies:
        copy.start()
    for copy in copies:
        copy.wait()


def columns_of(ref, at):
    return ref.at[:, pl.ds(pl.multiple_of(at * D, D), D)]


def pack_time_kernel(scalars, time_qkv, time_proj, vectors, out, sems):
    first, second = out.at[pl.ds(0, BLOCK), :], out.at[pl.ds(BLOCK, BLOCK), :]
    tail = pltpu.make_async_copy(vectors, out.at[pl.ds(2 * BLOCK, VECTOR_PAD), :], sems.at[2])
    tail.start()

    @pl.when(scalars[1] == 0)
    def _():
        pltpu.make_async_copy(columns_of(time_qkv, 0), first, sems.at[0]).start()
        pltpu.make_async_copy(columns_of(time_qkv, 1), second, sems.at[1]).start()

    @pl.when(scalars[1] != 0)
    def _():
        pltpu.make_async_copy(columns_of(time_qkv, 2), first, sems.at[0]).start()
        pltpu.make_async_copy(time_proj, second, sems.at[1]).start()

    pltpu.make_async_copy(time_proj, first, sems.at[0]).wait()
    pltpu.make_async_copy(time_proj, second, sems.at[1]).wait()
    tail.wait()


def pack_rest_kernel(
    scalars, time_qkv, time_proj, time_fc, space_qkv, space_proj, mlp_in, mlp_out, vectors,
    packed, space_half, in_half, out_half, sems,
):
    half = scalars[1]
    copies = []

    def add(source, target, row, rows):
        target = target.at[pl.ds(row, rows), :]
        copies.append(pltpu.make_async_copy(source, target, sems.at[len(copies)]))

    out_at = scalars[3]
    halves = pl.ds(pl.multiple_of(out_at * 2 * BLOCK, 2 * BLOCK), 2 * BLOCK)
    add(columns_of(mlp_in, 2 * half), in_half, 0, BLOCK)
    add(columns_of(mlp_in, 2 * half + 1), in_half, BLOCK, BLOCK)
    add(mlp_out.at[halves, :], out_half, 0, 2 * BLOCK)
    blocks = [columns_of(time_qkv, at) for at in range(3)] + [time_proj]
    blocks += [columns_of(space_qkv, 0), columns_of(space_qkv, 1), time_fc]
    blocks += [columns_of(space_qkv, 2), space_proj]
    blocks += [columns_of(mlp_in, at) for at in range(4)]
    for at, source in enumerate(blocks):
        add(source, packed, at * BLOCK, BLOCK)
    add(mlp_out, packed, 13 * BLOCK, 4 * BLOCK)
    add(vectors, packed, VECTOR_AT, VECTOR_PAD)
    at = len(copies)
    middle = BLOCK // 2

    def space(source, row, rows, sem):
        return pltpu.make_async_copy(source, space_half.at[pl.ds(row, rows), :], sems.at[sem])

    @pl.when(half == 0)
    def _():
        space(columns_of(space_qkv, 0), 0, BLOCK, at).start()
        space(columns_of(space_qkv, 1), BLOCK, BLOCK, at + 1).start()
        space(time_fc.at[pl.ds(0, middle), :], 2 * BLOCK, middle, at + 2).start()

    @pl.when(half != 0)
    def _():
        space(time_fc.at[pl.ds(middle, middle), :], 0, middle, at + 2).start()
        space(columns_of(space_qkv, 2), middle, BLOCK, at).start()
        space(space_proj, BLOCK + middle, BLOCK, at + 1).start()

    copy_all(copies)
    space(space_proj, 0, BLOCK, at).wait()
    space(space_proj, BLOCK, BLOCK, at + 1).wait()
    space(time_fc.at[pl.ds(0, middle), :], 2 * BLOCK, middle, at + 2).wait()


def pack_time(*operands):
    operands = [operands[0], *map(in_hbm, operands[1:])]
    return pl.pallas_call(
        pack_time_kernel, name="pack_time",
        compiler_params=pltpu.CompilerParams(vmem_limit_bytes=LIMITS.get("pack_time", 5) << 20), out_shape=shape(2 * BLOCK + VECTOR_PAD, D, bf16),
        in_specs=[SMEM, ANY, ANY, ANY], out_specs=VMEM,
        scratch_shapes=[pltpu.SemaphoreType.DMA((3,))],
        cost_estimate=pl.CostEstimate(flops=11 * 10**9, transcendentals=0, bytes_accessed=1024),
    )(*operands)


def pack_rest(*operands):
    operands = [operands[0], *map(in_hbm, operands[1:])]
    return pl.pallas_call(
        pack_rest_kernel, name="pack_rest",
        compiler_params=pltpu.CompilerParams(vmem_limit_bytes=LIMITS.get("pack_rest", 5) << 20),
        out_shape=[
            shape(VECTOR_AT + VECTOR_PAD, D, bf16), shape(480, D, bf16), shape(384, D, bf16),
            shape(384, D, bf16),
        ],
        in_specs=[SMEM] + [ANY] * 8, out_specs=[VMEM] * 4,
        scratch_shapes=[pltpu.SemaphoreType.DMA((21,))],
        cost_estimate=pl.CostEstimate(flops=11 * 10**9, transcendentals=0, bytes_accessed=1024),
    )(*operands)


def table_kernel(scalars, own, packed, direct, across, out, pieces, sems):
    copies = [
        pltpu.make_async_copy(source.at[pl.ds(row, VECTOR_PAD), :], pieces.at[at], sems.at[at])
        for at, (source, row) in enumerate(
            ((own, 0), (packed, VECTOR_AT), (direct, 2 * BLOCK), (across, 2 * BLOCK))
        )
    ]
    copy_all(copies)
    group_at = scalars[0]
    out[...] = jnp.zeros((VECTOR_PAD, D), f32)
    for shard in range(4):
        rows = pieces[group_at ^ shard].astype(f32)[:, :BLOCK]
        lanes = slice(shard * BLOCK, (shard + 1) * BLOCK)
        out[0:10, lanes] = rows[0:10]
        for row in range(2):
            lanes = slice((shard % 2) * 384 + row * BLOCK, (shard % 2) * 384 + (row + 1) * BLOCK)
            for first in (TIME_QV, SPACE_QV):
                source = rows[first + row : first + row + 1]
                out[first + shard // 2 : first + shard // 2 + 1, lanes] = source
        for row in range(4):
            lanes = slice(row * BLOCK, (row + 1) * BLOCK)
            source = rows[MLP_IN_B + row : MLP_IN_B + row + 1]
            out[MLP_IN_B + shard : MLP_IN_B + shard + 1, lanes] = source


def vector_table(*operands):
    return call(
        table_kernel, "table", [shape(VECTOR_PAD, D, f32)], [SMEM] + [ANY] * 4,
        [pltpu.VMEM((4, VECTOR_PAD, D), bf16), pltpu.SemaphoreType.DMA((4,))], operands, 1,
    )[0]


def unpack_kernel(scalars, mine, other, *outs, bit, parts):
    own_first = (scalars[2] // bit) % 2 == 0
    for half, row, rows, index, out_row, column in parts:
        rows = pl.ds(row, rows)
        near, far = mine[rows, :], other[rows, :]
        pair = (near, far) if half == 0 else (far, near)
        outs[index][out_row : out_row + rows.size, column * D : (column + 1) * D] = jnp.where(
            own_first, *pair
        ).astype(f32)


def unpack(scalars, mine, other, bit, parts, outs):
    kernel = functools.partial(unpack_kernel, bit=bit, parts=parts)
    return call(
        kernel, "unpack", [shape(*out, f32) for out in outs], [SMEM, VMEM, VMEM], [],
        (scalars, mine, other), 2,
    )


OUT_PARTS = ((0, 0, 384, 0, 0, 0), (1, 0, 384, 0, 384, 0))
IN_PARTS = (
    (0, 0, 192, 0, 0, 0), (0, 192, 192, 0, 0, 1), (1, 0, 192, 0, 0, 2), (1, 192, 192, 0, 0, 3),
)
SPACE_PARTS = (
    (0, 0, 192, 0, 0, 0), (0, 192, 192, 0, 0, 1), (1, 0, 192, 0, 0, 2), (1, 192, 192, 1, 0, 0),
)
SMALL_PARTS = ((0, 0, 192, 0, 0, 0), (1, 0, 192, 1, 0, 0))
TIME_PARTS = (
    (0, 0, 192, 0, 0, 0), (0, 192, 128, 0, 0, 1), (1, 0, 64, 0, 128, 1), (1, 64, 192, 0, 0, 2),
    (1, 256, 16, 1, 0, 0),
)


def last_sum(scalars, e1, received):
    return call(
        last_kernel, "last_sum", [shape(ROWS, D, f32)], [SMEM] + [VMEM] * 5, [],
        (scalars, e1, *received), 2,
    )[0]


def flip(array, axis, bit, size):
    return lax.ppermute(array, axis, [(at, at ^ bit) for at in range(size)])


def pick(array, at):
    return lax.dynamic_index_in_dim(array, at, 0, keepdims=False)


def add_rounded(left, right):
    return (left.astype(f32) + right.astype(f32)).astype(bf16)


def after(value, *others):
    return lax.optimization_barrier((value,) + others)[0]


def halves_of(own, half_at):
    return lax.dynamic_slice_in_dim(own, half_at * (own.shape[0] // 2), own.shape[0] // 2, 0)


def step_rows(rows):
    return next(step for step in (96, 80, 48, 16) if rows % step == 0)


def sum_split_kernel(scalars, kept, got, keep, send, *, bit):
    rows = keep.shape[-2]
    step = step_rows(rows)
    if bit == 0:
        mine = scalars[0] // 2
    else:
        mine = (scalars[2] // bit) % 2
    for target, at in ((keep, mine), (send, 1 - mine)):

        def body(index, carry, target=target, at=at):
            row = pl.multiple_of(index * step, 16)
            if bit == 0:
                total = kept[at, pl.ds(row, step), :].astype(f32)
                total = total + got[at, pl.ds(row, step), :].astype(f32)
                target[pl.ds(row, step), :] = total.astype(bf16)
            else:
                source = pl.ds(pl.multiple_of(at * rows + row, 16), step)
                for chip in range(2) if len(keep.shape) == 3 else [None]:
                    here = (source, slice(None)) if chip is None else (chip, source, slice(None))
                    there = (pl.ds(row, step), slice(None))
                    there = there if chip is None else (chip,) + there
                    total = kept[here].astype(f32) + got[here].astype(f32)
                    target[there] = total.astype(bf16)
            return carry

        lax.fori_loop(0, rows // step, body, 0)


def sum_split(scalars, kept, got, bit):
    dims = kept.shape
    out = dims[1:] if bit == 0 else dims[:-2] + (dims[-2] // 2, D)
    kernel = functools.partial(sum_split_kernel, bit=bit)
    outs = [jax.ShapeDtypeStruct(out, bf16)] * 2
    return call(kernel, "sum_split", outs, [SMEM, VMEM, VMEM], [], (scalars, kept, got), 0)


def join_kernel(scalars, mine, other, out, *, bit):
    rows = mine.shape[0]
    at = (scalars[2] // bit) % 2
    out[pl.ds(pl.multiple_of(at * rows, 16), rows), :] = mine[...]
    out[pl.ds(pl.multiple_of((1 - at) * rows, 16), rows), :] = other[...]


def join(scalars, mine, other, bit):
    kernel = functools.partial(join_kernel, bit=bit)
    outs = [shape(2 * mine.shape[0], D, bf16)]
    return call(kernel, "join", outs, [SMEM, VMEM, VMEM], [], (scalars, mine, other), 0)[0]


class Reduce:
    def __init__(self, parts, order, scalars, replica_at, ring_size):
        self.kept, sent = parts
        self.scalars, self.replica_at, self.ring_size = scalars, replica_at, ring_size
        self.steps = [("sum", bit) for bit in order]
        self.steps += [("gather", bit) for bit in reversed(order) if bit]
        self.flying = flip(sent, "group", 1, 4)
        self.halve = lambda array: array

    def split(self, bit):
        if bit == 0:
            chip = self.scalars[0] // 2
            return (lambda a: pick(a, chip)), (lambda a: pick(a, 1 - chip))
        mine = (self.replica_at // bit) % 2

        def half(at):
            def take(array):
                rows = array.shape[-2] // 2
                return lax.dynamic_slice_in_dim(array, at * rows, rows, array.ndim - 2)

            return take

        return half(mine), half(1 - mine)

    def flip(self, array, bit):
        axis = ("group", 2, 4) if bit == 0 else ("replica", bit, self.ring_size)
        return flip(array, *axis)

    def advance(self, *others):
        got = after(self.flying, *others) if others else self.flying
        if self.kept is not None:
            if self.steps[0][0] == "sum":
                bit = self.steps.pop(0)[1]
                if self.kept.shape[-2] % 32 == 0:
                    self.kept, sent = sum_split(self.scalars, self.kept, got, bit)
                else:
                    keep, send = self.split(bit)
                    sent = add_rounded(send(self.kept), send(got))
                    self.kept = add_rounded(keep(self.kept), keep(got))
            else:
                sent = self.current = add_rounded(self.kept, got)
                self.kept = None
                bit = self.steps[0][1]
        else:
            bit = self.steps.pop(0)[1]
            mine = (self.replica_at // bit) % 2
            if not self.steps:
                self.got, self.bit = got, bit
                return got
            if got.shape[0] % 16 == 0:
                self.current = join(self.scalars, self.current, got, bit)
            else:
                self.current = jnp.where(
                    mine == 0,
                    jnp.concatenate([self.current, got], 0),
                    jnp.concatenate([got, self.current], 0),
                )
            sent = self.current
            bit = self.steps[0][1]
        self.flying = self.flip(sent, bit)
        return sent

    def unpacked(self, parts, outs):
        return unpack(self.scalars, self.current, self.got, self.bit, parts, outs)


def block(array, at):
    return array[:, at * D : (at + 1) * D]


def unpack_grad(summed, blocks):
    return summed.reshape(blocks, BLOCK, D).transpose(1, 0, 2).reshape(BLOCK, blocks * D).astype(f32)


def exchange(chunks):
    return [chunks[0]] + [flip(chunks[d], "group", d, 4) for d in range(1, 4)]


def build(mesh):
    ring_size = mesh.shape["replica"]

    def on_device(tokens, out_grad, slot_mask, *shards):
        (
            time_norm_gain, time_norm_shift, time_qkv, time_qv_bias, time_proj, time_proj_bias,
            time_fc, time_fc_bias, space_norm_gain, space_norm_shift, space_qkv, space_qv_bias,
            space_proj, space_proj_bias, mlp_norm_gain, mlp_norm_shift, mlp_in, mlp_in_bias,
            mlp_out, mlp_out_bias,
        ) = shards
        group_at = lax.axis_index("group")
        replica_at = lax.axis_index("replica")
        half_at = replica_at % 2
        far_at = (replica_at // 2) % 2
        scalars = jnp.stack([group_at, half_at, replica_at, far_at]).astype(jnp.int32)
        live = slot_mask.astype(f32).reshape(1, 1)
        vectors = [
            time_norm_gain, time_norm_shift, time_proj_bias, time_fc_bias, space_norm_gain,
            space_norm_shift, space_proj_bias, mlp_norm_gain, mlp_norm_shift, mlp_out_bias,
            time_qv_bias, space_qv_bias, mlp_in_bias,
        ]
        cross = functools.partial(flip, axis="group", bit=2, size=4)
        near = functools.partial(flip, axis="group", bit=1, size=4)
        relay = functools.partial(flip, axis="replica", bit=1, size=ring_size)
        ends = [sum(v.shape[0] for v in vectors[: at + 1]) for at in range(len(vectors))]
        room = VECTOR_PAD * BLOCK
        flat = sum(jnp.pad(v, (at - v.shape[0], room - at)) for v, at in zip(vectors, ends))
        flat = jnp.pad(flat.reshape(VECTOR_PAD, BLOCK), ((0, 0), (0, D - BLOCK)))
        token_pieces = tokens[0].transpose(1, 0, 2).reshape(4, 49, 2, D)
        token_pieces = [pick(token_pieces, group_at ^ d) for d in range(4)]
        got = exchange(token_pieces)
        time_half = pack_time(scalars, time_qkv, time_proj, after(flat, *token_pieces))
        time_direct = cross(after(time_half, *got[1:]))
        place_tokens = jnp.pad(jnp.concatenate(got, axis=1), ((0, 3), (0, 0), (0, 0)))
        place_tokens = place_tokens.reshape(ROWS, D)

        packed, space_half, in_half, out_half = pack_rest(
            scalars, time_qkv, time_proj, time_fc, space_qkv, space_proj, mlp_in, mlp_out,
            after(flat, *got[1:]),
        )
        partner = near(packed)
        time_across = near(time_direct)
        time_relayed = relay(time_direct)
        space_direct = cross(after(space_half, time_direct))
        in_direct = cross(after(in_half, space_direct))
        out_direct = cross(after(out_half, space_direct))

        vec = vector_table(scalars, flat, partner, time_direct, time_across)
        time_pieces = (
            partner, time_direct, time_relayed, time_across, near(after(time_relayed, vec)),
        )
        pads = ((0, 0), (0, HALF - PLACES), (0, 0))
        frame_tokens = jnp.pad(tokens[0], pads).reshape(ROWS, D)
        frame_grad = jnp.pad(out_grad[0], pads).reshape(ROWS, D)

        space_across = near(space_direct)
        h1, qkv1, a1, o1, *sends = place_forward(
            scalars, after(place_tokens, space_direct), vec, (time_qkv, time_proj), time_pieces
        )
        received = exchange(sends)
        space_relayed = relay(space_direct)
        space_pieces = (
            partner, space_direct, space_relayed, space_across,
            near(after(space_relayed, o1)),
        )
        x1, h2, qkv2, a2, x2, h3 = frame_forward(
            scalars, after(frame_tokens, in_direct, out_direct), vec, received,
            (time_fc, space_qkv, space_proj), space_pieces,
        )
        in_relayed = relay(in_direct)
        in_pieces = (
            partner, in_direct, in_relayed, near(in_direct), near(after(in_relayed, x2)),
        )
        out_relayed = flip(out_direct, "replica", 2, ring_size)
        out_pieces = (
            partner, out_direct, out_relayed, near(after(out_direct, x2)),
            near(after(out_relayed, x2)),
        )
        layer_out, act, du, dm, e2, sums3 = mlp_both(
            scalars, live, vec, x2, h3, frame_grad, (mlp_in, mlp_out), in_pieces, out_pieces
        )
        layer_out = layer_out.reshape(2, HALF, D)[None, :, :PLACES]

        chunk = functools.partial(
            Reduce, scalars=scalars, replica_at=replica_at, ring_size=ring_size
        )
        bits = [1 << at for at in range(ring_size.bit_length() - 1)]
        along = [0] + bits
        names = {"x": 0, "y": bits[0], "u": bits[1], "w": bits[2]}

        def way(parts, order):
            return chunk(parts, [names[name] for name in order] + bits[3:])

        ways = {}
        last = ()

        back = {"sent": None, "got": [], "flying": None, "out": None}

        def move_back():
            nonlocal last
            sends, got = back["sent"], back["got"]
            if back["flying"] is not None:
                got.append(after(back["flying"], *last))
                last = (got[-1],)
            at = len(got) + 1
            if at < 4:
                back["flying"] = flip(after(sends[at], *last), "group", at, 4)
            else:
                back["out"] = last_sum(scalars, e1, [sends[0]] + got)
                back["flying"] = None
                last = (back["out"],)

        def advance(steps):
            nonlocal last
            for name in steps:
                if name == "a":
                    move_back()
                elif ways[name].steps:
                    last = (ways[name].advance(*last),)

        ways["o"] = way(weight_grads("mlp_out_grad", scalars, [(act, dm)]), ORDERS["o"])
        last = (ways["o"].kept,)
        advance(SCHEDULE[0])
        ways["i"] = way(
            weight_grads("mlp_in_grad", scalars, [(h3, after(du, *last))]), ORDERS["i"]
        )
        last = (ways["i"].kept,)
        advance(SCHEDULE[1])
        dqkv2, e1, dt2, sums2, *sends = space_back(
            scalars, vec, after(e2, *last), x1, qkv2, (space_proj, space_qkv), space_pieces
        )
        received = exchange(sends)
        last = (e1,)
        advance(SCHEDULE[2])
        ways["s"] = way(
            weight_grads("space_grad", scalars, [(h2, after(dqkv2, *last)), (a2, dt2)]),
            ORDERS["s"],
        )
        last = (ways["s"].kept,)
        advance(SCHEDULE[3])
        dt1, do1, da1, early = time_projections(
            scalars, [after(received[0], *last)] + received[1:], (time_fc, time_proj),
            space_pieces, time_pieces,
        )
        last = (do1,)
        advance(SCHEDULE[4])
        ways["p"] = way(
            weight_grads("time_small_grad", scalars, [(a1, after(do1, *last)), (o1, dt1)]),
            ORDERS["p"],
        )
        last = (ways["p"].kept,)
        advance(SCHEDULE[5])
        dqkv1, sums1, *sends = time_back(
            scalars, vec, place_tokens, qkv1, after(da1, *last), early, time_qkv, time_pieces
        )
        back["sent"] = sends
        last = (dqkv1,)
        advance(SCHEDULE[6])
        ways["t"] = way(
            weight_grads(
                "time_grad", scalars, [(h1, after(dqkv1, *last))], (sums1, sums2, sums3)
            ),
            ORDERS["t"],
        )
        last = (ways["t"].kept,)
        advance(SCHEDULE[7])
        while back["out"] is None:
            move_back()
        tokens_grad = back["out"].reshape(2, HALF, D)[None, :, :PLACES]
        while any(each.steps for each in ways.values()):
            advance([name for name in ways])
        way_out, way_in, way_space, way_small, way_time = (ways[name] for name in "oispt")
        (d_out,) = way_out.unpacked(OUT_PARTS, [(D, D)])
        (d_in,) = way_in.unpacked(IN_PARTS, [(BLOCK, FF)])
        d_space_qkv, d_space_proj = way_space.unpacked(SPACE_PARTS, [(BLOCK, 3 * D), (BLOCK, D)])
        d_proj, d_fc = way_small.unpacked(SMALL_PARTS, [(BLOCK, D), (BLOCK, D)])
        d_time_qkv, vectors = way_time.unpacked(TIME_PARTS, [(BLOCK, 3 * D), (16, D)])
        ones = vectors[:10, :BLOCK]
        return (
            layer_out, tokens_grad, ones[0], ones[1], d_time_qkv, vectors[10, : D // 2],
            d_proj, ones[2], d_fc, ones[3], ones[4], ones[5], d_space_qkv,
            vectors[11, : D // 2], d_space_proj, ones[6], ones[7], ones[8], d_in, vectors[12],
            d_out, ones[9],
        )

    return on_device


def solution(mesh):
    rows = P("group", None)
    vector = P("group")
    batch = P("replica", "group", None, None)
    params = (
        vector, vector, rows, vector, rows, vector, rows, vector, vector, vector, rows, vector,
        rows, vector, vector, vector, rows, vector, rows, vector,
    )
    return jax.shard_map(
        build(mesh),
        mesh=mesh,
        in_specs=(batch, batch, P("replica")) + params,
        out_specs=(batch, batch) + params,
        check_vma=False,
    )
```

```python
import functools

import jax
import jax.numpy as jnp
from jax import lax
from jax.experimental import pallas as pl
from jax.experimental.pallas import tpu as pltpu
from jax.sharding import PartitionSpec as P

D = 768
FF = 3072
HEADS = 12
HEAD_DIM = 64
PLACES = 196
BLOCK = 192
CHUNK = 104
HALF = 208
ROWS = 416
epsilon = 1e-06
bf16 = jnp.bfloat16
f32 = jnp.float32

TIME_GAIN, TIME_SHIFT, TIME_PROJ_B, TIME_FC_B, SPACE_GAIN, SPACE_SHIFT, SPACE_PROJ_B = range(7)
MLP_GAIN, MLP_SHIFT, MLP_OUT_B = 7, 8, 9
TIME_QV, SPACE_QV, MLP_IN_B = 10, 12, 14
VECTOR_ROWS = 18
EXTRA = 64
LIMITS = {
    "place_forward": 10, "frame_forward": 14, "mlp_both": 28, "space_back": 19, "time_back": 13,
    "mlp_out_grad": 8, "mlp_in_grad": 8, "space_grad": 7, "pack_rest": 8, "time_projections": 6,
}
ORDERS = {"o": "yuxw", "i": "uxyw", "s": "xyuw", "p": "yxuw", "t": "xyuw"}
SCHEDULE = ('', '', '', 'ois', '', '', 'ois', 'potsoisoitpostipotsiptoaspatapitspaitp')

TIME_QKV_PARTS = ((0, 0, 192, 0, 0), (0, 192, 192, 0, 1), (1, 0, 192, 0, 2))
TIME_PROJ_PARTS = ((1, 192, 192, 0, 0),)
SPACE_QKV_PARTS = ((0, 0, 192, 0, 0), (0, 192, 192, 0, 1), (1, 96, 192, 0, 2))
SPACE_PROJ_PARTS = ((1, 288, 192, 0, 0),)
TIME_FC_PARTS = ((0, 384, 96, 0, 0), (1, 0, 96, 96, 0))
MLP_IN_PARTS = ((0, 0, 192, 0, 0), (0, 192, 192, 0, 1), (1, 0, 192, 0, 2), (1, 192, 192, 0, 3))
MLP_OUT_PARTS = ((0, 0, 384, 0, 0), (1, 0, 384, 384, 0))
TIME_CHUNK, SPACE_CHUNK, IN_CHUNK, OUT_CHUNK = (0, 768), (768, 960), (1728, 768), (2496, 768)
VECTOR_AT = 3264
VECTOR_PAD = 24


def nn(left, right):
    return lax.dot_general(left, right, (((1,), (0,)), ((), ())), preferred_element_type=f32)


def nt(left, right):
    return lax.dot_general(left, right, (((1,), (1,)), ((), ())), preferred_element_type=f32)


def tn(left, right):
    return lax.dot_general(left, right, (((0,), (0,)), ((), ())), preferred_element_type=f32)


def norm_parts(values):
    centred = values - jnp.mean(values, axis=-1, keepdims=True)
    inverse = lax.rsqrt(jnp.mean(centred * centred, axis=-1, keepdims=True) + epsilon)
    return centred * inverse, inverse


class Weights:
    def __init__(self, scalars, own, pieces, parts, chunk, target, sems, half_at=1):
        self.half_at = half_at
        self.scalars, self.own, self.pieces, self.parts = scalars, own, pieces, parts
        self.chunk, self.target, self.sems = chunk, target, sems
        self.shard_rows = own.shape[0]

    def base(self, flipped):
        at = (self.scalars[0] ^ flipped) * self.shard_rows
        return pl.multiple_of(at, self.shard_rows)

    def copy(self, source, part, flipped, at):
        half, row, rows, block_row, column = part
        return pltpu.make_async_copy(
            source.at[pl.ds(row, rows), :],
            self.target.at[pl.ds(self.base(flipped) + block_row, rows), pl.ds(column * D, D)],
            self.sems.at[at],
        )

    def own_copy(self):
        target = self.target.at[pl.ds(self.base(0), self.shard_rows), :]
        return pltpu.make_async_copy(self.own, target, self.sems.at[0])

    def start(self):
        packed, direct, relayed, across, across_relayed = self.pieces
        self.own_copy().start()
        y = self.scalars[self.half_at]
        first, chunk_rows = self.chunk
        at = 1
        for part in self.parts:
            half, row, rows, block_row, column = part
            whole = (half, first + row + half * (chunk_rows // 2), rows, block_row, column)
            self.copy(packed, whole, 1, at).start()

            @pl.when(y == half)
            def _():
                self.copy(direct, part, 2, at + 1).start()
                self.copy(across, part, 3, at + 2).start()

            @pl.when(y != half)
            def _():
                self.copy(relayed, part, 2, at + 1).start()
                self.copy(across_relayed, part, 3, at + 2).start()

            at += 3

    def wait(self):
        direct, across = self.pieces[1], self.pieces[3]
        self.own_copy().wait()
        at = 1
        for part in self.parts:
            self.copy(direct, part, 1, at).wait()
            self.copy(direct, part, 2, at + 1).wait()
            self.copy(across, part, 3, at + 2).wait()
            at += 3


def lane_half(second):
    lane = lax.broadcasted_iota(jnp.int32, (HALF, 128), 1)
    return (lane >= 64) if second else (lane < 64)


def masked(values, second):
    return jnp.where(lane_half(second), values, jnp.zeros_like(values))


def key_mask(same_place):
    key = lax.broadcasted_iota(jnp.int32, (HALF, HALF), 0)
    query = lax.broadcasted_iota(jnp.int32, (HALF, HALF), 1)
    allowed = (key // 8 == query // 8) if same_place else (key < PLACES)
    return jnp.where(allowed, 0.0, -1e30).astype(f32)


def both_heads(pair):
    return jnp.concatenate([masked(pair, False), masked(pair, True)], axis=0)


def probs_of(keys, query_pair, mask):
    scores = nt(keys, query_pair).reshape(2, HALF, HALF) + mask[None]
    weights = jnp.exp(scores - jnp.max(scores, axis=1, keepdims=True))
    return weights * (1.0 / jnp.sum(weights, axis=1, keepdims=True))


def flat_heads(values):
    return values.astype(bf16).reshape(2 * HALF, HALF)


def attend(qkv_ref, mask, out_ref):
    def pair_step(pair, carry):
        column = pl.multiple_of(pair * 128, 128)
        for part in range(2):
            rows = pl.ds(part * HALF, HALF)
            query = qkv_ref[rows, pl.ds(column, 128)] * bf16(HEAD_DIM**-0.5)
            key_part = qkv_ref[rows, pl.ds(D + column, 128)]
            value_part = qkv_ref[rows, pl.ds(2 * D + column, 128)]
            mixed = []
            for second in (False, True):
                scores = nt(masked(key_part, second), query) + mask
                weights = jnp.exp(scores - jnp.max(scores, axis=0, keepdims=True))
                probs = weights * (1.0 / jnp.sum(weights, axis=0, keepdims=True))
                mixed.append(tn(value_part, probs.astype(bf16)))
            mixed = jnp.concatenate([mixed[0][:64], mixed[1][64:]], axis=0)
            out_ref[rows, pl.ds(column, 128)] = mixed.T.astype(bf16)
        return carry

    lax.fori_loop(0, HEADS // 2, pair_step, 0)


def attend_back(qkv_ref, mask, grad_ref, out_ref):
    first = lane_half(False)

    def pair_step(pair, carry):
        column = pl.multiple_of(pair * 128, 128)
        for part in range(2):
            rows = pl.ds(part * HALF, HALF)
            query = qkv_ref[rows, pl.ds(column, 128)] * bf16(HEAD_DIM**-0.5)
            keys = both_heads(qkv_ref[rows, pl.ds(D + column, 128)])
            values = both_heads(qkv_ref[rows, pl.ds(2 * D + column, 128)])
            grad = grad_ref[rows, pl.ds(column, 128)]
            probs = probs_of(keys, query, mask)
            grad_probs = nt(values, grad).reshape(2, HALF, HALF)
            centre = jnp.sum(grad_probs * probs, axis=1, keepdims=True)
            grad_scores = flat_heads(probs * (grad_probs - centre))
            grad_query = tn(keys, grad_scores).T * HEAD_DIM**-0.5
            out_ref[rows, pl.ds(column, 128)] = grad_query.astype(bf16)
            grad_key = nn(grad_scores, query)
            grad_key = jnp.where(first, grad_key[:HALF], grad_key[HALF:])
            out_ref[rows, pl.ds(D + column, 128)] = grad_key.astype(bf16)
            grad_value = nn(flat_heads(probs), grad)
            grad_value = jnp.where(first, grad_value[:HALF], grad_value[HALF:])
            out_ref[rows, pl.ds(2 * D + column, 128)] = grad_value.astype(bf16)
        return carry

    lax.fori_loop(0, HEADS // 2, pair_step, 0)


def project_qkv(normed, weight, vec, qv_row, out_ref):
    for member in range(3):
        packed = nn(normed, weight[:, member * D : (member + 1) * D])
        if member != 1:
            row = qv_row + member // 2
            packed = packed + vec[row : row + 1, :]
        out_ref[:, member * D : (member + 1) * D] = packed.astype(bf16)


def place_to_send(dest):
    local = lax.broadcasted_iota(jnp.int32, (CHUNK, ROWS), 0)
    col = lax.broadcasted_iota(jnp.int32, (CHUNK, ROWS), 1)
    source = (local // 2) * 8 + dest * 2 + local % 2
    return ((col == source) & (local < 98)).astype(bf16)


def recv_to_frame(group_at, source):
    row = lax.broadcasted_iota(jnp.int32, (ROWS, CHUNK), 0)
    col = lax.broadcasted_iota(jnp.int32, (ROWS, CHUNK), 1)
    second = (row >= HALF).astype(jnp.int32)
    spot = row - second * HALF
    local = (spot - (group_at ^ source) * 49) * 2 + second
    inside = (spot >= (group_at ^ source) * 49) & (spot < ((group_at ^ source) + 1) * 49)
    return ((col == local) & inside).astype(bf16)


def place_forward_kernel(
    scalars, tokens, vec, *refs
):
    own_qkv, own_proj, *pieces = refs[:7]
    h1, qkv, mixed, o1, *rest = refs[7:]
    sends, (w_qkv, w_proj, sem_a, sem_b) = rest[:4], rest[4:]
    qkv_copy = Weights(scalars, own_qkv, pieces, TIME_QKV_PARTS, TIME_CHUNK, w_qkv, sem_a)
    proj_copy = Weights(scalars, own_proj, pieces, TIME_PROJ_PARTS, TIME_CHUNK, w_proj, sem_b)
    qkv_copy.start()
    proj_copy.start()
    normal, unused = norm_parts(tokens[...].astype(f32))
    normed = (normal * vec[TIME_GAIN : TIME_GAIN + 1, :] + vec[TIME_SHIFT : TIME_SHIFT + 1, :])
    normed = normed.astype(bf16)
    h1[...] = normed
    qkv_copy.wait()
    project_qkv(normed, w_qkv, vec, TIME_QV, qkv)
    attend(qkv, key_mask(True), mixed)
    proj_copy.wait()
    out = (nn(mixed[...], w_proj[...]) + vec[TIME_PROJ_B : TIME_PROJ_B + 1, :]).astype(bf16)
    o1[...] = out
    for dest in range(4):
        sends[dest][...] = nn(place_to_send(dest), out).astype(bf16)


def frame_forward_kernel(scalars, tokens, vec, r0, r1, r2, r3, *refs):
    own_fc, own_qkv, own_proj, *pieces = refs[:8]
    x1, h2, qkv, mixed, x2, h3 = refs[8:14]
    w_fc, w_qkv, w_proj, sem_a, sem_b, sem_c = refs[14:]
    fc_copy = Weights(scalars, own_fc, pieces, TIME_FC_PARTS, SPACE_CHUNK, w_fc, sem_a)
    qkv_copy = Weights(scalars, own_qkv, pieces, SPACE_QKV_PARTS, SPACE_CHUNK, w_qkv, sem_b)
    proj_copy = Weights(scalars, own_proj, pieces, SPACE_PROJ_PARTS, SPACE_CHUNK, w_proj, sem_c)
    fc_copy.start()
    qkv_copy.start()
    proj_copy.start()
    group_at = scalars[0]
    received = sum(
        nn(recv_to_frame(group_at, source), ref[...]) for source, ref in enumerate((r0, r1, r2, r3))
    ).astype(bf16)
    fc_copy.wait()
    branch = nn(received, w_fc[...]) + vec[TIME_FC_B : TIME_FC_B + 1, :]
    after = tokens[...].astype(f32) + branch
    x1[...] = after
    normal, unused = norm_parts(after)
    normed = normal * vec[SPACE_GAIN : SPACE_GAIN + 1, :] + vec[SPACE_SHIFT : SPACE_SHIFT + 1, :]
    normed = normed.astype(bf16)
    h2[...] = normed
    qkv_copy.wait()
    project_qkv(normed, w_qkv, vec, SPACE_QV, qkv)
    attend(qkv, key_mask(False), mixed)
    proj_copy.wait()
    after = x1[...] + (nn(mixed[...], w_proj[...]) + vec[SPACE_PROJ_B : SPACE_PROJ_B + 1, :])
    x2[...] = after
    normal, unused = norm_parts(after)
    normed = normal * vec[MLP_GAIN : MLP_GAIN + 1, :] + vec[MLP_SHIFT : MLP_SHIFT + 1, :]
    h3[...] = normed.astype(bf16)


def norm_back(values, gain, grad_normed):
    normal, inverse = norm_parts(values)
    scaled = grad_normed * gain
    mean = jnp.mean(scaled, axis=-1, keepdims=True)
    along = jnp.mean(scaled * normal, axis=-1, keepdims=True)
    grad = inverse * (scaled - mean - normal * along)
    return (
        grad,
        jnp.sum(grad_normed * normal, axis=0, keepdims=True),
        jnp.sum(grad_normed, axis=0, keepdims=True),
    )


def column_sum(values):
    return jnp.sum(values.astype(f32), axis=0, keepdims=True)


def mlp_kernel(scalars, live, vec, x2, h3, out_grad, *refs):
    own_in, own_out, *pieces = refs[:11]
    in_pieces, out_pieces = [pieces[0]] + pieces[1:5], [pieces[0]] + pieces[5:9]
    layer_out, acts, du, dm, e2, sums, w_in, w_out, sem_a, sem_b = refs[11:]
    in_copy = Weights(scalars, own_in, in_pieces, MLP_IN_PARTS, IN_CHUNK, w_in, sem_a)
    out_copy = Weights(scalars, own_out, out_pieces, MLP_OUT_PARTS, OUT_CHUNK, w_out, sem_b, 3)
    in_copy.start()
    out_copy.start()
    e3 = live[0, 0] * out_grad[...].astype(f32)
    grad_branch = e3.astype(bf16)
    dm[...] = grad_branch
    sums[3:4, :] = column_sum(grad_branch)
    sums[4:8, :] = jnp.zeros((4, D), f32)
    normed = h3[...]
    in_copy.wait()
    out_copy.wait()
    x3 = x2[...] + vec[MLP_OUT_B : MLP_OUT_B + 1, :]
    e2[...] = x3
    back = None
    for part in range(4):
        columns = slice(part * D, (part + 1) * D)
        pre = nn(normed, w_in[:, columns]) + vec[MLP_IN_B + part : MLP_IN_B + part + 1, :]
        cdf = 0.5 * (1.0 + lax.erf(pre * (0.5**0.5)))
        act = (pre * cdf).astype(bf16)
        slope = cdf + pre * jnp.exp(-0.5 * pre * pre) * 0.3989422804014327
        acts[:, columns] = act
        grad = (slope * nt(grad_branch, w_out[columns, :])).astype(bf16)
        du[:, columns] = grad
        sums[4 + part : 5 + part, :] = column_sum(grad)
        e2[...] += nn(act, w_out[columns, :])
        piece = nt(grad, w_in[:, columns])
        back = piece if back is None else back + piece
    layer_out[...] = (live[0, 0] * e2[...]).astype(bf16)
    grad, gain_grad, shift_grad = norm_back(x2[...], vec[MLP_GAIN : MLP_GAIN + 1, :], back)
    sums[0:1, :] = gain_grad
    sums[1:2, :] = shift_grad
    sums[2:3, :] = jnp.zeros((1, D), f32)
    e2[...] = e3 + grad


def space_back_kernel(scalars, vec, e2, x1, qkv, *refs):
    own_proj, own_qkv, *pieces = refs[:7]
    dqkv, e1, dt2, sums, s0, s1, s2, s3, w_qkv, w_proj, da, sem_a, sem_b = refs[7:]
    proj_copy = Weights(scalars, own_proj, pieces, SPACE_PROJ_PARTS, SPACE_CHUNK, w_proj, sem_a)
    qkv_copy = Weights(scalars, own_qkv, pieces, SPACE_QKV_PARTS, SPACE_CHUNK, w_qkv, sem_b)
    proj_copy.start()
    qkv_copy.start()
    branch = e2[...].astype(bf16)
    dt2[...] = branch
    proj_copy.wait()
    da[...] = nt(branch, w_proj[...]).astype(bf16)
    attend_back(qkv, key_mask(False), da, dqkv)
    qkv_copy.wait()
    back = nt(dqkv[...], w_qkv[...])
    grad, gain_grad, shift_grad = norm_back(x1[...], vec[SPACE_GAIN : SPACE_GAIN + 1, :], back)
    total = e2[...] + grad
    e1[...] = total
    rounded = total.astype(bf16)
    for source, ref in enumerate((s0, s1, s2, s3)):
        ref[...] = tn(recv_to_frame(scalars[0], source), rounded).astype(bf16)
    sums[0:1, :] = gain_grad
    sums[1:2, :] = shift_grad
    sums[2:3, :] = column_sum(branch)
    sums[3:4, :] = column_sum(dqkv[:, :D])
    sums[4:5, :] = column_sum(dqkv[:, 2 * D :])
    sums[5:8, :] = jnp.zeros((3, D), f32)


def time_projections_kernel(scalars, r0, r1, r2, r3, *refs):
    own_fc, own_proj, packed, *pieces = refs[:11]
    dt1, do1, da1, sums, w_fc, w_proj, sem_a, sem_b = refs[11:]
    fc_pieces, pieces = [packed] + pieces[:4], [packed] + pieces[4:]
    fc_copy = Weights(scalars, own_fc, fc_pieces, TIME_FC_PARTS, SPACE_CHUNK, w_fc, sem_a)
    proj_copy = Weights(scalars, own_proj, pieces, TIME_PROJ_PARTS, TIME_CHUNK, w_proj, sem_b)
    fc_copy.start()
    proj_copy.start()
    branch = sum(
        tn(place_to_send(source), ref[...]) for source, ref in enumerate((r0, r1, r2, r3))
    ).astype(bf16)
    dt1[...] = branch
    fc_copy.wait()
    projected = nt(branch, w_fc[...]).astype(bf16)
    do1[...] = projected
    proj_copy.wait()
    da1[...] = nt(projected, w_proj[...]).astype(bf16)
    sums[0:1, :] = column_sum(projected)
    sums[1:2, :] = column_sum(branch)
    sums[2:8, :] = jnp.zeros((6, D), f32)


def time_back_kernel(scalars, vec, tokens, qkv, da1, early_sums, own_qkv, *refs):
    pieces, (dqkv, sums, s0, s1, s2, s3, w_qkv, sem) = refs[:5], refs[5:]
    qkv_copy = Weights(scalars, own_qkv, pieces, TIME_QKV_PARTS, TIME_CHUNK, w_qkv, sem)
    qkv_copy.start()
    attend_back(qkv, key_mask(True), da1, dqkv)
    qkv_copy.wait()
    back = nt(dqkv[...], w_qkv[...])
    grad, gain_grad, shift_grad = norm_back(
        tokens[...].astype(f32), vec[TIME_GAIN : TIME_GAIN + 1, :], back
    )
    rounded = grad.astype(bf16)
    for dest, ref in enumerate((s0, s1, s2, s3)):
        ref[...] = nn(place_to_send(dest), rounded).astype(bf16)
    sums[0:1, :] = gain_grad
    sums[1:2, :] = shift_grad
    sums[2:4, :] = early_sums[0:2, :]
    sums[4:5, :] = column_sum(dqkv[:, :D])
    sums[5:6, :] = column_sum(dqkv[:, 2 * D :])
    sums[6:8, :] = jnp.zeros((2, D), f32)


def weight_grad_kernel(scalars, *refs, count, tables):
    inputs, (kept, sent, turned, ordered) = refs[:-4], refs[-4:]
    core = scalars[0] % 2

    def store(shard, rows, columns, values):
        @pl.when(core == shard % 2)
        def _():
            kept[shard // 2, rows, columns] = values

        @pl.when(core != shard % 2)
        def _():
            sent[shard // 2, rows, columns] = values

    at = 0
    for index in range(count):
        left, right = inputs[2 * index : 2 * index + 2]
        width = left.shape[1]
        shard_rows = width // 4
        if shard_rows % 128 == 0:
            for spot in range(4):
                shard = 2 * (spot % 2) + (core if spot < 2 else 1 - core)
                source = pl.ds(pl.multiple_of(shard * shard_rows, shard_rows), shard_rows)
                target = kept if spot < 2 else sent
                for block in range(right.shape[1] // D):
                    total = tn(left[:, source], right[:, block * D : (block + 1) * D])
                    rows = slice(at + block * shard_rows, at + (block + 1) * shard_rows)
                    target[spot % 2, rows, :] = total.astype(bf16)
            at += shard_rows * (right.shape[1] // D)
            continue
        turned[0:width, :] = left[...].T
        for spot in range(4):
            shard = 2 * (spot % 2) + (core if spot < 2 else 1 - core)
            source = pl.ds(pl.multiple_of(shard * shard_rows, shard_rows), shard_rows)
            ordered[spot * shard_rows : (spot + 1) * shard_rows, :] = turned[source, :]
        for block in range(right.shape[1] // D):
            columns = slice(block * D, (block + 1) * D)
            total = nn(ordered[...], right[:, columns]).astype(bf16)
            for spot in range(4):
                target = kept if spot < 2 else sent
                target[spot % 2, at : at + shard_rows, :] = total[
                    spot * shard_rows : (spot + 1) * shard_rows, :
                ]
            at += shard_rows
    if tables:
        time, space, mlp = (ref[...] for ref in inputs[2 * count :])
        singles = jnp.concatenate([time[0:4], space[0:3], mlp[0:2], mlp[3:4]], axis=0)
        for ref in (kept, sent):
            for chip in range(2):
                ref[chip, at : at + EXTRA, :] = jnp.zeros((EXTRA, D), bf16)
        for shard in range(4):
            lanes = slice(shard * BLOCK, (shard + 1) * BLOCK)
            store(shard, slice(at, at + 10), slice(0, BLOCK), singles[:, lanes].astype(bf16))
            half = slice((shard % 2) * (D // 2), (shard % 2 + 1) * (D // 2))
            for row, pair in ((10, time[4:6]), (11, space[3:5])):
                values = pair[shard // 2 : shard // 2 + 1, half].astype(bf16)
                store(shard, slice(at + row, at + row + 1), slice(0, D // 2), values)
            values = mlp[4 + shard : 5 + shard, :].astype(bf16)
            store(shard, slice(at + 12, at + 13), slice(0, D), values)


def last_kernel(scalars, e1, r0, r1, r2, r3, out):
    total = e1[...]
    for source, ref in enumerate((r0, r1, r2, r3)):
        total = total + nn(recv_to_frame(scalars[0], source), ref[...])
    out[...] = total


def shape(rows, columns, kind):
    return jax.ShapeDtypeStruct((rows, columns), kind)


VMEM = pl.BlockSpec(memory_space=pltpu.MemorySpace.VMEM)
SMEM = pl.BlockSpec(memory_space=pltpu.MemorySpace.SMEM)
ANY = pl.BlockSpec(memory_space=pltpu.MemorySpace.HBM)


def in_hbm(array):
    return pltpu.with_memory_space_constraint(array, pltpu.MemorySpace.HBM)


def call(kernel, name, outs, specs, scratch, operands, microseconds):
    return pl.pallas_call(
        kernel,
        name=name,
        out_shape=outs,
        in_specs=specs,
        out_specs=[VMEM] * len(outs),
        scratch_shapes=scratch,
        compiler_params=pltpu.CompilerParams(vmem_limit_bytes=LIMITS.get(name, 5) << 20),
        cost_estimate=pl.CostEstimate(
            flops=int((microseconds + 8) * 1.1e9), transcendentals=0,
            bytes_accessed=1024,
        ),
    )(*operands)


def dma_sems(parts):
    return pltpu.SemaphoreType.DMA((1 + 3 * len(parts),))


def vmem(rows, columns, kind=bf16):
    return pltpu.VMEM((rows, columns), kind)


def place_forward(scalars, tokens, vec, owns, pieces):
    outs = [shape(ROWS, D, bf16), shape(ROWS, 3 * D, bf16), shape(ROWS, D, bf16)]
    outs += [shape(ROWS, D, bf16)] + [shape(CHUNK, D, bf16)] * 4
    return call(
        place_forward_kernel, "place_forward", outs, [SMEM, VMEM, VMEM] + [ANY] * 7,
        [vmem(D, 3 * D), vmem(D, D), dma_sems(TIME_QKV_PARTS), dma_sems(TIME_PROJ_PARTS)],
        (scalars, tokens, vec, *owns, *pieces), 11,
    )


def frame_forward(scalars, tokens, vec, received, owns, pieces):
    outs = [shape(ROWS, D, f32), shape(ROWS, D, bf16), shape(ROWS, 3 * D, bf16)]
    outs += [shape(ROWS, D, bf16), shape(ROWS, D, f32), shape(ROWS, D, bf16)]
    return call(
        frame_forward_kernel, "frame_forward", outs, [SMEM] + [VMEM] * 6 + [ANY] * 8,
        [
            vmem(D, D), vmem(D, 3 * D), vmem(D, D),
            dma_sems(TIME_FC_PARTS), dma_sems(SPACE_QKV_PARTS), dma_sems(SPACE_PROJ_PARTS),
        ],
        (scalars, tokens, vec, *received, *owns, *pieces), 13,
    )


def mlp_both(scalars, live, vec, x2, h3, out_grad, owns, in_pieces, out_pieces):
    outs = [
        shape(ROWS, D, bf16), shape(ROWS, FF, bf16), shape(ROWS, FF, bf16),
        shape(ROWS, D, bf16), shape(ROWS, D, f32), shape(8, D, f32),
    ]
    return call(
        mlp_kernel, "mlp_both", outs, [SMEM, SMEM] + [VMEM] * 4 + [ANY] * 11,
        [vmem(D, FF), vmem(FF, D), dma_sems(MLP_IN_PARTS), dma_sems(MLP_OUT_PARTS)],
        (scalars, live, vec, x2, h3, out_grad, *owns, *in_pieces, *out_pieces[1:]), 18,
    )


def space_back(scalars, vec, e2, x1, qkv, owns, pieces):
    outs = [shape(ROWS, 3 * D, bf16), shape(ROWS, D, f32), shape(ROWS, D, bf16)]
    outs += [shape(8, D, f32)] + [shape(CHUNK, D, bf16)] * 4
    return call(
        space_back_kernel, "space_back", outs, [SMEM] + [VMEM] * 4 + [ANY] * 7,
        [
            vmem(D, 3 * D), vmem(D, D), vmem(ROWS, D),
            dma_sems(SPACE_PROJ_PARTS), dma_sems(SPACE_QKV_PARTS),
        ],
        (scalars, vec, e2, x1, qkv, *owns, *pieces), 20,
    )


def time_projections(scalars, received, owns, fc_pieces, pieces):
    outs = [shape(ROWS, D, bf16)] * 3 + [shape(8, D, f32)]
    return call(
        time_projections_kernel, "time_projections", outs, [SMEM] + [VMEM] * 4 + [ANY] * 11,
        [vmem(D, D), vmem(D, D), dma_sems(TIME_FC_PARTS), dma_sems(TIME_PROJ_PARTS)],
        (scalars, *received, *owns, *fc_pieces, *pieces[1:]), 4,
    )


def time_back(scalars, vec, tokens, qkv, da1, early_sums, own, pieces):
    outs = [shape(ROWS, 3 * D, bf16), shape(8, D, f32)] + [shape(CHUNK, D, bf16)] * 4
    return call(
        time_back_kernel, "time_back", outs, [SMEM] + [VMEM] * 5 + [ANY] * 6,
        [vmem(D, 3 * D), dma_sems(TIME_QKV_PARTS)],
        (scalars, vec, tokens, qkv, da1, early_sums, own, *pieces), 16,
    )


def weight_grads(name, scalars, groups, tables=()):
    rows = sum(g[0].shape[1] // 4 * (g[1].shape[1] // D) for g in groups)
    flat = [array for group in groups for array in group] + list(tables)
    rows += EXTRA if tables else 0
    kernel = functools.partial(weight_grad_kernel, count=len(groups), tables=len(tables))
    return call(
        kernel, name, [jax.ShapeDtypeStruct((2, rows, D), bf16)] * 2, [SMEM] + [VMEM] * len(flat),
        [vmem(D, ROWS)] * 2, (scalars, *flat), rows / 150,
    )


def copy_all(copies):
    for copy in copies:
        copy.start()
    for copy in copies:
        copy.wait()


def columns_of(ref, at):
    return ref.at[:, pl.ds(pl.multiple_of(at * D, D), D)]


def pack_time_kernel(scalars, time_qkv, time_proj, vectors, out, sems):
    first, second = out.at[pl.ds(0, BLOCK), :], out.at[pl.ds(BLOCK, BLOCK), :]
    tail = pltpu.make_async_copy(vectors, out.at[pl.ds(2 * BLOCK, VECTOR_PAD), :], sems.at[2])
    tail.start()

    @pl.when(scalars[1] == 0)
    def _():
        pltpu.make_async_copy(columns_of(time_qkv, 0), first, sems.at[0]).start()
        pltpu.make_async_copy(columns_of(time_qkv, 1), second, sems.at[1]).start()

    @pl.when(scalars[1] != 0)
    def _():
        pltpu.make_async_copy(columns_of(time_qkv, 2), first, sems.at[0]).start()
        pltpu.make_async_copy(time_proj, second, sems.at[1]).start()

    pltpu.make_async_copy(time_proj, first, sems.at[0]).wait()
    pltpu.make_async_copy(time_proj, second, sems.at[1]).wait()
    tail.wait()


def pack_rest_kernel(
    scalars, time_qkv, time_proj, time_fc, space_qkv, space_proj, mlp_in, mlp_out, vectors,
    packed, space_half, in_half, out_half, sems,
):
    half = scalars[1]
    copies = []

    def add(source, target, row, rows):
        target = target.at[pl.ds(row, rows), :]
        copies.append(pltpu.make_async_copy(source, target, sems.at[len(copies)]))

    out_at = scalars[3]
    halves = pl.ds(pl.multiple_of(out_at * 2 * BLOCK, 2 * BLOCK), 2 * BLOCK)
    add(columns_of(mlp_in, 2 * half), in_half, 0, BLOCK)
    add(columns_of(mlp_in, 2 * half + 1), in_half, BLOCK, BLOCK)
    add(mlp_out.at[halves, :], out_half, 0, 2 * BLOCK)
    blocks = [columns_of(time_qkv, at) for at in range(3)] + [time_proj]
    blocks += [columns_of(space_qkv, 0), columns_of(space_qkv, 1), time_fc]
    blocks += [columns_of(space_qkv, 2), space_proj]
    blocks += [columns_of(mlp_in, at) for at in range(4)]
    for at, source in enumerate(blocks):
        add(source, packed, at * BLOCK, BLOCK)
    add(mlp_out, packed, 13 * BLOCK, 4 * BLOCK)
    add(vectors, packed, VECTOR_AT, VECTOR_PAD)
    at = len(copies)
    middle = BLOCK // 2

    def space(source, row, rows, sem):
        return pltpu.make_async_copy(source, space_half.at[pl.ds(row, rows), :], sems.at[sem])

    @pl.when(half == 0)
    def _():
        space(columns_of(space_qkv, 0), 0, BLOCK, at).start()
        space(columns_of(space_qkv, 1), BLOCK, BLOCK, at + 1).start()
        space(time_fc.at[pl.ds(0, middle), :], 2 * BLOCK, middle, at + 2).start()

    @pl.when(half != 0)
    def _():
        space(time_fc.at[pl.ds(middle, middle), :], 0, middle, at + 2).start()
        space(columns_of(space_qkv, 2), middle, BLOCK, at).start()
        space(space_proj, BLOCK + middle, BLOCK, at + 1).start()

    copy_all(copies)
    space(space_proj, 0, BLOCK, at).wait()
    space(space_proj, BLOCK, BLOCK, at + 1).wait()
    space(time_fc.at[pl.ds(0, middle), :], 2 * BLOCK, middle, at + 2).wait()


def pack_time(*operands):
    operands = [operands[0], *map(in_hbm, operands[1:])]
    return pl.pallas_call(
        pack_time_kernel, name="pack_time",
        compiler_params=pltpu.CompilerParams(vmem_limit_bytes=LIMITS.get("pack_time", 5) << 20), out_shape=shape(2 * BLOCK + VECTOR_PAD, D, bf16),
        in_specs=[SMEM, ANY, ANY, ANY], out_specs=VMEM,
        scratch_shapes=[pltpu.SemaphoreType.DMA((3,))],
        cost_estimate=pl.CostEstimate(flops=11 * 10**9, transcendentals=0, bytes_accessed=1024),
    )(*operands)


def pack_rest(*operands):
    operands = [operands[0], *map(in_hbm, operands[1:])]
    return pl.pallas_call(
        pack_rest_kernel, name="pack_rest",
        compiler_params=pltpu.CompilerParams(vmem_limit_bytes=LIMITS.get("pack_rest", 5) << 20),
        out_shape=[
            shape(VECTOR_AT + VECTOR_PAD, D, bf16), shape(480, D, bf16), shape(384, D, bf16),
            shape(384, D, bf16),
        ],
        in_specs=[SMEM] + [ANY] * 8, out_specs=[VMEM] * 4,
        scratch_shapes=[pltpu.SemaphoreType.DMA((21,))],
        cost_estimate=pl.CostEstimate(flops=11 * 10**9, transcendentals=0, bytes_accessed=1024),
    )(*operands)


def table_kernel(scalars, own, packed, direct, across, out, pieces, sems):
    copies = [
        pltpu.make_async_copy(source.at[pl.ds(row, VECTOR_PAD), :], pieces.at[at], sems.at[at])
        for at, (source, row) in enumerate(
            ((own, 0), (packed, VECTOR_AT), (direct, 2 * BLOCK), (across, 2 * BLOCK))
        )
    ]
    copy_all(copies)
    group_at = scalars[0]
    out[...] = jnp.zeros((VECTOR_PAD, D), f32)
    for shard in range(4):
        rows = pieces[group_at ^ shard].astype(f32)[:, :BLOCK]
        lanes = slice(shard * BLOCK, (shard + 1) * BLOCK)
        out[0:10, lanes] = rows[0:10]
        for row in range(2):
            lanes = slice((shard % 2) * 384 + row * BLOCK, (shard % 2) * 384 + (row + 1) * BLOCK)
            for first in (TIME_QV, SPACE_QV):
                source = rows[first + row : first + row + 1]
                out[first + shard // 2 : first + shard // 2 + 1, lanes] = source
        for row in range(4):
            lanes = slice(row * BLOCK, (row + 1) * BLOCK)
            source = rows[MLP_IN_B + row : MLP_IN_B + row + 1]
            out[MLP_IN_B + shard : MLP_IN_B + shard + 1, lanes] = source


def vector_table(*operands):
    return call(
        table_kernel, "table", [shape(VECTOR_PAD, D, f32)], [SMEM] + [ANY] * 4,
        [pltpu.VMEM((4, VECTOR_PAD, D), bf16), pltpu.SemaphoreType.DMA((4,))], operands, 1,
    )[0]


def unpack_kernel(scalars, mine, other, *outs, bit, parts):
    own_first = (scalars[2] // bit) % 2 == 0
    for half, row, rows, index, out_row, column in parts:
        rows = pl.ds(row, rows)
        near, far = mine[rows, :], other[rows, :]
        pair = (near, far) if half == 0 else (far, near)
        outs[index][out_row : out_row + rows.size, column * D : (column + 1) * D] = jnp.where(
            own_first, *pair
        ).astype(f32)


def unpack(scalars, mine, other, bit, parts, outs):
    kernel = functools.partial(unpack_kernel, bit=bit, parts=parts)
    return call(
        kernel, "unpack", [shape(*out, f32) for out in outs], [SMEM, VMEM, VMEM], [],
        (scalars, mine, other), 2,
    )


OUT_PARTS = ((0, 0, 384, 0, 0, 0), (1, 0, 384, 0, 384, 0))
IN_PARTS = (
    (0, 0, 192, 0, 0, 0), (0, 192, 192, 0, 0, 1), (1, 0, 192, 0, 0, 2), (1, 192, 192, 0, 0, 3),
)
SPACE_PARTS = (
    (0, 0, 192, 0, 0, 0), (0, 192, 192, 0, 0, 1), (1, 0, 192, 0, 0, 2), (1, 192, 192, 1, 0, 0),
)
SMALL_PARTS = ((0, 0, 192, 0, 0, 0), (1, 0, 192, 1, 0, 0))
TIME_PARTS = (
    (0, 0, 192, 0, 0, 0), (0, 192, 128, 0, 0, 1), (1, 0, 64, 0, 128, 1), (1, 64, 192, 0, 0, 2),
    (1, 256, 16, 1, 0, 0),
)


def last_sum(scalars, e1, received):
    return call(
        last_kernel, "last_sum", [shape(ROWS, D, f32)], [SMEM] + [VMEM] * 5, [],
        (scalars, e1, *received), 2,
    )[0]


def flip(array, axis, bit, size):
    return lax.ppermute(array, axis, [(at, at ^ bit) for at in range(size)])


def pick(array, at):
    return lax.dynamic_index_in_dim(array, at, 0, keepdims=False)


def add_rounded(left, right):
    return (left.astype(f32) + right.astype(f32)).astype(bf16)


def after(value, *others):
    return lax.optimization_barrier((value,) + others)[0]


def halves_of(own, half_at):
    return lax.dynamic_slice_in_dim(own, half_at * (own.shape[0] // 2), own.shape[0] // 2, 0)


def step_rows(rows):
    return next(step for step in (96, 80, 48, 16) if rows % step == 0)


def sum_split_kernel(scalars, kept, got, keep, send, *, bit):
    rows = keep.shape[-2]
    step = step_rows(rows)
    if bit == 0:
        mine = scalars[0] // 2
    else:
        mine = (scalars[2] // bit) % 2
    for target, at in ((keep, mine), (send, 1 - mine)):

        def body(index, carry, target=target, at=at):
            row = pl.multiple_of(index * step, 16)
            if bit == 0:
                total = kept[at, pl.ds(row, step), :].astype(f32)
                total = total + got[at, pl.ds(row, step), :].astype(f32)
                target[pl.ds(row, step), :] = total.astype(bf16)
            else:
                source = pl.ds(pl.multiple_of(at * rows + row, 16), step)
                for chip in range(2) if len(keep.shape) == 3 else [None]:
                    here = (source, slice(None)) if chip is None else (chip, source, slice(None))
                    there = (pl.ds(row, step), slice(None))
                    there = there if chip is None else (chip,) + there
                    total = kept[here].astype(f32) + got[here].astype(f32)
                    target[there] = total.astype(bf16)
            return carry

        lax.fori_loop(0, rows // step, body, 0)


def sum_split(scalars, kept, got, bit):
    dims = kept.shape
    out = dims[1:] if bit == 0 else dims[:-2] + (dims[-2] // 2, D)
    kernel = functools.partial(sum_split_kernel, bit=bit)
    outs = [jax.ShapeDtypeStruct(out, bf16)] * 2
    return call(kernel, "sum_split", outs, [SMEM, VMEM, VMEM], [], (scalars, kept, got), 0)


def join_kernel(scalars, mine, other, out, *, bit):
    rows = mine.shape[0]
    at = (scalars[2] // bit) % 2
    out[pl.ds(pl.multiple_of(at * rows, 16), rows), :] = mine[...]
    out[pl.ds(pl.multiple_of((1 - at) * rows, 16), rows), :] = other[...]


def join(scalars, mine, other, bit):
    kernel = functools.partial(join_kernel, bit=bit)
    outs = [shape(2 * mine.shape[0], D, bf16)]
    return call(kernel, "join", outs, [SMEM, VMEM, VMEM], [], (scalars, mine, other), 0)[0]


class Reduce:
    def __init__(self, parts, order, scalars, replica_at, ring_size):
        self.kept, sent = parts
        self.scalars, self.replica_at, self.ring_size = scalars, replica_at, ring_size
        self.steps = [("sum", bit) for bit in order]
        self.steps += [("gather", bit) for bit in reversed(order) if bit]
        self.flying = flip(sent, "group", 1, 4)
        self.halve = lambda array: array

    def split(self, bit):
        if bit == 0:
            chip = self.scalars[0] // 2
            return (lambda a: pick(a, chip)), (lambda a: pick(a, 1 - chip))
        mine = (self.replica_at // bit) % 2

        def half(at):
            def take(array):
                rows = array.shape[-2] // 2
                return lax.dynamic_slice_in_dim(array, at * rows, rows, array.ndim - 2)

            return take

        return half(mine), half(1 - mine)

    def flip(self, array, bit):
        axis = ("group", 2, 4) if bit == 0 else ("replica", bit, self.ring_size)
        return flip(array, *axis)

    def advance(self, *others):
        got = after(self.flying, *others) if others else self.flying
        if self.kept is not None:
            if self.steps[0][0] == "sum":
                bit = self.steps.pop(0)[1]
                if self.kept.shape[-2] % 32 == 0:
                    self.kept, sent = sum_split(self.scalars, self.kept, got, bit)
                else:
                    keep, send = self.split(bit)
                    sent = add_rounded(send(self.kept), send(got))
                    self.kept = add_rounded(keep(self.kept), keep(got))
            else:
                sent = self.current = add_rounded(self.kept, got)
                self.kept = None
                bit = self.steps[0][1]
        else:
            bit = self.steps.pop(0)[1]
            mine = (self.replica_at // bit) % 2
            if not self.steps:
                self.got, self.bit = got, bit
                return got
            if got.shape[0] % 16 == 0:
                self.current = join(self.scalars, self.current, got, bit)
            else:
                self.current = jnp.where(
                    mine == 0,
                    jnp.concatenate([self.current, got], 0),
                    jnp.concatenate([got, self.current], 0),
                )
            sent = self.current
            bit = self.steps[0][1]
        self.flying = self.flip(sent, bit)
        return sent

    def unpacked(self, parts, outs):
        return unpack(self.scalars, self.current, self.got, self.bit, parts, outs)


def block(array, at):
    return array[:, at * D : (at + 1) * D]


def unpack_grad(summed, blocks):
    return summed.reshape(blocks, BLOCK, D).transpose(1, 0, 2).reshape(BLOCK, blocks * D).astype(f32)


def exchange(chunks):
    return [chunks[0]] + [flip(chunks[d], "group", d, 4) for d in range(1, 4)]


def build(mesh):
    ring_size = mesh.shape["replica"]

    def on_device(tokens, out_grad, slot_mask, *shards):
        (
            time_norm_gain, time_norm_shift, time_qkv, time_qv_bias, time_proj, time_proj_bias,
            time_fc, time_fc_bias, space_norm_gain, space_norm_shift, space_qkv, space_qv_bias,
            space_proj, space_proj_bias, mlp_norm_gain, mlp_norm_shift, mlp_in, mlp_in_bias,
            mlp_out, mlp_out_bias,
        ) = shards
        group_at = lax.axis_index("group")
        replica_at = lax.axis_index("replica")
        half_at = replica_at % 2
        far_at = (replica_at // 2) % 2
        scalars = jnp.stack([group_at, half_at, replica_at, far_at]).astype(jnp.int32)
        live = slot_mask.astype(f32).reshape(1, 1)
        vectors = [
            time_norm_gain, time_norm_shift, time_proj_bias, time_fc_bias, space_norm_gain,
            space_norm_shift, space_proj_bias, mlp_norm_gain, mlp_norm_shift, mlp_out_bias,
            time_qv_bias, space_qv_bias, mlp_in_bias,
        ]
        cross = functools.partial(flip, axis="group", bit=2, size=4)
        near = functools.partial(flip, axis="group", bit=1, size=4)
        relay = functools.partial(flip, axis="replica", bit=1, size=ring_size)
        ends = [sum(v.shape[0] for v in vectors[: at + 1]) for at in range(len(vectors))]
        room = VECTOR_PAD * BLOCK
        flat = sum(jnp.pad(v, (at - v.shape[0], room - at)) for v, at in zip(vectors, ends))
        flat = jnp.pad(flat.reshape(VECTOR_PAD, BLOCK), ((0, 0), (0, D - BLOCK)))
        token_pieces = tokens[0].transpose(1, 0, 2).reshape(4, 49, 2, D)
        token_pieces = [pick(token_pieces, group_at ^ d) for d in range(4)]
        got = exchange(token_pieces)
        time_half = pack_time(scalars, time_qkv, time_proj, after(flat, *token_pieces))
        time_direct = cross(after(time_half, *got[1:]))
        place_tokens = jnp.pad(jnp.concatenate(got, axis=1), ((0, 3), (0, 0), (0, 0)))
        place_tokens = place_tokens.reshape(ROWS, D)

        packed, space_half, in_half, out_half = pack_rest(
            scalars, time_qkv, time_proj, time_fc, space_qkv, space_proj, mlp_in, mlp_out,
            after(flat, *got[1:]),
        )
        partner = near(packed)
        time_across = near(time_direct)
        time_relayed = relay(time_direct)
        space_direct = cross(after(space_half, time_direct))
        in_direct = cross(after(in_half, space_direct))
        out_direct = cross(after(out_half, space_direct))

        vec = vector_table(scalars, flat, partner, time_direct, time_across)
        time_pieces = (
            partner, time_direct, time_relayed, time_across, near(after(time_relayed, vec)),
        )
        pads = ((0, 0), (0, HALF - PLACES), (0, 0))
        frame_tokens = jnp.pad(tokens[0], pads).reshape(ROWS, D)
        frame_grad = jnp.pad(out_grad[0], pads).reshape(ROWS, D)

        space_across = near(space_direct)
        h1, qkv1, a1, o1, *sends = place_forward(
            scalars, after(place_tokens, space_direct), vec, (time_qkv, time_proj), time_pieces
        )
        received = exchange(sends)
        space_relayed = relay(space_direct)
        space_pieces = (
            partner, space_direct, space_relayed, space_across,
            near(after(space_relayed, o1)),
        )
        x1, h2, qkv2, a2, x2, h3 = frame_forward(
            scalars, after(frame_tokens, in_direct, out_direct), vec, received,
            (time_fc, space_qkv, space_proj), space_pieces,
        )
        in_relayed = relay(in_direct)
        in_pieces = (
            partner, in_direct, in_relayed, near(in_direct), near(after(in_relayed, x2)),
        )
        out_relayed = flip(out_direct, "replica", 2, ring_size)
        out_pieces = (
            partner, out_direct, out_relayed, near(after(out_direct, x2)),
            near(after(out_relayed, x2)),
        )
        layer_out, act, du, dm, e2, sums3 = mlp_both(
            scalars, live, vec, x2, h3, frame_grad, (mlp_in, mlp_out), in_pieces, out_pieces
        )
        layer_out = layer_out.reshape(2, HALF, D)[None, :, :PLACES]

        chunk = functools.partial(
            Reduce, scalars=scalars, replica_at=replica_at, ring_size=ring_size
        )
        bits = [1 << at for at in range(ring_size.bit_length() - 1)]
        along = [0] + bits
        names = {"x": 0, "y": bits[0], "u": bits[1], "w": bits[2]}

        def way(parts, order):
            return chunk(parts, [names[name] for name in order] + bits[3:])

        ways = {}
        last = ()

        back = {"sent": None, "got": [], "flying": None, "out": None}

        def move_back():
            nonlocal last
            sends, got = back["sent"], back["got"]
            if back["flying"] is not None:
                got.append(after(back["flying"], *last))
                last = (got[-1],)
            at = len(got) + 1
            if at < 4:
                back["flying"] = flip(after(sends[at], *last), "group", at, 4)
            else:
                back["out"] = last_sum(scalars, e1, [sends[0]] + got)
                back["flying"] = None
                last = (back["out"],)

        def advance(steps):
            nonlocal last
            for name in steps:
                if name == "a":
                    move_back()
                elif ways[name].steps:
                    last = (ways[name].advance(*last),)

        ways["o"] = way(weight_grads("mlp_out_grad", scalars, [(act, dm)]), ORDERS["o"])
        last = (ways["o"].kept,)
        advance(SCHEDULE[0])
        ways["i"] = way(
            weight_grads("mlp_in_grad", scalars, [(h3, after(du, *last))]), ORDERS["i"]
        )
        last = (ways["i"].kept,)
        advance(SCHEDULE[1])
        dqkv2, e1, dt2, sums2, *sends = space_back(
            scalars, vec, after(e2, *last), x1, qkv2, (space_proj, space_qkv), space_pieces
        )
        received = exchange(sends)
        last = (e1,)
        advance(SCHEDULE[2])
        ways["s"] = way(
            weight_grads("space_grad", scalars, [(h2, after(dqkv2, *last)), (a2, dt2)]),
            ORDERS["s"],
        )
        last = (ways["s"].kept,)
        advance(SCHEDULE[3])
        dt1, do1, da1, early = time_projections(
            scalars, [after(received[0], *last)] + received[1:], (time_fc, time_proj),
            space_pieces, time_pieces,
        )
        last = (do1,)
        advance(SCHEDULE[4])
        ways["p"] = way(
            weight_grads("time_small_grad", scalars, [(a1, after(do1, *last)), (o1, dt1)]),
            ORDERS["p"],
        )
        last = (ways["p"].kept,)
        advance(SCHEDULE[5])
        dqkv1, sums1, *sends = time_back(
            scalars, vec, place_tokens, qkv1, after(da1, *last), early, time_qkv, time_pieces
        )
        back["sent"] = sends
        last = (dqkv1,)
        advance(SCHEDULE[6])
        ways["t"] = way(
            weight_grads(
                "time_grad", scalars, [(h1, after(dqkv1, *last))], (sums1, sums2, sums3)
            ),
            ORDERS["t"],
        )
        last = (ways["t"].kept,)
        advance(SCHEDULE[7])
        while back["out"] is None:
            move_back()
        tokens_grad = back["out"].reshape(2, HALF, D)[None, :, :PLACES]
        while any(each.steps for each in ways.values()):
            advance([name for name in ways])
        way_out, way_in, way_space, way_small, way_time = (ways[name] for name in "oispt")
        (d_out,) = way_out.unpacked(OUT_PARTS, [(D, D)])
        (d_in,) = way_in.unpacked(IN_PARTS, [(BLOCK, FF)])
        d_space_qkv, d_space_proj = way_space.unpacked(SPACE_PARTS, [(BLOCK, 3 * D), (BLOCK, D)])
        d_proj, d_fc = way_small.unpacked(SMALL_PARTS, [(BLOCK, D), (BLOCK, D)])
        d_time_qkv, vectors = way_time.unpacked(TIME_PARTS, [(BLOCK, 3 * D), (16, D)])
        ones = vectors[:10, :BLOCK]
        return (
            layer_out, tokens_grad, ones[0], ones[1], d_time_qkv, vectors[10, : D // 2],
            d_proj, ones[2], d_fc, ones[3], ones[4], ones[5], d_space_qkv,
            vectors[11, : D // 2], d_space_proj, ones[6], ones[7], ones[8], d_in, vectors[12],
            d_out, ones[9],
        )

    return on_device


def solution(mesh):
    rows = P("group", None)
    vector = P("group")
    batch = P("replica", "group", None, None)
    params = (
        vector, vector, rows, vector, rows, vector, rows, vector, vector, vector, rows, vector,
        rows, vector, vector, vector, rows, vector, rows, vector,
    )
    return jax.shard_map(
        build(mesh),
        mesh=mesh,
        in_specs=(batch, batch, P("replica")) + params,
        out_specs=(batch, batch) + params,
        check_vma=False,
    )
```
